32 devices in a mesh: shard: 8 (over z, x), ctx: 2 (over core), tp: 2 (over y).
Axes of the slice: x: 2, y: 2, z: 4, core: 2. Of those that a mesh axis runs over, the one named last changes fastest.
Arguments:
- tokens: bfloat16 [2, 8, 1024, 1280], P(None, 'shard', 'ctx'), may hold values from -6 to 6
- patch_meta: int32 [3, 2, 8, 1024], P(None, None, 'shard'), may hold values from -1 to 31, as said below
- attn_norm_gain: float32 [1280], replicated, may hold values from 0.5 to 1.5
- attn_norm_bias: float32 [1280], replicated, may hold values from -3 to 3
- qkv_weight: bfloat16 [3, 1280, 1280], P(None, 'shard', 'tp'), may hold values from -0.15625 to 0.15625
- qkv_bias: float32 [3, 1280], P(None, 'tp'), may hold values from -3 to 3
- proj_weight: bfloat16 [1280, 1280], P('tp', 'shard'), may hold values from -0.625 to 0.625
- proj_bias: float32 [1280], replicated, may hold values from -3 to 3
- mlp_norm_gain: float32 [1280], replicated, may hold values from 0.5 to 1.5
- mlp_norm_bias: float32 [1280], replicated, may hold values from -3 to 3
- fc1_weight: bfloat16 [1280, 5120], P('shard', 'tp'), may hold values from -0.15625 to 0.15625
- fc1_bias: float32 [5120], P('tp'), may hold values from -3 to 3
- fc2_weight: bfloat16 [5120, 1280], P('tp', 'shard'), may hold values from -0.078125 to 0.078125
- fc2_bias: float32 [1280], replicated, may hold values from -3 to 3
- cotangent: bfloat16 [2, 8, 1024, 1280], P(None, 'shard', 'ctx'), may hold values from -6 to 6
Outputs:
- block_output: bfloat16 [2, 8, 1024, 1280], P(None, 'shard', 'ctx')
- input_grad: float32 [2, 8, 1024, 1280], P(None, 'shard', 'ctx')
- grad_attn_norm_gain: float32 [1280], replicated
- grad_attn_norm_bias: float32 [1280], replicated
- grad_qkv_weight: float32 [3, 1280, 1280], P(None, 'shard', 'tp')
- grad_qkv_bias: float32 [3, 1280], P(None, 'tp')
- grad_proj_weight: float32 [1280, 1280], P('tp', 'shard')
- grad_proj_bias: float32 [1280], replicated
- grad_mlp_norm_gain: float32 [1280], replicated
- grad_mlp_norm_bias: float32 [1280], replicated
- grad_fc1_weight: float32 [1280, 5120], P('shard', 'tp')
- grad_fc1_bias: float32 [5120], P('tp')
- grad_fc2_weight: float32 [5120, 1280], P('tp', 'shard')
- grad_fc2_bias: float32 [1280], replicated
The draws below stay inside these ranges and needn't reach their ends.
Inputs may be any that keep to these rules, and one draw needn't show every extreme that they name: patch_meta[0] holds each slot's picture id, counting up from 0 along a packed row, and -1 on padding slots, which lie only at a row's end; patch_meta[1] and patch_meta[2] hold the patch's row and column inside its picture (0 on padding). Pictures are rectangles of 10 to 32 patches a side filled row by row; only a row's last picture may have fewer picture rows. Fewer than 32 slots of a row are padding.
All inputs are finite; a program needn't handle non-finite values.
Results may differ from the reference program's by a relative error of at most 0.012.
Values may be sent and summed in bfloat16 or wider, within the bound.
A program may use at most 256 MiB of HBM per device.

```python
import math
import jax
import jax.numpy as jnp
from jax import lax

D = 1280
HEADS = 16
HDIM = 80
FF = 5120
ROW = 1024
SIDE = 32
MICRO = 2
ROWS = 8


def picture_row(row_key):
    smallest = SIDE // 3
    picture_slots = ROW // (smallest * smallest) + 1
    height_key, width_key = jax.random.split(row_key)
    heights = jax.random.randint(height_key, (picture_slots,), smallest, SIDE + 1)
    widths = jax.random.randint(width_key, (picture_slots,), smallest, SIDE + 1)
    picture_area = heights * widths
    starts = jnp.cumsum(picture_area) - picture_area
    room_left = ROW - starts
    kept_height = jnp.where(picture_area <= room_left, heights, jnp.clip(room_left // widths, 0, SIDE))
    kept_area = kept_height * widths
    finish = jnp.cumsum(kept_area)
    begins = finish - kept_area
    position = jnp.arange(ROW)
    filled = finish[-1]
    picture = jnp.sum((position[:, None] >= finish[None, :]).astype(jnp.int32), axis=1)
    inside = position < filled
    chosen = (picture[:, None] == jnp.arange(picture_slots)[None, :]).astype(jnp.int32)
    offset_in = position - jnp.sum(chosen * begins[None, :], axis=1)
    width_of = jnp.maximum(jnp.sum(chosen * widths[None, :], axis=1), 1)
    patch_row = jnp.where(inside, offset_in // width_of, 0)
    patch_col = jnp.where(inside, offset_in % width_of, 0)
    picture = jnp.where(inside, picture, -1)
    return jnp.stack([picture, patch_row, patch_col]).astype(jnp.int32)


def draw_patch_meta(key, part):
    row_keys = jax.random.split(key, MICRO * ROWS)
    drawn = jax.vmap(picture_row)(row_keys)
    return jnp.transpose(drawn, (1, 0, 2)).reshape(3, MICRO, ROWS, ROW)


def block_scale(rng, dims, cuts, low, largest):
    level, own = 1.0, jax.random.fold_in(rng, 6)
    for dim, parts in cuts:
        steps = jnp.exp(jax.random.uniform(jax.random.fold_in(own, dim), (parts,), jnp.float32, low / len(cuts), largest / len(cuts)))
        level = level * jnp.repeat(steps, dims[dim] // parts).reshape([-1 if axis == dim else 1 for axis in range(len(dims))])
    return level


def bell_draw(rng, shape, width, bound, shards=(), kind=jnp.bfloat16):
    entries = jax.random.normal(rng, shape, jnp.float32) * width
    if len(shards) > 0:
        entries = block_scale(rng, shape, shards, -0.22, 0.18) * entries
    return jnp.clip(entries, min=-bound, max=bound).astype(kind)


def setup_inputs(seed: int = 0) -> dict:
    splits = jax.random.split(jax.random.key(seed), 16)
    tokens = bell_draw(splits[0], (MICRO, ROWS, ROW, D), 1.0, 6.0, ((1, 8), (2, 2)))
    patch_meta = draw_patch_meta(jax.random.fold_in(splits[15], 71), 0)
    attn_norm_gain = jnp.clip(1.0 + 0.1 * jax.random.normal(splits[2], (D,), jnp.float32), 0.5, 1.5)
    attn_norm_bias = bell_draw(splits[3], (D,), 0.5, 3.0, (), jnp.float32)
    qkv_weight = bell_draw(splits[4], (3, D, D), D ** -0.5, 0.15625, ((1, 8), (2, 2)))
    qkv_bias = bell_draw(splits[5], (3, D), 0.5, 3.0, ((1, 2),), jnp.float32)
    proj_weight = bell_draw(splits[6], (D, D), (D // 16) ** -0.5, 0.625, ((0, 2), (1, 8)))
    proj_bias = bell_draw(splits[7], (D,), 0.5, 3.0, (), jnp.float32)
    mlp_norm_gain = jnp.clip(1.0 + 0.1 * jax.random.normal(splits[8], (D,), jnp.float32), 0.5, 1.5)
    mlp_norm_bias = bell_draw(splits[9], (D,), 0.5, 3.0, (), jnp.float32)
    fc1_weight = bell_draw(splits[10], (D, FF), D ** -0.5, 0.15625, ((0, 8), (1, 2)))
    fc1_bias = bell_draw(splits[11], (FF,), 0.5, 3.0, ((0, 2),), jnp.float32)
    fc2_weight = bell_draw(splits[12], (FF, D), FF ** -0.5, 0.078125, ((0, 2), (1, 8)))
    fc2_bias = bell_draw(splits[13], (D,), 0.5, 3.0, (), jnp.float32)
    cotangent = bell_draw(splits[14], (MICRO, ROWS, ROW, D), 1.0, 6.0, ((1, 8), (2, 2)))
    return {"tokens": tokens, "patch_meta": patch_meta, "attn_norm_gain": attn_norm_gain, "attn_norm_bias": attn_norm_bias, "qkv_weight": qkv_weight, "qkv_bias": qkv_bias, "proj_weight": proj_weight, "proj_bias": proj_bias, "mlp_norm_gain": mlp_norm_gain, "mlp_norm_bias": mlp_norm_bias, "fc1_weight": fc1_weight, "fc1_bias": fc1_bias, "fc2_weight": fc2_weight, "fc2_bias": fc2_bias, "cotangent": cotangent}


norm_epsilon = 1e-06
gelu_factor = 1.702
rope_base = 10000.0
highest = lax.Precision.HIGHEST

@jax.custom_vjp
def low(v):
    return lax.optimization_barrier(v.astype(jnp.bfloat16)).astype(jnp.float32)

@jax.custom_vjp
def low_back(v):
    return v

def low_keep(v):
    return (low(v), None)

def low_pass(kept, grad):
    return (grad,)

def back_keep(v):
    return (v, None)

def back_low(kept, grad):
    return (low(grad),)
low.defvjp(low_keep, low_pass)
low_back.defvjp(back_keep, back_low)

def layer_norm(values, gain, shift):
    center = values - lax.optimization_barrier(jnp.mean(values, -1, keepdims=True))
    spread = lax.optimization_barrier(jnp.mean(center * center, -1, keepdims=True))
    return center * lax.rsqrt(spread + norm_epsilon) * gain + shift

def rope_tables(patch_row, patch_col, head_size):
    quarter = head_size // 4
    frequency = rope_base ** (-2.0 * jnp.arange(quarter, dtype=jnp.float32) / (head_size // 2))
    angles = jnp.concatenate([patch_row.astype(jnp.float32)[:, None] * frequency[None, :], patch_col.astype(jnp.float32)[:, None] * frequency[None, :]], axis=1)
    angles = jnp.concatenate([angles, angles], axis=1)
    return (jnp.cos(angles)[:, None, :], jnp.sin(angles)[:, None, :])

def rotate_half(tensor):
    half_size = tensor.shape[-1] // 2
    return jnp.concatenate([-tensor[..., half_size:], tensor[..., :half_size]], axis=-1)

def apply_rope(tensor, cosine, sine_table):
    return tensor * cosine + rotate_half(tensor) * sine_table

def forward(params, inputs, picture, cosine, sine_table):
    attn_gain, attn_shift, qkv_mat, qkv_shift, proj_mat, proj_shift, mlp_gain, mlp_shift, first_mat, first_shift, second_mat, second_shift = params
    length = inputs.shape[0]
    normed = low(layer_norm(inputs, attn_gain, attn_shift))
    projected = low_back(jnp.einsum('nd,cde->cne', normed, qkv_mat, precision=highest) + qkv_shift[:, None, :])
    query = low(apply_rope(projected[0].reshape(length, HEADS, HDIM), cosine, sine_table))
    key_part = low(apply_rope(projected[1].reshape(length, HEADS, HDIM), cosine, sine_table))
    value_part = low(projected[2].reshape(length, HEADS, HDIM))
    logits = low_back(jnp.einsum('qhd,khd->hqk', query, key_part, precision=highest) * (1.0 / math.sqrt(HDIM)))
    allowed = picture[:, None] == picture[None, :]
    logits = jnp.where(allowed[None, :, :], logits, -1e+30)
    probs_low = low(jax.nn.softmax(logits, axis=-1))
    mixed = jnp.einsum('hqk,khd->qhd', probs_low, value_part, precision=highest).reshape(length, D)
    mixed = low(low_back(mixed))
    attn_out = low_back(jnp.dot(mixed, proj_mat, precision=highest) + proj_shift)
    hidden = inputs + attn_out
    normed_two = low(layer_norm(hidden, mlp_gain, mlp_shift))
    pre_act = low_back(jnp.dot(normed_two, first_mat, precision=highest) + first_shift)
    activated = low(pre_act * jax.nn.sigmoid(gelu_factor * pre_act))
    mlp_out = low_back(jnp.dot(activated, second_mat, precision=highest) + second_shift)
    return hidden + mlp_out

def reference(tokens, patch_meta, attn_norm_gain, attn_norm_bias, qkv_weight, qkv_bias, proj_weight, proj_bias, mlp_norm_gain, mlp_norm_bias, fc1_weight, fc1_bias, fc2_weight, fc2_bias, cotangent):
    params = tuple((entry.astype(jnp.float32) for entry in (attn_norm_gain, attn_norm_bias, qkv_weight, qkv_bias, proj_weight, proj_bias, mlp_norm_gain, mlp_norm_bias, fc1_weight, fc1_bias, fc2_weight, fc2_bias)))
    row_count = MICRO * ROWS
    inputs = tokens.astype(jnp.float32).reshape(row_count, ROW, D)
    incoming = cotangent.astype(jnp.float32).reshape(row_count, ROW, D)
    meta_rows = patch_meta.reshape(3, row_count, ROW)

    def one_row(running_sum, sample_row):
        row_input, row_cotangent, picture, patch_row, patch_col = sample_row
        cosine, sine_table = rope_tables(patch_row, patch_col, HDIM)
        result, pullback = jax.vjp(lambda weights_in, values: forward(weights_in, values, picture, cosine, sine_table), params, row_input)
        grad_params, grad_input = pullback(row_cotangent)
        running_sum = jax.tree.map(lambda earlier, fresh: earlier + fresh, running_sum, grad_params)
        return (running_sum, (result.astype(jnp.bfloat16), grad_input))
    zero_grads = jax.tree.map(jnp.zeros_like, params)
    totals, (outputs, input_grads) = lax.scan(one_row, zero_grads, (inputs, incoming, meta_rows[0], meta_rows[1], meta_rows[2]))
    shape_out = (MICRO, ROWS, ROW, D)
    return (outputs.reshape(shape_out), input_grads.reshape(shape_out), totals[0], totals[1], totals[2], totals[3], totals[4], totals[5], totals[6], totals[7], totals[8], totals[9], totals[10], totals[11])
```

```python
import functools
import math

import jax
import jax.numpy as jnp
from jax import lax
from jax.experimental import pallas as pl
from jax.experimental.pallas import tpu as pltpu
from jax.sharding import PartitionSpec as P

HDIM = 80
NORM_EPS = 1e-06
GELU = 1.702
ROPE_BASE = 10000.0
SCALE = 1.0 / math.sqrt(HDIM)
LOG2E = 1.0 / math.log(2.0)
NEG = -1e30
F32 = jnp.float32
BF16 = jnp.bfloat16
AXES = ("shard", "ctx", "tp")
QB = 256


def dg(left, right, dims, out=F32):
    return lax.dot_general(left, right, (dims, ((), ())), preferred_element_type=F32).astype(out)


def rope_rows(t, cosine, sine):
    half = t.shape[0] // 2
    first, second = t[:half], t[half:]
    return jnp.concatenate([first * cosine - second * sine, second * cosine + first * sine], axis=0)


def rope_rows_back(t, cosine, sine):
    half = t.shape[0] // 2
    first, second = t[:half], t[half:]
    return jnp.concatenate([first * cosine + second * sine, second * cosine - first * sine], axis=0)


def fill_bias(bias, idc_ref, idr_ref):
    @pl.when(pl.program_id(0) == 0)
    def _():
        bias[...] = jnp.where(idc_ref[...] == idr_ref[...], 0.0, NEG)


def attend_kernel(x_ref, cos_ref, sin_ref, idc_ref, idr_ref, low_ref, out_ref, outf_ref, lse_ref, bias):
    fill_bias(bias, idc_ref, idr_ref)
    cosine, sine = cos_ref[...], sin_ref[...]
    query = rope_rows(x_ref[0], cosine, sine).astype(BF16)
    key_f = rope_rows(x_ref[1], cosine, sine)
    value = x_ref[2].astype(BF16)
    low_ref[0] = query
    low_ref[1] = key_f.astype(BF16)
    low_ref[2] = value
    key_nat = key_f.T.astype(BF16)
    length = query.shape[1]
    factor = SCALE * LOG2E
    for start in range(0, length, QB):
        cols = slice(start, start + QB)
        logits = dg(key_nat, query[:, cols], ((1,), (0,))) + bias[:, cols]
        peak = jnp.max(logits, axis=0, keepdims=True)
        probs = jnp.exp2((logits - peak) * factor)
        total = jnp.sum(probs, axis=0, keepdims=True)
        mixed = dg(value, probs.astype(BF16), ((1,), (0,))) * (1.0 / total)
        out_ref[:, cols] = mixed.astype(BF16)
        outf_ref[:, cols] = mixed
        lse_ref[0, :, cols] = peak * factor + jnp.log2(total)


def attend(qkv, cosine, sine, ids):
    _, width, length = qkv.shape
    heads = width // HDIM
    half = HDIM // 2
    head = lambda h: (0, h, 0)
    whole = lambda h: (0, 0)
    return pl.pallas_call(
        attend_kernel,
        grid=(heads,),
        in_specs=[
            pl.BlockSpec((3, HDIM, length), head),
            pl.BlockSpec((half, length), whole),
            pl.BlockSpec((half, length), whole),
            pl.BlockSpec((length, 1), whole),
            pl.BlockSpec((1, length), whole),
        ],
        out_specs=[
            pl.BlockSpec((3, HDIM, length), head),
            pl.BlockSpec((HDIM, length), lambda h: (h, 0)),
            pl.BlockSpec((HDIM, length), lambda h: (h, 0)),
            pl.BlockSpec((1, 1, length), lambda h: (h, 0, 0)),
        ],
        out_shape=[
            jax.ShapeDtypeStruct((3, width, length), BF16),
            jax.ShapeDtypeStruct((width, length), BF16),
            jax.ShapeDtypeStruct((width, length), F32),
            jax.ShapeDtypeStruct((heads, 1, length), F32),
        ],
        scratch_shapes=[pltpu.VMEM((length, length), F32)],
        compiler_params=pltpu.CompilerParams(vmem_limit_bytes=48 << 20),
        cost_estimate=pl.CostEstimate(
            flops=4 * width * length * length,
            transcendentals=heads * length * length,
            bytes_accessed=26 * width * length,
        ),
        name="attend",
    )(qkv, cosine, sine, ids[:, None], ids[None, :])


def attend_back_kernel(
    low_ref, grad_ref, outf_ref, lse_ref, cos_ref, sin_ref, idc_ref, idr_ref, dproj_ref, bias, dq, dk, dv
):
    fill_bias(bias, idc_ref, idr_ref)
    cosine, sine = cos_ref[...], sin_ref[...]
    query, key = low_ref[0], low_ref[1]
    grad = grad_ref[...]
    grad_f = grad.astype(F32)
    delta = jnp.sum(grad_f * outf_ref[...], axis=0, keepdims=True)
    nat = lambda t: t.astype(F32).T.astype(BF16)
    query_nat, key_nat, value_nat, grad_nat = nat(query), nat(key), nat(low_ref[2]), nat(grad)
    lse = lse_ref[0]
    length = query.shape[1]
    factor = SCALE * LOG2E
    for start in range(0, length, QB):
        cols = slice(start, start + QB)
        logits = dg(key_nat, query[:, cols], ((1,), (0,)))
        probs = jnp.exp2(logits * factor + bias[:, cols] - lse[:, cols])
        d_probs = dg(value_nat, grad[:, cols], ((1,), (0,)))
        d_logits = (probs * (d_probs - delta[:, cols])).astype(BF16)
        part_v = dg(probs.astype(BF16), grad_nat[cols], ((1,), (0,)))
        part_k = dg(d_logits, query_nat[cols], ((1,), (0,)))
        dq[:, cols] = dg(key, d_logits, ((1,), (0,)))
        if start == 0:
            dv[...] = part_v
            dk[...] = part_k
        else:
            dv[...] += part_v
            dk[...] += part_k
    dproj_ref[0] = rope_rows_back(dq[...] * SCALE, cosine, sine).astype(BF16)
    dproj_ref[1] = rope_rows_back(dk[...].T * SCALE, cosine, sine).astype(BF16)
    dproj_ref[2] = dv[...].T.astype(BF16)


def attend_back(low, grad, outf, lse, cosine, sine, ids):
    _, width, length = low.shape
    heads = width // HDIM
    half = HDIM // 2
    head = lambda h: (0, h, 0)
    whole = lambda h: (0, 0)
    return pl.pallas_call(
        attend_back_kernel,
        grid=(heads,),
        in_specs=[
            pl.BlockSpec((3, HDIM, length), head),
            pl.BlockSpec((HDIM, length), lambda h: (h, 0)),
            pl.BlockSpec((HDIM, length), lambda h: (h, 0)),
            pl.BlockSpec((1, 1, length), lambda h: (h, 0, 0)),
            pl.BlockSpec((half, length), whole),
            pl.BlockSpec((half, length), whole),
            pl.BlockSpec((length, 1), whole),
            pl.BlockSpec((1, length), whole),
        ],
        out_specs=pl.BlockSpec((3, HDIM, length), head),
        out_shape=jax.ShapeDtypeStruct((3, width, length), BF16),
        scratch_shapes=[
            pltpu.VMEM((length, length), F32),
            pltpu.VMEM((HDIM, length), F32),
            pltpu.VMEM((length, HDIM), F32),
            pltpu.VMEM((length, HDIM), F32),
        ],
        compiler_params=pltpu.CompilerParams(vmem_limit_bytes=48 << 20),
        cost_estimate=pl.CostEstimate(
            flops=10 * width * length * length,
            transcendentals=heads * length * length,
            bytes_accessed=18 * width * length,
        ),
        name="attend_back",
    )(low, grad, outf, lse, cosine, sine, ids[:, None], ids[None, :])


def rope_tables(patch_row, patch_col):
    quarter = HDIM // 4
    frequency = ROPE_BASE ** (-2.0 * jnp.arange(quarter, dtype=F32) / (HDIM // 2))
    angles = jnp.concatenate(
        [
            frequency[:, None] * patch_row.astype(F32)[None, :],
            frequency[:, None] * patch_col.astype(F32)[None, :],
        ],
        axis=0,
    )
    return jnp.cos(angles), jnp.sin(angles)


def norm_stats(values):
    center = values - jnp.mean(values, -1, keepdims=True)
    spread = jnp.mean(center * center, -1, keepdims=True)
    inverse = lax.rsqrt(spread + NORM_EPS)
    return center * inverse, inverse


def norm_back(grad_out, normal, inverse, gain):
    scaled = grad_out * gain
    return inverse * (
        scaled
        - jnp.mean(scaled, -1, keepdims=True)
        - normal * jnp.mean(scaled * normal, -1, keepdims=True)
    )


class Links:
    def __init__(self, shards):
        self.shards = shards
        self.lines = shards // 2
        self.s = lax.axis_index("shard")
        self.c = lax.axis_index("ctx")
        self.y = lax.axis_index("tp")
        self.line = self.s // 2
        self.side = self.s % 2
        self.diag = self.c == self.y

    def send(self, value, target, where=lambda c, y: True):
        flat = lambda s, c, y: (s * 2 + c) * 2 + y
        pairs = []
        for s in range(self.shards):
            for c in range(2):
                for y in range(2):
                    if where(c, y):
                        pairs.append((flat(s, c, y), flat(*target(s, c, y))))
        return lax.ppermute(value, AXES, pairs)

    def core(self, value):
        return self.send(value, lambda s, c, y: (s, 1 - c, y))

    def across(self, value, where=lambda c, y: True):
        return self.send(value, lambda s, c, y: (s, c, 1 - y), where)

    def beside(self, value, where=lambda c, y: True):
        return self.send(value, lambda s, c, y: (s ^ 1, c, y), where)

    def along(self, value, step, where=lambda c, y: True):
        lines = self.lines
        return self.send(value, lambda s, c, y: (((s // 2 + step) % lines) * 2 + s % 2, c, y), where)

    def gather(self, block, where=lambda c, y: True):
        near = [block] + [self.along(block, k, where) for k in range(1, self.lines)]
        far = [self.beside(piece, where) for piece in near]
        return near, far

    def place(self, near, far):
        full = jnp.zeros((self.shards,) + near[0].shape, near[0].dtype)
        for k in range(self.lines):
            row = ((self.line - k) % self.lines) * 2
            full = lax.dynamic_update_index_in_dim(full, near[k], row + self.side, 0)
            full = lax.dynamic_update_index_in_dim(full, far[k], row + 1 - self.side, 0)
        return full

    def scatter(self, blocks, where=lambda c, y: True):
        pick = lambda t, i, d: lax.dynamic_index_in_dim(t, i, d, False)
        other = pick(blocks, 1 - self.side, 1)
        mine = pick(blocks, self.side, 1).astype(F32) + self.beside(other, where).astype(F32)
        low = mine.astype(BF16)
        total = pick(mine, self.line, 0)
        for k in range(1, self.lines):
            piece = pick(low, (self.line + k) % self.lines, 0)
            total = total + self.along(piece, k, where).astype(F32)
        return total


def on_diag(c, y):
    return c == y


def off_diag(c, y):
    return c != y


def per_device(
    tokens,
    patch_meta,
    attn_norm_gain,
    attn_norm_bias,
    qkv_weight,
    qkv_bias,
    proj_weight,
    proj_bias,
    mlp_norm_gain,
    mlp_norm_bias,
    fc1_weight,
    fc1_bias,
    fc2_weight,
    fc2_bias,
    cotangent,
    *,
    shards,
):
    net = Links(shards)
    c, y = net.c, net.y
    local = tokens.shape[2]
    width = tokens.shape[3]
    full = patch_meta.shape[3]
    inner = qkv_weight.shape[2]
    rows = width // shards
    quarter = fc1_weight.shape[1] // 2
    pick = lambda t, i, d=0: lax.dynamic_index_in_dim(t, i, d, False)
    mine_or = lambda own, other: jnp.where(net.diag, own, other)

    def both(own, other, index):
        return jnp.where(index == 0, jnp.stack([own, other]), jnp.stack([other, own]))

    attn_block = jnp.concatenate([qkv_weight, proj_weight.T[None]], axis=0)
    early = attn_block[3:]
    early_peer = net.across(early, on_diag)
    late_near, late_far = net.gather(attn_block[:3], on_diag)
    early_near, early_far = net.gather(mine_or(early, early_peer))
    late_near_peer = [net.across(p, on_diag) for p in late_near]
    late_far_peer = [net.across(p, on_diag) for p in late_far]
    late_near = [mine_or(p, q) for p, q in zip(late_near, late_near_peer)]
    late_far = [mine_or(p, q) for p, q in zip(late_far, late_far_peer)]
    qkv_full = jnp.moveaxis(net.place(late_near, late_far), 0, 1).reshape(3, width, inner)
    proj_full = net.place(early_near, early_far).reshape(width, inner)

    fc1_block = lax.dynamic_slice_in_dim(fc1_weight, c * quarter, quarter, 1)
    fc2_block = lax.dynamic_slice_in_dim(fc2_weight, c * quarter, quarter, 0).T
    fc1_full = net.place(*net.gather(fc1_block)).reshape(width, quarter)
    fc2_full = net.place(*net.gather(fc2_block)).reshape(width, quarter)
    bias_qkv = mine_or(qkv_bias, net.across(qkv_bias, on_diag))
    bias_fc1 = lax.dynamic_slice_in_dim(fc1_bias, c * quarter, quarter, 0)

    inputs = pick(tokens, y).reshape(local, width).astype(F32)
    normal_one, inverse_one = norm_stats(inputs)
    normed_own = (normal_one * attn_norm_gain + attn_norm_bias).astype(BF16)
    normed = both(normed_own, net.core(normed_own), c).reshape(full, width)
    meta = pick(patch_meta, y, 1).reshape(3, full)
    ids = meta[0]
    cosine, sine = rope_tables(meta[1], meta[2])
    qkv = (
        jnp.einsum("cde,rd->cer", qkv_full, normed, preferred_element_type=F32)
        + bias_qkv[:, :, None]
    )
    low, mixed, mixed_f, lse = attend(qkv, cosine, sine, ids)
    attn_part = dg(mixed, proj_full, ((0,), (1,))).reshape(2, local, width)
    attn_own = pick(attn_part, c) + net.core(pick(attn_part, 1 - c))
    hidden = inputs + attn_own + proj_bias

    normal_two, inverse_two = norm_stats(hidden)
    two_own = (normal_two * mlp_norm_gain + mlp_norm_bias).astype(BF16)
    two_peer = net.across(two_own)
    two = [
        jnp.concatenate([two_own, net.core(two_own)]),
        jnp.concatenate([two_peer, net.core(two_peer)]),
    ]
    grad_out = cotangent.reshape(2, local, width)
    grad_out_sib = net.core(grad_out)
    dy_own = pick(grad_out, y)
    dy = [jnp.concatenate([pick(grad_out, m), pick(grad_out_sib, m)]) for m in (y, 1 - y)]

    acts, d_pres, d_twos = [], [], []
    for part, dy_part in zip(two, dy):
        pre = dg(part, fc1_full, ((1,), (0,))) + bias_fc1
        sig = jax.nn.sigmoid(GELU * pre)
        acts.append((pre * sig).astype(BF16))
        d_act = dg(dy_part, fc2_full, ((1,), (0,)))
        d_pre = (d_act * (sig + GELU * pre * sig * (1.0 - sig))).astype(BF16)
        d_pres.append(d_pre)
        d_twos.append(dg(d_pre, fc1_full, ((1,), (1,))))

    def reduce_slots(parts):
        own, other = parts
        other = other[:local] + net.core(other[local:].astype(BF16)).astype(F32)
        from_peer = net.across(other.astype(BF16)).astype(F32)
        own = own[:local] + net.core(own[local:].astype(BF16)).astype(F32)
        return own + from_peer

    d_two = reduce_slots(d_twos)
    mlp_out = reduce_slots([dg(a, fc2_full, ((1,), (1,))) for a in acts])
    out_own = (hidden + mlp_out + fc2_bias).astype(BF16)
    block_output = both(out_own, net.across(out_own), y)

    def weight_sum(lefts, rights):
        total = sum(dg(l, r, ((0,), (0,))) for l, r in zip(lefts, rights))
        return total.astype(BF16).reshape(net.lines, 2, rows, quarter)

    def all_hidden(block):
        return both(block, net.core(block), c)

    grad_fc2 = all_hidden(net.scatter(weight_sum(dy, acts)))
    grad_fc1 = all_hidden(net.scatter(weight_sum(two, d_pres)))
    grad_fc1 = jnp.moveaxis(grad_fc1, 0, 1).reshape(rows, 2 * quarter)
    grad_fc2 = jnp.moveaxis(grad_fc2, 1, 2).reshape(2 * quarter, rows)

    d_hidden = dy_own.astype(F32) + norm_back(d_two, normal_two, inverse_two, mlp_norm_gain)
    d_attn_own = d_hidden.astype(BF16)
    d_attn = both(d_attn_own, net.core(d_attn_own), c).reshape(full, width)
    grad_proj_part = dg(d_attn, mixed, ((0,), (1,)), BF16)
    d_mixed = dg(proj_full, d_attn, ((0,), (1,)), BF16)
    d_proj = attend_back(low, d_mixed, mixed_f, lse, cosine, sine, ids)
    grad_qkv_part = jnp.einsum("cer,rd->cde", d_proj, normed, preferred_element_type=F32).astype(BF16)
    d_one_part = jnp.einsum("cer,cde->rd", d_proj, qkv_full, preferred_element_type=F32)
    d_one_part = d_one_part.reshape(2, local, width)
    d_one = pick(d_one_part, c) + net.core(pick(d_one_part, 1 - c))
    grad_in = d_hidden + norm_back(d_one, normal_one, inverse_one, attn_norm_gain)
    grad_in = grad_in.astype(BF16)
    input_grad = both(grad_in, net.across(grad_in), y).astype(F32)

    proj_plane = net.scatter(grad_proj_part.reshape(net.lines, 2, rows, inner))
    proj_sum = proj_plane + net.across(proj_plane.astype(BF16), off_diag).astype(F32)
    qkv_pair = grad_qkv_part.astype(F32) + net.across(grad_qkv_part, off_diag).astype(F32)
    qkv_pair = jnp.moveaxis(qkv_pair.astype(BF16).reshape(3, net.lines, 2, rows, inner), 0, 2)
    qkv_sum = net.scatter(qkv_pair, on_diag)
    attn_sum = jnp.concatenate([qkv_sum, proj_sum[None]])
    attn_sum = mine_or(attn_sum, net.send(attn_sum, lambda s, c, y: (s, 1 - c, y), on_diag))
    grad_qkv, grad_proj = attn_sum[:3], attn_sum[3].T

    sums = lambda t: jnp.sum(t.astype(F32), axis=0)
    qkv_shift = jnp.sum(d_proj.astype(F32), axis=2)
    fc1_shift = sum(sums(d) for d in d_pres)
    zero_qkv, zero_fc1 = jnp.zeros_like(qkv_shift), jnp.zeros_like(fc1_shift)
    small = jnp.concatenate(
        [
            sums(d_one * normal_one),
            sums(d_one),
            sums(d_attn_own),
            sums(d_two * normal_two),
            sums(d_two),
            sums(dy_own),
            jnp.where(c == 0, qkv_shift, zero_qkv).reshape(-1),
            jnp.where(c == 1, qkv_shift, zero_qkv).reshape(-1),
        ]
        + [jnp.where((y == i) & (c == j), fc1_shift, zero_fc1) for i in range(2) for j in range(2)]
    )
    small = lax.psum(small, AXES)
    vec = lambda i: small[i * width : (i + 1) * width]
    at = 6 * width
    qkv_shifts = small[at : at + 6 * inner].reshape(2, 3, inner)
    fc1_shifts = small[at + 6 * inner :].reshape(2, 2 * quarter)
    out_shape = tokens.shape
    return (
        block_output.reshape(out_shape),
        input_grad.reshape(out_shape),
        vec(0),
        vec(1),
        grad_qkv,
        pick(qkv_shifts, y),
        grad_proj,
        vec(2),
        vec(3),
        vec(4),
        grad_fc1,
        pick(fc1_shifts, y),
        grad_fc2,
        vec(5),
    )


def solution(mesh):
    slots = P(None, "shard", "ctx", None)
    placed = (
        slots,
        P(None, None, "shard", None),
        P(),
        P(),
        P(None, "shard", "tp"),
        P(None, "tp"),
        P("tp", "shard"),
        P(),
        P(),
        P(),
        P("shard", "tp"),
        P("tp"),
        P("tp", "shard"),
        P(),
        slots,
    )
    return jax.shard_map(
        functools.partial(per_device, shards=mesh.shape["shard"]),
        mesh=mesh,
        in_specs=placed,
        out_specs=(
            slots,
            slots,
            P(),
            P(),
            P(None, "shard", "tp"),
            P(None, "tp"),
            P("tp", "shard"),
            P(),
            P(),
            P(),
            P("shard", "tp"),
            P("tp"),
            P("tp", "shard"),
            P(),
        ),
        check_vma=False,
    )
```

```python
import functools
import math

import jax
import jax.numpy as jnp
from jax import lax
from jax.experimental import pallas as pl
from jax.experimental.pallas import tpu as pltpu
from jax.sharding import PartitionSpec as P

HDIM = 80
NORM_EPS = 1e-06
GELU = 1.702
ROPE_BASE = 10000.0
SCALE = 1.0 / math.sqrt(HDIM)
LOG2E = 1.0 / math.log(2.0)
NEG = -1e30
F32 = jnp.float32
BF16 = jnp.bfloat16
AXES = ("shard", "ctx", "tp")
QB = 256


def dg(left, right, dims, out=F32):
    return lax.dot_general(left, right, (dims, ((), ())), preferred_element_type=F32).astype(out)


def rope_rows(t, cosine, sine):
    half = t.shape[0] // 2
    first, second = t[:half], t[half:]
    return jnp.concatenate([first * cosine - second * sine, second * cosine + first * sine], axis=0)


def rope_rows_back(t, cosine, sine):
    half = t.shape[0] // 2
    first, second = t[:half], t[half:]
    return jnp.concatenate([first * cosine + second * sine, second * cosine - first * sine], axis=0)


def fill_bias(bias, idc_ref, idr_ref):
    @pl.when(pl.program_id(0) == 0)
    def _():
        bias[...] = jnp.where(idc_ref[...] == idr_ref[...], 0.0, NEG)


def attend_kernel(x_ref, cos_ref, sin_ref, idc_ref, idr_ref, low_ref, out_ref, outf_ref, lse_ref, bias):
    fill_bias(bias, idc_ref, idr_ref)
    cosine, sine = cos_ref[...], sin_ref[...]
    query = rope_rows(x_ref[0], cosine, sine).astype(BF16)
    key_f = rope_rows(x_ref[1], cosine, sine)
    value = x_ref[2].astype(BF16)
    low_ref[0] = query
    low_ref[1] = key_f.astype(BF16)
    low_ref[2] = value
    key_nat = key_f.T.astype(BF16)
    length = query.shape[1]
    factor = SCALE * LOG2E
    for start in range(0, length, QB):
        cols = slice(start, start + QB)
        logits = dg(key_nat, query[:, cols], ((1,), (0,))) + bias[:, cols]
        peak = jnp.max(logits, axis=0, keepdims=True)
        probs = jnp.exp2((logits - peak) * factor)
        total = jnp.sum(probs, axis=0, keepdims=True)
        mixed = dg(value, probs.astype(BF16), ((1,), (0,))) * (1.0 / total)
        out_ref[:, cols] = mixed.astype(BF16)
        outf_ref[:, cols] = mixed
        lse_ref[0, :, cols] = peak * factor + jnp.log2(total)


def attend(qkv, cosine, sine, ids):
    _, width, length = qkv.shape
    heads = width // HDIM
    half = HDIM // 2
    head = lambda h: (0, h, 0)
    whole = lambda h: (0, 0)
    return pl.pallas_call(
        attend_kernel,
        grid=(heads,),
        in_specs=[
            pl.BlockSpec((3, HDIM, length), head),
            pl.BlockSpec((half, length), whole),
            pl.BlockSpec((half, length), whole),
            pl.BlockSpec((length, 1), whole),
            pl.BlockSpec((1, length), whole),
        ],
        out_specs=[
            pl.BlockSpec((3, HDIM, length), head),
            pl.BlockSpec((HDIM, length), lambda h: (h, 0)),
            pl.BlockSpec((HDIM, length), lambda h: (h, 0)),
            pl.BlockSpec((1, 1, length), lambda h: (h, 0, 0)),
        ],
        out_shape=[
            jax.ShapeDtypeStruct((3, width, length), BF16),
            jax.ShapeDtypeStruct((width, length), BF16),
            jax.ShapeDtypeStruct((width, length), F32),
            jax.ShapeDtypeStruct((heads, 1, length), F32),
        ],
        scratch_shapes=[pltpu.VMEM((length, length), F32)],
        compiler_params=pltpu.CompilerParams(vmem_limit_bytes=48 << 20),
        cost_estimate=pl.CostEstimate(
            flops=4 * width * length * length,
            transcendentals=heads * length * length,
            bytes_accessed=26 * width * length,
        ),
        name="attend",
    )(qkv, cosine, sine, ids[:, None], ids[None, :])


def attend_back_kernel(
    low_ref, grad_ref, outf_ref, lse_ref, cos_ref, sin_ref, idc_ref, idr_ref, dproj_ref, bias, dq, dk, dv
):
    fill_bias(bias, idc_ref, idr_ref)
    cosine, sine = cos_ref[...], sin_ref[...]
    query, key = low_ref[0], low_ref[1]
    grad = grad_ref[...]
    grad_f = grad.astype(F32)
    delta = jnp.sum(grad_f * outf_ref[...], axis=0, keepdims=True)
    nat = lambda t: t.astype(F32).T.astype(BF16)
    query_nat, key_nat, value_nat, grad_nat = nat(query), nat(key), nat(low_ref[2]), nat(grad)
    lse = lse_ref[0]
    length = query.shape[1]
    factor = SCALE * LOG2E
    for start in range(0, length, QB):
        cols = slice(start, start + QB)
        logits = dg(key_nat, query[:, cols], ((1,), (0,)))
        probs = jnp.exp2(logits * factor + bias[:, cols] - lse[:, cols])
        d_probs = dg(value_nat, grad[:, cols], ((1,), (0,)))
        d_logits = (probs * (d_probs - delta[:, cols])).astype(BF16)
        part_v = dg(probs.astype(BF16), grad_nat[cols], ((1,), (0,)))
        part_k = dg(d_logits, query_nat[cols], ((1,), (0,)))
        dq[:, cols] = dg(key, d_logits, ((1,), (0,)))
        if start == 0:
            dv[...] = part_v
            dk[...] = part_k
        else:
            dv[...] += part_v
            dk[...] += part_k
    dproj_ref[0] = rope_rows_back(dq[...] * SCALE, cosine, sine).astype(BF16)
    dproj_ref[1] = rope_rows_back(dk[...].T * SCALE, cosine, sine).astype(BF16)
    dproj_ref[2] = dv[...].T.astype(BF16)


def attend_back(low, grad, outf, lse, cosine, sine, ids):
    _, width, length = low.shape
    heads = width // HDIM
    half = HDIM // 2
    head = lambda h: (0, h, 0)
    whole = lambda h: (0, 0)
    return pl.pallas_call(
        attend_back_kernel,
        grid=(heads,),
        in_specs=[
            pl.BlockSpec((3, HDIM, length), head),
            pl.BlockSpec((HDIM, length), lambda h: (h, 0)),
            pl.BlockSpec((HDIM, length), lambda h: (h, 0)),
            pl.BlockSpec((1, 1, length), lambda h: (h, 0, 0)),
            pl.BlockSpec((half, length), whole),
            pl.BlockSpec((half, length), whole),
            pl.BlockSpec((length, 1), whole),
            pl.BlockSpec((1, length), whole),
        ],
        out_specs=pl.BlockSpec((3, HDIM, length), head),
        out_shape=jax.ShapeDtypeStruct((3, width, length), BF16),
        scratch_shapes=[
            pltpu.VMEM((length, length), F32),
            pltpu.VMEM((HDIM, length), F32),
            pltpu.VMEM((length, HDIM), F32),
            pltpu.VMEM((length, HDIM), F32),
        ],
        compiler_params=pltpu.CompilerParams(vmem_limit_bytes=48 << 20),
        cost_estimate=pl.CostEstimate(
            flops=10 * width * length * length,
            transcendentals=heads * length * length,
            bytes_accessed=18 * width * length,
        ),
        name="attend_back",
    )(low, grad, outf, lse, cosine, sine, ids[:, None], ids[None, :])


def rope_tables(patch_row, patch_col):
    quarter = HDIM // 4
    frequency = ROPE_BASE ** (-2.0 * jnp.arange(quarter, dtype=F32) / (HDIM // 2))
    angles = jnp.concatenate(
        [
            frequency[:, None] * patch_row.astype(F32)[None, :],
            frequency[:, None] * patch_col.astype(F32)[None, :],
        ],
        axis=0,
    )
    return jnp.cos(angles), jnp.sin(angles)


MESH = pl.DeviceIdType.MESH


def remote(src, dst, send_sem, recv_sem, device):
    return pltpu.make_async_remote_copy(
        src_ref=src,
        dst_ref=dst,
        send_sem=send_sem,
        recv_sem=recv_sem,
        device_id=device,
        device_id_type=MESH,
    )


class Place:
    def __init__(self, lines):
        self.lines = lines
        self.s = lax.axis_index("shard")
        self.c = lax.axis_index("ctx")
        self.y = lax.axis_index("tp")
        self.line = self.s // 2
        self.side = lax.rem(self.s, 2)
        self.sib = (self.s, 1 - self.c, self.y)
        self.peer = (self.s, self.c, 1 - self.y)
        self.beside = (self.line * 2 + 1 - self.side, self.c, self.y)

    def ahead(self, k):
        return (lax.rem(self.line + k, self.lines) * 2 + self.side, self.c, self.y)

    def source(self, k):
        return lax.rem(self.line + self.lines - k, self.lines) * 2

    def greet(self):
        barrier = pltpu.get_barrier_semaphore()
        others = [self.sib, self.peer, self.beside] + [self.ahead(k) for k in range(1, self.lines)]
        for other in others:
            pl.semaphore_signal(barrier, inc=1, device_id=other, device_id_type=MESH)
        pl.semaphore_wait(barrier, len(others))


def norm_rows(values):
    center = values - jnp.mean(values, -1, keepdims=True)
    spread = jnp.mean(center * center, -1, keepdims=True)
    return center * lax.rsqrt(spread + NORM_EPS)


def collect_kernel(
    lines, pieces, block, tok, gain, shift, dy, qb,
    out, normed, dy_sib, qb_out,
    norm_buf, own_sem, zs, zr, xs, xr, ys, yr, ms, mr,
):
    at = Place(lines)
    diag = at.c == at.y

    def part(p, s):
        j, first, count, _ = pieces[p]
        return out.at[j, s, :, pl.ds(first, count)]

    def own(p):
        j, first, count, _ = pieces[p]
        return block.at[j, :, pl.ds(first, count)]

    def z_copy(p, k, src):
        return remote(src, part(p, at.s), zs.at[p, k], zr.at[p, k], at.ahead(k))

    def x_copy(p, k, src):
        return remote(src, part(p, at.source(k) + at.side), xs.at[p, k], xr.at[p, k], at.beside)

    def y_copy(p, i, src, s):
        return remote(src, part(p, s), ys.at[p, i], yr.at[p, i], at.peer)

    def near(k):
        return at.source(k) + at.side

    def far(k):
        return at.source(k) + 1 - at.side

    def z_wait(p, k):
        z_copy(p, k, part(p, near(k))).wait_recv()

    def x_wait(p, k):
        x_copy(p, k, part(p, far(k))).wait_recv()

    def y_wait(p, i, s):
        y_copy(p, i, part(p, s), s).wait_recv()

    late = [p for p in range(len(pieces)) if pieces[p][3]]
    early = [p for p in range(len(pieces)) if not pieces[p][3]]
    order = late + early
    at.greet()

    own_copy = pltpu.make_async_copy(block, out.at[:, at.s], own_sem.at[0])
    bias_copy = pltpu.make_async_copy(qb, qb_out, own_sem.at[1])

    @pl.when(diag)
    def _():
        own_copy.start()
        bias_copy.start()
        remote(qb, qb_out, ms.at[0], mr.at[0], at.peer).start()
        for p in early:
            y_copy(p, 0, own(p), at.s).start()
        for p in order:
            for k in range(1, lines):
                z_copy(p, k, own(p)).start()
            x_copy(p, 0, own(p)).start()
            if p in late:
                y_copy(p, 0, own(p), at.s).start()

    dy_copy = remote(dy, dy_sib, ms.at[1], mr.at[1], at.sib)
    dy_copy.start()
    norm_buf[...] = (norm_rows(tok[...].astype(F32)) * gain[...] + shift[...]).astype(BF16)
    norm_copy = remote(norm_buf, normed.at[at.c], ms.at[2], mr.at[2], at.sib)
    norm_copy.start()
    norm_keep = pltpu.make_async_copy(norm_buf, normed.at[at.c], own_sem.at[2])
    norm_keep.start()

    @pl.when(diag)
    def _():
        for step in range(len(order) + 1):
            if step < len(order):
                p = order[step]
                for k in range(1, lines):
                    z_wait(p, k)
                    x_copy(p, k, part(p, near(k))).start()
                    if p in late:
                        y_copy(p, k, part(p, near(k)), near(k)).start()
            if step > 0:
                p = order[step - 1]
                for k in range(lines):
                    x_wait(p, k)
                    if p in late:
                        y_copy(p, lines + k, part(p, far(k)), far(k)).start()
        own_copy.wait()
        bias_copy.wait()
        remote(qb, qb_out, ms.at[0], mr.at[0], at.peer).wait_send()
        for p in order:
            for k in range(1, lines):
                z_copy(p, k, own(p)).wait_send()
            for k in range(lines):
                x_copy(p, k, part(p, near(k))).wait_send()
            y_copy(p, 0, own(p), at.s).wait_send()
            if p in late:
                for k in range(1, lines):
                    y_copy(p, k, part(p, near(k)), near(k)).wait_send()
                for k in range(lines):
                    y_copy(p, lines + k, part(p, far(k)), far(k)).wait_send()

    @pl.when(jnp.logical_not(diag))
    def _():
        for p in early:
            y_wait(p, 0, at.s)
            for k in range(1, lines):
                z_copy(p, k, part(p, at.s)).start()
            x_copy(p, 0, part(p, at.s)).start()
        for step in range(len(early) + 1):
            if step < len(early):
                p = early[step]
                for k in range(1, lines):
                    z_wait(p, k)
                    x_copy(p, k, part(p, near(k))).start()
            if step > 0:
                for k in range(lines):
                    x_wait(early[step - 1], k)
        for p in early:
            for k in range(1, lines):
                z_copy(p, k, part(p, at.s)).wait_send()
            for k in range(lines):
                x_copy(p, k, part(p, near(k))).wait_send()
        remote(qb, qb_out, ms.at[0], mr.at[0], at.peer).wait_recv()
        for p in late:
            for k in range(lines):
                y_wait(p, k, near(k))
                y_wait(p, lines + k, far(k))

    dy_copy.wait()
    norm_copy.wait_send()
    remote(norm_buf, normed.at[1 - at.c], ms.at[2], mr.at[2], at.sib).wait_recv()
    norm_keep.wait()


def collect(lines, block, tok, gain, shift, dy, qb):
    groups, rows, inner = block.shape
    local, width = tok.shape
    cut = (inner * 3 // 5) // 128 * 128
    pieces = [(0, 0, inner, True), (1, 0, inner, True), (2, 0, cut, True), (2, cut, inner - cut, False), (3, 0, inner, False)]
    n = len(pieces)
    anywhere = pl.BlockSpec(memory_space=pl.ANY)
    vmem = pl.BlockSpec(memory_space=pltpu.VMEM)
    dma = pltpu.SemaphoreType.DMA
    return pl.pallas_call(
        functools.partial(collect_kernel, lines, pieces),
        in_specs=[anywhere, vmem, vmem, vmem, anywhere, anywhere],
        out_specs=[anywhere] * 4,
        out_shape=[
            jax.ShapeDtypeStruct((groups, 2 * lines, rows, inner), BF16),
            jax.ShapeDtypeStruct((2, local, width), BF16),
            jax.ShapeDtypeStruct(dy.shape, BF16),
            jax.ShapeDtypeStruct(qb.shape, F32),
        ],
        scratch_shapes=[
            pltpu.VMEM((local, width), BF16),
            dma((3,)),
            dma((n, lines)),
            dma((n, lines)),
            dma((n, lines)),
            dma((n, lines)),
            dma((n, 2 * lines)),
            dma((n, 2 * lines)),
            dma((3,)),
            dma((3,)),
        ],
        compiler_params=pltpu.CompilerParams(
            collective_id=0, has_side_effects=True, vmem_limit_bytes=24 << 20
        ),
        name="collect",
    )(block, tok, gain[None], shift[None], dy, qb)


def norm_stats(values):
    center = values - jnp.mean(values, -1, keepdims=True)
    spread = jnp.mean(center * center, -1, keepdims=True)
    inverse = lax.rsqrt(spread + NORM_EPS)
    return center * inverse, inverse


def norm_back(grad_out, normal, inverse, gain):
    scaled = grad_out * gain
    return inverse * (
        scaled
        - jnp.mean(scaled, -1, keepdims=True)
        - normal * jnp.mean(scaled * normal, -1, keepdims=True)
    )


class Links:
    def __init__(self, shards):
        self.shards = shards
        self.lines = shards // 2
        self.s = lax.axis_index("shard")
        self.c = lax.axis_index("ctx")
        self.y = lax.axis_index("tp")
        self.line = self.s // 2
        self.side = self.s % 2
        self.diag = self.c == self.y

    def send(self, value, target, where=lambda c, y: True):
        flat = lambda s, c, y: (s * 2 + c) * 2 + y
        pairs = []
        for s in range(self.shards):
            for c in range(2):
                for y in range(2):
                    if where(c, y):
                        pairs.append((flat(s, c, y), flat(*target(s, c, y))))
        return lax.ppermute(value, AXES, pairs)

    def core(self, value):
        return self.send(value, lambda s, c, y: (s, 1 - c, y))

    def across(self, value, where=lambda c, y: True):
        return self.send(value, lambda s, c, y: (s, c, 1 - y), where)

    def beside(self, value, where=lambda c, y: True):
        return self.send(value, lambda s, c, y: (s ^ 1, c, y), where)

    def along(self, value, step, where=lambda c, y: True):
        lines = self.lines
        return self.send(value, lambda s, c, y: (((s // 2 + step) % lines) * 2 + s % 2, c, y), where)

    def gather(self, block, where=lambda c, y: True):
        near = [block] + [self.along(block, k, where) for k in range(1, self.lines)]
        far = [self.beside(piece, where) for piece in near]
        return near, far

    def place(self, near, far):
        full = jnp.zeros((self.shards,) + near[0].shape, near[0].dtype)
        for k in range(self.lines):
            row = ((self.line - k) % self.lines) * 2
            full = lax.dynamic_update_index_in_dim(full, near[k], row + self.side, 0)
            full = lax.dynamic_update_index_in_dim(full, far[k], row + 1 - self.side, 0)
        return full

    def scatter(self, blocks, where=lambda c, y: True):
        pick = lambda t, i, d: lax.dynamic_index_in_dim(t, i, d, False)
        other = pick(blocks, 1 - self.side, 1)
        mine = pick(blocks, self.side, 1).astype(F32) + self.beside(other, where).astype(F32)
        low = mine.astype(BF16)
        total = pick(mine, self.line, 0)
        for k in range(1, self.lines):
            piece = pick(low, (self.line + k) % self.lines, 0)
            total = total + self.along(piece, k, where).astype(F32)
        return total


def on_diag(c, y):
    return c == y


def off_diag(c, y):
    return c != y


def per_device(
    tokens,
    patch_meta,
    attn_norm_gain,
    attn_norm_bias,
    qkv_weight,
    qkv_bias,
    proj_weight,
    proj_bias,
    mlp_norm_gain,
    mlp_norm_bias,
    fc1_weight,
    fc1_bias,
    fc2_weight,
    fc2_bias,
    cotangent,
    *,
    shards,
):
    net = Links(shards)
    c, y = net.c, net.y
    local = tokens.shape[2]
    width = tokens.shape[3]
    full = patch_meta.shape[3]
    inner = qkv_weight.shape[2]
    rows = width // shards
    quarter = fc1_weight.shape[1] // 2
    pick = lambda t, i, d=0: lax.dynamic_index_in_dim(t, i, d, False)
    mine_or = lambda own, other: jnp.where(net.diag, own, other)

    def both(own, other, index):
        return jnp.where(index == 0, jnp.stack([own, other]), jnp.stack([other, own]))

    attn_block = jnp.concatenate([qkv_weight, proj_weight.T[None]], axis=0)
    grad_out = cotangent.reshape(2, local, width)
    tok = pick(tokens, y).reshape(local, width)
    attn_full, normed, grad_out_sib, bias_qkv = collect(
        net.lines, attn_block, tok, attn_norm_gain, attn_norm_bias, grad_out, qkv_bias
    )
    normed = normed.reshape(full, width)
    qkv_full = attn_full[:3].reshape(3, width, inner)
    proj_full = attn_full[3].reshape(width, inner)

    fc_block = jnp.stack(
        [
            lax.dynamic_slice_in_dim(fc1_weight, c * quarter, quarter, 1),
            lax.dynamic_slice_in_dim(fc2_weight, c * quarter, quarter, 0).T,
        ]
    )
    fc_block, _ = lax.optimization_barrier((fc_block, bias_qkv))
    fc_full = net.place(*net.gather(fc_block))
    fc1_full, fc2_full = [fc_full[:, i].reshape(width, quarter) for i in range(2)]
    bias_fc1 = lax.dynamic_slice_in_dim(fc1_bias, c * quarter, quarter, 0)

    inputs = tok.astype(F32)
    normal_one, inverse_one = norm_stats(inputs)
    meta = pick(patch_meta, y, 1).reshape(3, full)
    ids = meta[0]
    cosine, sine = rope_tables(meta[1], meta[2])
    qkv = (
        jnp.einsum("cde,rd->cer", qkv_full, normed, preferred_element_type=F32)
        + bias_qkv[:, :, None]
    )
    low, mixed, mixed_f, lse = attend(qkv, cosine, sine, ids)
    attn_part = dg(mixed, proj_full, ((0,), (1,))).reshape(2, local, width)
    attn_own = pick(attn_part, c) + net.core(pick(attn_part, 1 - c))
    hidden = inputs + attn_own + proj_bias

    normal_two, inverse_two = norm_stats(hidden)
    two_own = (normal_two * mlp_norm_gain + mlp_norm_bias).astype(BF16)
    two_peer = net.across(two_own)
    two = [
        jnp.concatenate([two_own, net.core(two_own)]),
        jnp.concatenate([two_peer, net.core(two_peer)]),
    ]
    dy_own = pick(grad_out, y)
    dy = [jnp.concatenate([pick(grad_out, m), pick(grad_out_sib, m)]) for m in (y, 1 - y)]

    acts, d_pres, d_twos = [], [], []
    for part, dy_part in zip(two, dy):
        pre = dg(part, fc1_full, ((1,), (0,))) + bias_fc1
        sig = jax.nn.sigmoid(GELU * pre)
        acts.append((pre * sig).astype(BF16))
        d_act = dg(dy_part, fc2_full, ((1,), (0,)))
        d_pre = (d_act * (sig + GELU * pre * sig * (1.0 - sig))).astype(BF16)
        d_pres.append(d_pre)
        d_twos.append(dg(d_pre, fc1_full, ((1,), (1,))))

    def reduce_slots(parts):
        own, other = parts
        other = other[:local] + net.core(other[local:].astype(BF16)).astype(F32)
        from_peer = net.across(other.astype(BF16)).astype(F32)
        own = own[:local] + net.core(own[local:].astype(BF16)).astype(F32)
        return own + from_peer

    d_two = reduce_slots(d_twos)
    mlp_out = reduce_slots([dg(a, fc2_full, ((1,), (1,))) for a in acts])
    out_own = (hidden + mlp_out + fc2_bias).astype(BF16)
    block_output = both(out_own, net.across(out_own), y)

    def weight_sum(lefts, rights):
        total = sum(dg(l, r, ((0,), (0,))) for l, r in zip(lefts, rights))
        return total.astype(BF16).reshape(net.lines, 2, rows, quarter)

    def all_hidden(block):
        return both(block, net.core(block), c)

    grad_fc2 = all_hidden(net.scatter(weight_sum(dy, acts)))
    grad_fc1 = all_hidden(net.scatter(weight_sum(two, d_pres)))
    grad_fc1 = jnp.moveaxis(grad_fc1, 0, 1).reshape(rows, 2 * quarter)
    grad_fc2 = jnp.moveaxis(grad_fc2, 1, 2).reshape(2 * quarter, rows)

    d_hidden = dy_own.astype(F32) + norm_back(d_two, normal_two, inverse_two, mlp_norm_gain)
    d_attn_own = d_hidden.astype(BF16)
    d_attn = both(d_attn_own, net.core(d_attn_own), c).reshape(full, width)
    grad_proj_part = dg(d_attn, mixed, ((0,), (1,)), BF16)
    d_mixed = dg(proj_full, d_attn, ((0,), (1,)), BF16)
    d_proj = attend_back(low, d_mixed, mixed_f, lse, cosine, sine, ids)
    grad_qkv_part = jnp.einsum("cer,rd->cde", d_proj, normed, preferred_element_type=F32).astype(BF16)
    d_one_part = jnp.einsum("cer,cde->rd", d_proj, qkv_full, preferred_element_type=F32)
    d_one_part = d_one_part.reshape(2, local, width)
    d_one = pick(d_one_part, c) + net.core(pick(d_one_part, 1 - c))
    grad_in = d_hidden + norm_back(d_one, normal_one, inverse_one, attn_norm_gain)
    grad_in = grad_in.astype(BF16)
    input_grad = both(grad_in, net.across(grad_in), y).astype(F32)

    proj_plane = net.scatter(grad_proj_part.reshape(net.lines, 2, rows, inner))
    proj_sum = proj_plane + net.across(proj_plane.astype(BF16), off_diag).astype(F32)
    qkv_pair = grad_qkv_part.astype(F32) + net.across(grad_qkv_part, off_diag).astype(F32)
    qkv_pair = jnp.moveaxis(qkv_pair.astype(BF16).reshape(3, net.lines, 2, rows, inner), 0, 2)
    qkv_sum = net.scatter(qkv_pair, on_diag)
    attn_sum = jnp.concatenate([qkv_sum, proj_sum[None]])
    attn_sum = mine_or(attn_sum, net.send(attn_sum, lambda s, c, y: (s, 1 - c, y), on_diag))
    grad_qkv, grad_proj = attn_sum[:3], attn_sum[3].T

    sums = lambda t: jnp.sum(t.astype(F32), axis=0)
    qkv_shift = jnp.sum(d_proj.astype(F32), axis=2)
    fc1_shift = sum(sums(d) for d in d_pres)
    zero_qkv, zero_fc1 = jnp.zeros_like(qkv_shift), jnp.zeros_like(fc1_shift)
    small = jnp.concatenate(
        [
            sums(d_one * normal_one),
            sums(d_one),
            sums(d_attn_own),
            sums(d_two * normal_two),
            sums(d_two),
            sums(dy_own),
            jnp.where(c == 0, qkv_shift, zero_qkv).reshape(-1),
            jnp.where(c == 1, qkv_shift, zero_qkv).reshape(-1),
        ]
        + [jnp.where((y == i) & (c == j), fc1_shift, zero_fc1) for i in range(2) for j in range(2)]
    )
    small = lax.psum(small, AXES)
    vec = lambda i: small[i * width : (i + 1) * width]
    at = 6 * width
    qkv_shifts = small[at : at + 6 * inner].reshape(2, 3, inner)
    fc1_shifts = small[at + 6 * inner :].reshape(2, 2 * quarter)
    out_shape = tokens.shape
    return (
        block_output.reshape(out_shape),
        input_grad.reshape(out_shape),
        vec(0),
        vec(1),
        grad_qkv,
        pick(qkv_shifts, y),
        grad_proj,
        vec(2),
        vec(3),
        vec(4),
        grad_fc1,
        pick(fc1_shifts, y),
        grad_fc2,
        vec(5),
    )


def solution(mesh):
    slots = P(None, "shard", "ctx", None)
    placed = (
        slots,
        P(None, None, "shard", None),
        P(),
        P(),
        P(None, "shard", "tp"),
        P(None, "tp"),
        P("tp", "shard"),
        P(),
        P(),
        P(),
        P("shard", "tp"),
        P("tp"),
        P("tp", "shard"),
        P(),
        slots,
    )
    return jax.shard_map(
        functools.partial(per_device, shards=mesh.shape["shard"]),
        mesh=mesh,
        in_specs=placed,
        out_specs=(
            slots,
            slots,
            P(),
            P(),
            P(None, "shard", "tp"),
            P(None, "tp"),
            P("tp", "shard"),
            P(),
            P(),
            P(),
            P("shard", "tp"),
            P("tp"),
            P("tp", "shard"),
            P(),
        ),
        check_vma=False,
    )
```

```python
import functools
import math

import jax
import jax.numpy as jnp
from jax import lax
from jax.experimental import pallas as pl
from jax.experimental.pallas import tpu as pltpu
from jax.sharding import PartitionSpec as P

HDIM = 80
NORM_EPS = 1e-06
GELU = 1.702
ROPE_BASE = 10000.0
SCALE = 1.0 / math.sqrt(HDIM)
LOG2E = 1.0 / math.log(2.0)
NEG = -1e30
F32 = jnp.float32
BF16 = jnp.bfloat16
AXES = ("shard", "ctx", "tp")
QB = 256
AHEAD = 1
FIRST = 8


def dg(left, right, dims, out=F32):
    return lax.dot_general(left, right, (dims, ((), ())), preferred_element_type=F32).astype(out)


def rope_rows(t, cosine, sine):
    half = t.shape[0] // 2
    first, second = t[:half], t[half:]
    return jnp.concatenate([first * cosine - second * sine, second * cosine + first * sine], axis=0)


def rope_rows_back(t, cosine, sine):
    half = t.shape[0] // 2
    first, second = t[:half], t[half:]
    return jnp.concatenate([first * cosine + second * sine, second * cosine - first * sine], axis=0)


def fill_bias(bias, idc_ref, idr_ref):
    @pl.when(pl.program_id(0) == 0)
    def _():
        bias[...] = jnp.where(idc_ref[...] == idr_ref[...], 0.0, NEG)


def attend_kernel(x_ref, cos_ref, sin_ref, idc_ref, idr_ref, low_ref, out_ref, outf_ref, lse_ref, bias):
    fill_bias(bias, idc_ref, idr_ref)
    cosine, sine = cos_ref[...], sin_ref[...]
    query = rope_rows(x_ref[0], cosine, sine).astype(BF16)
    key_f = rope_rows(x_ref[1], cosine, sine)
    value = x_ref[2].astype(BF16)
    low_ref[0] = query
    low_ref[1] = key_f.astype(BF16)
    low_ref[2] = value
    key_nat = key_f.T.astype(BF16)
    length = query.shape[1]
    factor = SCALE * LOG2E
    for start in range(0, length, QB):
        cols = slice(start, start + QB)
        logits = dg(key_nat, query[:, cols], ((1,), (0,))) + bias[:, cols]
        peak = jnp.max(logits, axis=0, keepdims=True)
        probs = jnp.exp2((logits - peak) * factor)
        total = jnp.sum(probs, axis=0, keepdims=True)
        mixed = dg(value, probs.astype(BF16), ((1,), (0,))) * (1.0 / total)
        out_ref[:, cols] = mixed.astype(BF16)
        outf_ref[:, cols] = mixed
        lse_ref[0, :, cols] = peak * factor + jnp.log2(total)


def attend(qkv, cosine, sine, ids):
    _, width, length = qkv.shape
    heads = width // HDIM
    half = HDIM // 2
    head = lambda h: (0, h, 0)
    whole = lambda h: (0, 0)
    return pl.pallas_call(
        attend_kernel,
        grid=(heads,),
        in_specs=[
            pl.BlockSpec((3, HDIM, length), head),
            pl.BlockSpec((half, length), whole),
            pl.BlockSpec((half, length), whole),
            pl.BlockSpec((length, 1), whole),
            pl.BlockSpec((1, length), whole),
        ],
        out_specs=[
            pl.BlockSpec((3, HDIM, length), head),
            pl.BlockSpec((HDIM, length), lambda h: (h, 0)),
            pl.BlockSpec((HDIM, length), lambda h: (h, 0)),
            pl.BlockSpec((1, 1, length), lambda h: (h, 0, 0)),
        ],
        out_shape=[
            jax.ShapeDtypeStruct((3, width, length), BF16),
            jax.ShapeDtypeStruct((width, length), BF16),
            jax.ShapeDtypeStruct((width, length), F32),
            jax.ShapeDtypeStruct((heads, 1, length), F32),
        ],
        scratch_shapes=[pltpu.VMEM((length, length), F32)],
        compiler_params=pltpu.CompilerParams(vmem_limit_bytes=48 << 20),
        cost_estimate=pl.CostEstimate(
            flops=4 * width * length * length,
            transcendentals=heads * length * length,
            bytes_accessed=26 * width * length,
        ),
        name="attend",
    )(qkv, cosine, sine, ids[:, None], ids[None, :])


def attend_back_kernel(
    low_ref, grad_ref, outf_ref, lse_ref, cos_ref, sin_ref, idc_ref, idr_ref, dproj_ref, bias, dq, dk, dv
):
    fill_bias(bias, idc_ref, idr_ref)
    cosine, sine = cos_ref[...], sin_ref[...]
    query, key = low_ref[0], low_ref[1]
    grad = grad_ref[...]
    grad_f = grad.astype(F32)
    delta = jnp.sum(grad_f * outf_ref[...], axis=0, keepdims=True)
    nat = lambda t: t.astype(F32).T.astype(BF16)
    query_nat, key_nat, value_nat, grad_nat = nat(query), nat(key), nat(low_ref[2]), nat(grad)
    lse = lse_ref[0]
    length = query.shape[1]
    factor = SCALE * LOG2E
    for start in range(0, length, QB):
        cols = slice(start, start + QB)
        logits = dg(key_nat, query[:, cols], ((1,), (0,)))
        probs = jnp.exp2(logits * factor + bias[:, cols] - lse[:, cols])
        d_probs = dg(value_nat, grad[:, cols], ((1,), (0,)))
        d_logits = (probs * (d_probs - delta[:, cols])).astype(BF16)
        part_v = dg(probs.astype(BF16), grad_nat[cols], ((1,), (0,)))
        part_k = dg(d_logits, query_nat[cols], ((1,), (0,)))
        dq[:, cols] = dg(key, d_logits, ((1,), (0,)))
        if start == 0:
            dv[...] = part_v
            dk[...] = part_k
        else:
            dv[...] += part_v
            dk[...] += part_k
    dproj_ref[0] = rope_rows_back(dq[...] * SCALE, cosine, sine).astype(BF16)
    dproj_ref[1] = rope_rows_back(dk[...].T * SCALE, cosine, sine).astype(BF16)
    dproj_ref[2] = dv[...].T.astype(BF16)


def attend_back(low, grad, outf, lse, cosine, sine, ids):
    _, width, length = low.shape
    heads = width // HDIM
    half = HDIM // 2
    head = lambda h: (0, h, 0)
    whole = lambda h: (0, 0)
    return pl.pallas_call(
        attend_back_kernel,
        grid=(heads,),
        in_specs=[
            pl.BlockSpec((3, HDIM, length), head),
            pl.BlockSpec((HDIM, length), lambda h: (h, 0)),
            pl.BlockSpec((HDIM, length), lambda h: (h, 0)),
            pl.BlockSpec((1, 1, length), lambda h: (h, 0, 0)),
            pl.BlockSpec((half, length), whole),
            pl.BlockSpec((half, length), whole),
            pl.BlockSpec((length, 1), whole),
            pl.BlockSpec((1, length), whole),
        ],
        out_specs=pl.BlockSpec((3, HDIM, length), head),
        out_shape=jax.ShapeDtypeStruct((3, width, length), BF16),
        scratch_shapes=[
            pltpu.VMEM((length, length), F32),
            pltpu.VMEM((HDIM, length), F32),
            pltpu.VMEM((length, HDIM), F32),
            pltpu.VMEM((length, HDIM), F32),
        ],
        compiler_params=pltpu.CompilerParams(vmem_limit_bytes=48 << 20),
        cost_estimate=pl.CostEstimate(
            flops=10 * width * length * length,
            transcendentals=heads * length * length,
            bytes_accessed=18 * width * length,
        ),
        name="attend_back",
    )(low, grad, outf, lse, cosine, sine, ids[:, None], ids[None, :])


def rope_tables(patch_row, patch_col):
    quarter = HDIM // 4
    frequency = ROPE_BASE ** (-2.0 * jnp.arange(quarter, dtype=F32) / (HDIM // 2))
    angles = jnp.concatenate(
        [
            frequency[:, None] * patch_row.astype(F32)[None, :],
            frequency[:, None] * patch_col.astype(F32)[None, :],
        ],
        axis=0,
    )
    return jnp.cos(angles), jnp.sin(angles)


MESH = pl.DeviceIdType.MESH


def remote(src, dst, send_sem, recv_sem, device):
    return pltpu.make_async_remote_copy(
        src_ref=src,
        dst_ref=dst,
        send_sem=send_sem,
        recv_sem=recv_sem,
        device_id=device,
        device_id_type=MESH,
    )


class Place:
    def __init__(self, lines):
        self.lines = lines
        self.s = lax.axis_index("shard")
        self.c = lax.axis_index("ctx")
        self.y = lax.axis_index("tp")
        self.line = self.s // 2
        self.side = lax.rem(self.s, 2)
        self.sib = (self.s, 1 - self.c, self.y)
        self.peer = (self.s, self.c, 1 - self.y)
        self.beside = (self.line * 2 + 1 - self.side, self.c, self.y)

    def ahead(self, k):
        return (lax.rem(self.line + k, self.lines) * 2 + self.side, self.c, self.y)

    def source(self, k):
        return lax.rem(self.line + self.lines - k, self.lines) * 2

    def greet(self):
        barrier = pltpu.get_barrier_semaphore()
        others = [self.sib, self.peer, self.beside] + [self.ahead(k) for k in range(1, self.lines)]
        for other in others:
            pl.semaphore_signal(barrier, inc=1, device_id=other, device_id_type=MESH)
        pl.semaphore_wait(barrier, len(others))


def norm_rows(values):
    center = values - jnp.mean(values, -1, keepdims=True)
    spread = jnp.mean(center * center, -1, keepdims=True)
    return center * lax.rsqrt(spread + NORM_EPS)


def collect_kernel(
    lines, pieces, block, tok, gain, shift, dy, qb,
    out, normed, dy_sib, qb_out,
    norm_buf, own_sem, zs, zr, xs, xr, ys, yr, ms, mr,
):
    at = Place(lines)
    diag = at.c == at.y

    def part(p, s):
        j, first, count, _ = pieces[p]
        return out.at[j, s, :, pl.ds(first, count)]

    def own(p):
        j, first, count, _ = pieces[p]
        return block.at[j, :, pl.ds(first, count)]

    def z_copy(p, k, src):
        return remote(src, part(p, at.s), zs.at[p, k], zr.at[p, k], at.ahead(k))

    def x_copy(p, k, src):
        return remote(src, part(p, at.source(k) + at.side), xs.at[p, k], xr.at[p, k], at.beside)

    def y_copy(p, i, src, s):
        return remote(src, part(p, s), ys.at[p, i], yr.at[p, i], at.peer)

    def near(k):
        return at.source(k) + at.side

    def far(k):
        return at.source(k) + 1 - at.side

    def z_wait(p, k):
        z_copy(p, k, part(p, near(k))).wait_recv()

    def x_wait(p, k):
        x_copy(p, k, part(p, far(k))).wait_recv()

    def y_wait(p, i, s):
        y_copy(p, i, part(p, s), s).wait_recv()

    late = [p for p in range(len(pieces)) if pieces[p][3]]
    early = [p for p in range(len(pieces)) if not pieces[p][3]]
    order = late + early
    at.greet()

    own_copy = pltpu.make_async_copy(block, out.at[:, at.s], own_sem.at[0])
    bias_copy = pltpu.make_async_copy(qb, qb_out, own_sem.at[1])

    @pl.when(diag)
    def _():
        own_copy.start()
        bias_copy.start()
        remote(qb, qb_out, ms.at[0], mr.at[0], at.peer).start()
        for p in early:
            y_copy(p, 0, own(p), at.s).start()
        for p in order[:AHEAD]:
            for k in range(1, lines):
                z_copy(p, k, own(p)).start()

    dy_copy = remote(dy, dy_sib, ms.at[1], mr.at[1], at.sib)
    dy_copy.start()
    norm_buf[...] = (norm_rows(tok[...].astype(F32)) * gain[...] + shift[...]).astype(BF16)
    norm_copy = remote(norm_buf, normed.at[at.c], ms.at[2], mr.at[2], at.sib)
    norm_copy.start()
    norm_keep = pltpu.make_async_copy(norm_buf, normed.at[at.c], own_sem.at[2])
    norm_keep.start()

    @pl.when(diag)
    def _():
        for step in range(len(order) + 1):
            if step < len(order):
                p = order[step]
                if step + AHEAD < len(order):
                    for k in range(1, lines):
                        z_copy(order[step + AHEAD], k, own(order[step + AHEAD])).start()
                x_copy(p, 0, own(p)).start()
                if p in late:
                    y_copy(p, 0, own(p), at.s).start()
                for k in range(1, lines):
                    z_wait(p, k)
                    x_copy(p, k, part(p, near(k))).start()
                    if p in late:
                        y_copy(p, k, part(p, near(k)), near(k)).start()
            if step > 0:
                p = order[step - 1]
                for k in range(lines):
                    x_wait(p, k)
                    if p in late:
                        y_copy(p, lines + k, part(p, far(k)), far(k)).start()
        own_copy.wait()
        bias_copy.wait()
        remote(qb, qb_out, ms.at[0], mr.at[0], at.peer).wait_send()
        for p in order:
            for k in range(1, lines):
                z_copy(p, k, own(p)).wait_send()
            for k in range(lines):
                x_copy(p, k, part(p, near(k))).wait_send()
            y_copy(p, 0, own(p), at.s).wait_send()
            if p in late:
                for k in range(1, lines):
                    y_copy(p, k, part(p, near(k)), near(k)).wait_send()
                for k in range(lines):
                    y_copy(p, lines + k, part(p, far(k)), far(k)).wait_send()

    @pl.when(jnp.logical_not(diag))
    def _():
        for p in early:
            y_wait(p, 0, at.s)
            for k in range(1, lines):
                z_copy(p, k, part(p, at.s)).start()
            x_copy(p, 0, part(p, at.s)).start()
        for step in range(len(early) + 1):
            if step < len(early):
                p = early[step]
                for k in range(1, lines):
                    z_wait(p, k)
                    x_copy(p, k, part(p, near(k))).start()
            if step > 0:
                for k in range(lines):
                    x_wait(early[step - 1], k)
        for p in early:
            for k in range(1, lines):
                z_copy(p, k, part(p, at.s)).wait_send()
            for k in range(lines):
                x_copy(p, k, part(p, near(k))).wait_send()
        remote(qb, qb_out, ms.at[0], mr.at[0], at.peer).wait_recv()
        for p in late:
            for k in range(lines):
                y_wait(p, k, near(k))
                y_wait(p, lines + k, far(k))

    dy_copy.wait()
    norm_copy.wait_send()
    remote(norm_buf, normed.at[1 - at.c], ms.at[2], mr.at[2], at.sib).wait_recv()
    norm_keep.wait()


def collect(lines, block, tok, gain, shift, dy, qb):
    groups, rows, inner = block.shape
    local, width = tok.shape
    cut = (inner * 3 // 5) // 128 * 128
    pieces = [(j, f, n, i < 5) for i, (j, f, n) in enumerate((j, f, n) for j in range(4) for f, n in ((0, cut), (cut, inner - cut)))]
    n = len(pieces)
    anywhere = pl.BlockSpec(memory_space=pl.ANY)
    vmem = pl.BlockSpec(memory_space=pltpu.VMEM)
    dma = pltpu.SemaphoreType.DMA
    return pl.pallas_call(
        functools.partial(collect_kernel, lines, pieces),
        in_specs=[anywhere, vmem, vmem, vmem, anywhere, anywhere],
        out_specs=[anywhere] * 4,
        out_shape=[
            jax.ShapeDtypeStruct((groups, 2 * lines, rows, inner), BF16),
            jax.ShapeDtypeStruct((2, local, width), BF16),
            jax.ShapeDtypeStruct(dy.shape, BF16),
            jax.ShapeDtypeStruct(qb.shape, F32),
        ],
        scratch_shapes=[
            pltpu.VMEM((local, width), BF16),
            dma((3,)),
            dma((n, lines)),
            dma((n, lines)),
            dma((n, lines)),
            dma((n, lines)),
            dma((n, 2 * lines)),
            dma((n, 2 * lines)),
            dma((3,)),
            dma((3,)),
        ],
        compiler_params=pltpu.CompilerParams(
            collective_id=0, has_side_effects=True, vmem_limit_bytes=24 << 20
        ),
        name="collect",
    )(block, tok, gain[None], shift[None], dy, qb)


class Scatter:
    def __init__(self, at, src, xbuf, zbuf, zin, xs, xr, zs, zr):
        self.at, self.src, self.xbuf, self.zbuf, self.zin = at, src, xbuf, zbuf, zin
        self.xs, self.xr, self.zs, self.zr = xs, xr, zs, zr

    def x_copy(self):
        return remote(self.src.at[:, 1 - self.at.side], self.xbuf, self.xs, self.xr, self.at.beside)

    def z_copy(self, k):
        row = lax.rem(self.at.line + k, self.at.lines)
        return remote(self.zbuf.at[row], self.zin.at[k], self.zs.at[k], self.zr.at[k], self.at.ahead(k))

    def start(self):
        self.x_copy().start()

    def middle(self):
        self.x_copy().wait_recv()
        for row in range(self.at.lines):
            total = self.src[row, self.at.side].astype(F32) + self.xbuf[row].astype(F32)
            self.zbuf[row] = total.astype(BF16)
        for k in range(1, self.at.lines):
            self.z_copy(k).start()

    def finish(self):
        total = self.src[self.at.line, self.at.side].astype(F32) + self.xbuf[self.at.line].astype(F32)
        for k in range(1, self.at.lines):
            self.z_copy(k).wait_recv()
            total += self.zin[k].astype(F32)
        return total

    def drain(self):
        self.x_copy().wait_send()
        for k in range(1, self.at.lines):
            self.z_copy(k).wait_send()


def flow(units, ahead, begin, done):
    count = len(units)
    for i in range(min(ahead, count)):
        begin(i)
    for step in range(count + 1):
        if step < count:
            if step + ahead < count:
                begin(step + ahead)
            units[step].middle()
        if step > 0:
            done(step - 1, units[step - 1].finish())


def settle_kernel(
    lines, pieces, fc_cols, attn, fc, grad_in, vec,
    attn_out, fc_out, grad_peer, vec_out,
    ax, az, ai, ay, al, fx, fz, fi, vbuf, vin,
    axs, axr, azs, azr, ays, ayr, fxs, fxr, fzs, fzr, cs, cr, fs, fr, vs, vr, ms, mr,
):
    at = Place(lines)
    diag = at.c == at.y
    rows = attn.shape[3]
    first = [p for p in range(len(pieces)) if pieces[p][3]]
    last = [p for p in range(len(pieces)) if not pieces[p][3]]

    def cut(ref, p):
        _, start, count, _ = pieces[p]
        return ref.at[..., pl.ds(start, count)]

    def attn_unit(p, src):
        j = pieces[p][0]
        return Scatter(
            at, src, cut(ax.at[j], p), cut(az.at[j], p), cut(ai.at[j], p),
            axs.at[p], axr.at[p], azs.at[p], azr.at[p],
        )

    def pair_copy(p, half):
        side = (1 - at.side, at.side)[half]
        j = pieces[p][0]
        return remote(
            cut(attn.at[j, :, side], p), cut(ay.at[j, :, side], p), ays.at[p, half], ayr.at[p, half], at.peer
        )

    def last_copy(p):
        j = pieces[p][0]
        here = cut(al.at[j, 0], p)
        return remote(here, cut(al.at[j, 1], p), ays.at[p, 0], ayr.at[p, 0], at.peer)

    def attn_share(p):
        here = cut(attn_out.at[pieces[p][0]], p)
        return remote(here, here, cs.at[p], cr.at[p], at.sib)

    wide = fc_cols[0][2]
    fc_units = [
        Scatter(
            at, fc.at[m, :, :, :, pl.ds(start, wide)], fx.at[i], fz.at[i], fi.at[i],
            fxs.at[i], fxr.at[i], fzs.at[i], fzr.at[i],
        )
        for i, (m, start, _) in enumerate(fc_cols)
    ]

    def fc_share(i):
        m, start, _ = fc_cols[i]
        here = fc_out.at[at.c, m, :, pl.ds(start, wide)]
        return remote(here, here, fs.at[i], fr.at[i], at.sib)

    def fc_arrive(i):
        m, start, _ = fc_cols[i]
        there = fc_out.at[1 - at.c, m, :, pl.ds(start, wide)]
        return remote(there, there, fs.at[i], fr.at[i], at.sib)

    def fc_done(i, total):
        m, start, _ = fc_cols[i]
        fc_out[at.c, m, :, start : start + wide] = total
        fc_share(i).start()

    at.greet()

    @pl.when(jnp.logical_not(diag))
    def _():
        for p in first:
            for half in range(2):
                pair_copy(p, half).start()

    grad_copy = remote(grad_in, grad_peer, ms, mr, at.peer)
    grad_copy.start()

    def small_copy(stage, src, device):
        return remote(src, vin.at[stage], vs.at[stage], vr.at[stage], device)

    steps = [at.sib, at.peer, at.beside]

    def small_start(stage):
        small_copy(stage, vec if stage == 0 else vbuf.at[stage - 1], steps[stage]).start()

    def small_add(stage):
        small_copy(stage, vbuf.at[0], steps[stage]).wait_recv()
        before = vec[...] if stage == 0 else vbuf[stage - 1]
        vbuf[stage] = before + vin[stage]

    def line_copy(k):
        return remote(vbuf.at[2], vin.at[3 + at.line], vs.at[2 + k], vr.at[2 + k], at.ahead(k))

    def line_wait(k):
        remote(
            vbuf.at[2], vin.at[3 + at.source(k) // 2], vs.at[2 + k], vr.at[2 + k], at.ahead(k)
        ).wait_recv()

    small_start(0)
    small_add(0)
    small_start(1)
    flow(fc_units, 1, lambda i: fc_units[i].start(), fc_done)
    small_add(1)
    small_start(2)

    @pl.when(diag)
    def _():
        units = [attn_unit(p, cut(attn.at[pieces[p][0]], p)) for p in last]
        units += [attn_unit(p, cut(ay.at[pieces[p][0]], p)) for p in first]
        order = last + first

        def begin(i):
            p = order[i]
            if p in first:
                j, start, count, _ = pieces[p]
                for half in range(2):
                    pair_copy(p, half).wait_recv()
                for row in range(lines):
                    for side in range(2):
                        both = cut(attn.at[j, row, side], p)[...].astype(F32)
                        both = both + cut(ay.at[j, row, side], p)[...].astype(F32)
                        ay[j, row, side, :, start : start + count] = both.astype(BF16)
            units[i].start()

        def done(i, total):
            p = order[i]
            j, start, count, _ = pieces[p]
            if p in last:
                last_copy(p).wait_recv()
                total = total + cut(al.at[j, 1], p)[...].astype(F32)
            attn_out[j, :, start : start + count] = total
            attn_share(p).start()

        flow(units, 1, begin, done)
        for unit in units:
            unit.drain()
        for p in order:
            attn_share(p).wait_send()

    @pl.when(jnp.logical_not(diag))
    def _():
        units = [attn_unit(p, cut(attn.at[pieces[p][0]], p)) for p in last]

        def done(i, total):
            j, start, count, _ = pieces[last[i]]
            al[j, 0, :, start : start + count] = total.astype(BF16)
            last_copy(last[i]).start()

        flow(units, 1, lambda i: units[i].start(), done)
        for unit in units:
            unit.drain()
        for p in last:
            last_copy(p).wait_send()
        for p in first:
            for half in range(2):
                pair_copy(p, half).wait_send()
        for p in first + last:
            attn_share(p).wait_recv()

    small_add(2)
    for k in range(1, lines):
        line_copy(k).start()
    vin[3 + at.line] = vbuf[2]
    for k in range(1, lines):
        line_wait(k)
    total = vin[3]
    for row in range(1, lines):
        total = total + vin[3 + row]
    vec_out[...] = total
    small_copy(0, vec, at.sib).wait_send()
    small_copy(1, vbuf.at[0], at.peer).wait_send()
    small_copy(2, vbuf.at[1], at.beside).wait_send()
    for k in range(1, lines):
        line_copy(k).wait_send()
    for i, unit in enumerate(fc_units):
        unit.drain()
        fc_share(i).wait_send()
        fc_arrive(i).wait_recv()
    grad_copy.wait()


def settle(lines, attn, fc, grad_in, vec):
    groups, _, _, rows, inner = attn.shape
    mats, quarter = fc.shape[0], fc.shape[4]
    cut = (inner * 3 // 5) // 128 * 128
    columns = ((0, cut), (cut, inner - cut))
    pieces = [(j, f, n, 2 * j + i < FIRST) for j in range(groups) for i, (f, n) in enumerate(columns)]
    wide = quarter // 2 // 128 * 128
    fc_cols = [(m, f, wide) for m in range(mats) for f in (0, wide)]
    n, fn = len(pieces), len(fc_cols)
    anywhere = pl.BlockSpec(memory_space=pl.ANY)
    vmem = pl.BlockSpec(memory_space=pltpu.VMEM)
    dma = pltpu.SemaphoreType.DMA
    stage = (groups, lines, rows, inner)
    fstage = (fn, lines, rows, wide)
    return pl.pallas_call(
        functools.partial(settle_kernel, lines, pieces, fc_cols),
        in_specs=[vmem, vmem, anywhere, vmem],
        out_specs=[vmem, vmem, anywhere, vmem],
        out_shape=[
            jax.ShapeDtypeStruct((groups, rows, inner), F32),
            jax.ShapeDtypeStruct((2, mats, rows, quarter), F32),
            jax.ShapeDtypeStruct(grad_in.shape, BF16),
            jax.ShapeDtypeStruct(vec.shape, F32),
        ],
        scratch_shapes=[
            pltpu.VMEM(stage, BF16),
            pltpu.VMEM(stage, BF16),
            pltpu.VMEM(stage, BF16),
            pltpu.VMEM(attn.shape, BF16),
            pltpu.VMEM((groups, 2, rows, inner), BF16),
            pltpu.VMEM(fstage, BF16),
            pltpu.VMEM(fstage, BF16),
            pltpu.VMEM(fstage, BF16),
            pltpu.VMEM((3,) + vec.shape, F32),
            pltpu.VMEM((3 + lines,) + vec.shape, F32),
            dma((n,)), dma((n,)), dma((n, lines)), dma((n, lines)), dma((n, 2)), dma((n, 2)),
            dma((fn,)), dma((fn,)), dma((fn, lines)), dma((fn, lines)),
            dma((n,)), dma((n,)), dma((fn,)), dma((fn,)), dma((2 + lines,)), dma((2 + lines,)),
            dma, dma,
        ],
        compiler_params=pltpu.CompilerParams(
            collective_id=1, has_side_effects=True, vmem_limit_bytes=60 << 20
        ),
        name="settle",
    )(attn, fc, grad_in, vec)


TILE = 256


def feed_kernel(
    lines, part, tok, proj_bias, gain, shift, b1, b2, w1_in, w2_in, dy_in, dy_sib,
    d_attn, d_hid, base, mlp_other, g1, g2, vec,
    w1, w2, two, dy, act, dpre, hid, part_in, sbuf, rbuf, mbuf, ybuf, yin, acc, low_tile, grad_tile, out_low,
    loads, ps, pr, ns, nr, ss, sr, ts, tr, ys, yr, os, dos, dor, gs,
):
    at = Place(lines)
    c, y = at.c, at.y
    local = tok.shape[0]
    tiles = local // TILE

    def rows(g, q):
        return pl.ds((g * tiles + q) * TILE, TILE)

    def group(g):
        return pl.ds(g * local, local)

    def near_rows(q):
        return pl.ds(q * TILE, TILE)

    copies = [
        pltpu.make_async_copy(w1_in, w1, loads.at[0]),
        pltpu.make_async_copy(w2_in, w2, loads.at[1]),
        pltpu.make_async_copy(dy_in.at[y], dy.at[group(0)], loads.at[2]),
        pltpu.make_async_copy(dy_sib.at[y], dy.at[group(1)], loads.at[3]),
        pltpu.make_async_copy(dy_in.at[1 - y], dy.at[group(2)], loads.at[4]),
        pltpu.make_async_copy(dy_sib.at[1 - y], dy.at[group(3)], loads.at[5]),
    ]
    for copy in copies:
        copy.start()
    at.greet()
    part_copy = remote(part.at[1 - c], part_in, ps, pr, at.sib)
    part_copy.start()

    def two_sib(q):
        return remote(two.at[rows(0, q)], two.at[rows(1, q)], ns.at[0, q], nr.at[0, q], at.sib)

    def two_peer(q):
        return remote(two.at[rows(0, q)], two.at[rows(2, q)], ns.at[1, q], nr.at[1, q], at.peer)

    def two_pass(q):
        return remote(two.at[rows(2, q)], two.at[rows(3, q)], ns.at[2, q], nr.at[2, q], at.sib)

    part_copy.wait_recv()
    for q in range(tiles):
        r = near_rows(q)
        value = tok[r].astype(F32) + part[c, r].astype(F32) + part_in[r].astype(F32) + proj_bias[...]
        hid[r] = value
        two[rows(0, q)] = (norm_rows(value) * gain[...] + shift[...]).astype(BF16)
        two_peer(q).start()
        two_sib(q).start()

    def first_layer(start, count):
        def body(i, carry):
            r = pl.ds(pl.multiple_of((start + i) * TILE, TILE), TILE)
            pre = dg(two[r], w1[...], ((1,), (0,))) + b1[...]
            sig = jax.nn.sigmoid(GELU * pre)
            act[r] = (pre * sig).astype(BF16)
            dpre[r] = (sig + GELU * pre * sig * (1.0 - sig)).astype(BF16)
            return carry

        lax.fori_loop(0, count, body, 0)

    copies[0].wait()
    first_layer(0, tiles)
    for q in range(tiles):
        two_sib(q).wait_recv()
    first_layer(tiles, tiles)
    for q in range(tiles):
        two_peer(q).wait_recv()
        two_pass(q).start()
        first_layer(2 * tiles + q, 1)
    for q in range(tiles):
        two_pass(q).wait_recv()
    first_layer(3 * tiles, tiles)
    for copy in copies[1:]:
        copy.wait()

    shift_sum = jnp.zeros((1, b1.shape[1]), F32)

    def to_norm(g, q):
        r = rows(g, q)
        low = (dg(dy[r], w2[...], ((1,), (0,))) * dpre[r].astype(F32)).astype(BF16)
        dpre[r] = low
        return dg(low, w1[...], ((1,), (1,))), jnp.sum(low.astype(F32), axis=0, keepdims=True)

    def swap(kind, q):
        r = near_rows(q)
        return remote(sbuf.at[kind, r], rbuf.at[kind, r], ss.at[kind, q], sr.at[kind, q], at.sib)

    def y_copy(q):
        r = near_rows(q)
        return remote(ybuf.at[r], yin.at[r], ys.at[q], yr.at[q], at.peer)

    for kind in range(2):
        for q in range(tiles):
            r = near_rows(q)
            value, total = to_norm(3 - 2 * kind, q)
            sbuf[kind, r] = value.astype(BF16)
            shift_sum += total
            swap(kind, q).start()
            value, total = to_norm(2 - 2 * kind, q)
            shift_sum += total
            swap(kind, q).wait_recv()
            value += rbuf[kind, r].astype(F32)
            if kind == 0:
                ybuf[r] = value.astype(BF16)
                y_copy(q).start()
            else:
                acc[r] = value

    def weight_grad(left, right, out, sem):
        count = out.shape[0] // TILE

        def copy(i):
            slot = lax.rem(i, 2)
            where = pl.ds(pl.multiple_of(i * TILE, TILE), TILE)
            return pltpu.make_async_copy(grad_tile.at[slot], out.at[where], sem.at[slot])

        def body(i, carry):
            cols = pl.ds(pl.multiple_of(i * TILE, TILE), TILE)

            @pl.when(i >= 2)
            def _():
                copy(i - 2).wait()

            grad_tile[lax.rem(i, 2)] = dg(left[:, cols], right[...], ((0,), (0,))).astype(BF16)
            copy(i).start()
            return carry

        lax.fori_loop(0, count, body, 0)
        for i in range(max(0, count - 2), count):
            copy(i).wait()

    weight_grad(dy, act, g2, gs)
    weight_grad(two, dpre, g1, gs)

    def swap_out(kind, q):
        r = near_rows(q)
        return remote(sbuf.at[kind, r], mbuf.at[kind, r], ts.at[kind, q], tr.at[kind, q], at.sib)

    for kind in range(2):
        for q in range(tiles):
            r = near_rows(q)
            swap(kind, q).wait_send()
            sbuf[kind, r] = dg(act[rows(3 - 2 * kind, q)], w2[...], ((1,), (1,)), BF16)
            swap_out(kind, q).start()
            value = dg(act[rows(2 - 2 * kind, q)], w2[...], ((1,), (1,)))
            swap_out(kind, q).wait_recv()
            value += mbuf[kind, r].astype(F32)
            if kind == 0:
                mlp_other[r] = value.astype(BF16)
            else:
                base[r] = hid[r] + value + b2[...]

    def attn_copy(q):
        r = near_rows(q)
        return remote(out_low.at[r], d_attn.at[c, r], dos.at[q], dor.at[q], at.sib)

    def attn_keep(q):
        r = near_rows(q)
        return pltpu.make_async_copy(out_low.at[r], d_attn.at[c, r], os.at[q])

    sums = [jnp.zeros((1, tok.shape[1]), F32) for _ in range(4)]
    for q in range(tiles):
        r = near_rows(q)
        y_copy(q).wait_recv()
        grad = acc[r] + yin[r].astype(F32)
        value = hid[r]
        center = value - jnp.mean(value, -1, keepdims=True)
        inverse = lax.rsqrt(jnp.mean(center * center, -1, keepdims=True) + NORM_EPS)
        normal = center * inverse
        out_grad = dy[rows(0, q)].astype(F32)
        total = out_grad + norm_back(grad, normal, inverse, gain[...])
        low = total.astype(BF16)
        d_hid[r] = total
        out_low[r] = low
        attn_copy(q).start()
        attn_keep(q).start()
        for i, t in enumerate((low.astype(F32), grad * normal, grad, out_grad)):
            sums[i] += jnp.sum(t, axis=0, keepdims=True)
    for i in range(4):
        vec[i : i + 1] = sums[i]
    vec[4:5] = shift_sum
    vec[5:8] = jnp.zeros((3, tok.shape[1]), F32)

    part_copy.wait_send()
    for q in range(tiles):
        two_sib(q).wait_send()
        two_peer(q).wait_send()
        two_pass(q).wait_send()
        y_copy(q).wait_send()
        for kind in range(2):
            swap_out(kind, q).wait_send()
        attn_copy(q).wait_send()
        attn_keep(q).wait()
        there = d_attn.at[1 - c, near_rows(q)]
        remote(there, there, dos.at[q], dor.at[q], at.sib).wait_recv()


def feed(lines, part, tok, proj_bias, gain, shift, b1, b2, w1, w2, dy, dy_sib):
    local, width = tok.shape
    quarter = w1.shape[1]
    tiles = local // TILE
    anywhere = pl.BlockSpec(memory_space=pl.ANY)
    vmem = pl.BlockSpec(memory_space=pltpu.VMEM)
    dma = pltpu.SemaphoreType.DMA
    slots = pltpu.VMEM((local, width), BF16)
    shape = jax.ShapeDtypeStruct
    return pl.pallas_call(
        functools.partial(feed_kernel, lines),
        in_specs=[vmem] * 7 + [anywhere] * 4,
        out_specs=[anywhere, vmem, vmem, vmem, anywhere, anywhere, vmem],
        out_shape=[
            shape((2, local, width), BF16),
            shape((local, width), F32),
            shape((local, width), F32),
            shape((local, width), BF16),
            shape((width, quarter), BF16),
            shape((width, quarter), BF16),
            shape((8, width), F32),
        ],
        scratch_shapes=[
            pltpu.VMEM((width, quarter), BF16),
            pltpu.VMEM((width, quarter), BF16),
            pltpu.VMEM((4 * local, width), BF16),
            pltpu.VMEM((4 * local, width), BF16),
            pltpu.VMEM((4 * local, quarter), BF16),
            pltpu.VMEM((4 * local, quarter), BF16),
            pltpu.VMEM((local, width), F32),
            slots,
            pltpu.VMEM((2, local, width), BF16),
            pltpu.VMEM((2, local, width), BF16),
            pltpu.VMEM((2, local, width), BF16),
            slots,
            slots,
            pltpu.VMEM((local, width), F32),
            pltpu.VMEM((8, 128), BF16),
            pltpu.VMEM((2, TILE, quarter), BF16),
            slots,
            dma((6,)), dma, dma,
            dma((3, tiles)), dma((3, tiles)),
            dma((2, tiles)), dma((2, tiles)), dma((2, tiles)), dma((2, tiles)),
            dma((tiles,)), dma((tiles,)), dma((tiles,)), dma((tiles,)), dma((tiles,)), dma((2,)),
        ],
        compiler_params=pltpu.CompilerParams(
            collective_id=2, has_side_effects=True, vmem_limit_bytes=63 << 20
        ),
        name="feed",
    )(part, tok, proj_bias[None], gain[None], shift[None], b1[None], b2[None], w1, w2, dy, dy_sib)


def norm_stats(values):
    center = values - jnp.mean(values, -1, keepdims=True)
    spread = jnp.mean(center * center, -1, keepdims=True)
    inverse = lax.rsqrt(spread + NORM_EPS)
    return center * inverse, inverse


def norm_back(grad_out, normal, inverse, gain):
    scaled = grad_out * gain
    return inverse * (
        scaled
        - jnp.mean(scaled, -1, keepdims=True)
        - normal * jnp.mean(scaled * normal, -1, keepdims=True)
    )


class Links:
    def __init__(self, shards):
        self.shards = shards
        self.lines = shards // 2
        self.s = lax.axis_index("shard")
        self.c = lax.axis_index("ctx")
        self.y = lax.axis_index("tp")
        self.line = self.s // 2
        self.side = self.s % 2
        self.diag = self.c == self.y

    def send(self, value, target, where=lambda c, y: True):
        flat = lambda s, c, y: (s * 2 + c) * 2 + y
        pairs = []
        for s in range(self.shards):
            for c in range(2):
                for y in range(2):
                    if where(c, y):
                        pairs.append((flat(s, c, y), flat(*target(s, c, y))))
        return lax.ppermute(value, AXES, pairs)

    def core(self, value):
        return self.send(value, lambda s, c, y: (s, 1 - c, y))

    def across(self, value, where=lambda c, y: True):
        return self.send(value, lambda s, c, y: (s, c, 1 - y), where)

    def beside(self, value, where=lambda c, y: True):
        return self.send(value, lambda s, c, y: (s ^ 1, c, y), where)

    def along(self, value, step, where=lambda c, y: True):
        lines = self.lines
        return self.send(value, lambda s, c, y: (((s // 2 + step) % lines) * 2 + s % 2, c, y), where)

    def gather(self, block, where=lambda c, y: True):
        near = [block] + [self.along(block, k, where) for k in range(1, self.lines)]
        far = [self.beside(piece, where) for piece in near]
        return near, far

    def place(self, near, far):
        full = jnp.zeros((self.shards,) + near[0].shape, near[0].dtype)
        for k in range(self.lines):
            row = ((self.line - k) % self.lines) * 2
            full = lax.dynamic_update_index_in_dim(full, near[k], row + self.side, 0)
            full = lax.dynamic_update_index_in_dim(full, far[k], row + 1 - self.side, 0)
        return full

    def scatter(self, blocks, where=lambda c, y: True):
        pick = lambda t, i, d: lax.dynamic_index_in_dim(t, i, d, False)
        other = pick(blocks, 1 - self.side, 1)
        mine = pick(blocks, self.side, 1).astype(F32) + self.beside(other, where).astype(F32)
        low = mine.astype(BF16)
        total = pick(mine, self.line, 0)
        for k in range(1, self.lines):
            piece = pick(low, (self.line + k) % self.lines, 0)
            total = total + self.along(piece, k, where).astype(F32)
        return total


def on_diag(c, y):
    return c == y


def off_diag(c, y):
    return c != y


def per_device(
    tokens,
    patch_meta,
    attn_norm_gain,
    attn_norm_bias,
    qkv_weight,
    qkv_bias,
    proj_weight,
    proj_bias,
    mlp_norm_gain,
    mlp_norm_bias,
    fc1_weight,
    fc1_bias,
    fc2_weight,
    fc2_bias,
    cotangent,
    *,
    shards,
):
    net = Links(shards)
    c, y = net.c, net.y
    local = tokens.shape[2]
    width = tokens.shape[3]
    full = patch_meta.shape[3]
    inner = qkv_weight.shape[2]
    rows = width // shards
    quarter = fc1_weight.shape[1] // 2
    pick = lambda t, i, d=0: lax.dynamic_index_in_dim(t, i, d, False)
    mine_or = lambda own, other: jnp.where(net.diag, own, other)

    def both(own, other, index):
        return jnp.where(index == 0, jnp.stack([own, other]), jnp.stack([other, own]))

    attn_block = jnp.concatenate([qkv_weight, proj_weight.T[None]], axis=0)
    grad_out = cotangent.reshape(2, local, width)
    tok = pick(tokens, y).reshape(local, width)
    attn_full, normed, grad_out_sib, bias_qkv = collect(
        net.lines, attn_block, tok, attn_norm_gain, attn_norm_bias, grad_out, qkv_bias
    )
    normed = normed.reshape(full, width)
    qkv_full = attn_full[:3].reshape(3, width, inner)
    proj_full = attn_full[3].reshape(width, inner)

    fc_block = jnp.stack(
        [
            lax.dynamic_slice_in_dim(fc1_weight, c * quarter, quarter, 1),
            lax.dynamic_slice_in_dim(fc2_weight, c * quarter, quarter, 0).T,
        ]
    )
    fc_block, _ = lax.optimization_barrier((fc_block, bias_qkv))
    fc_full = net.place(*net.gather(fc_block))
    fc1_full, fc2_full = [fc_full[:, i].reshape(width, quarter) for i in range(2)]
    bias_fc1 = lax.dynamic_slice_in_dim(fc1_bias, c * quarter, quarter, 0)

    inputs = tok.astype(F32)
    normal_one, inverse_one = norm_stats(inputs)
    meta = pick(patch_meta, y, 1).reshape(3, full)
    ids = meta[0]
    cosine, sine = rope_tables(meta[1], meta[2])
    qkv = (
        jnp.einsum("cde,rd->cer", qkv_full, normed, preferred_element_type=F32)
        + bias_qkv[:, :, None]
    )
    low, mixed, mixed_f, lse = attend(qkv, cosine, sine, ids)
    attn_part = dg(mixed, proj_full, ((0,), (1,)), BF16).reshape(2, local, width)
    d_attn, d_hidden, base, mlp_other, grad_fc1_part, grad_fc2_part, sums_two = feed(
        net.lines, attn_part, tok, proj_bias, mlp_norm_gain, mlp_norm_bias, bias_fc1, fc2_bias,
        fc1_full, fc2_full, grad_out, grad_out_sib,
    )
    out_own = (base + net.across(mlp_other).astype(F32)).astype(BF16)
    block_output = both(out_own, net.across(out_own), y)
    d_attn = d_attn.reshape(full, width)
    grad_proj_part = dg(d_attn, mixed, ((0,), (1,)), BF16)
    d_mixed = dg(proj_full, d_attn, ((0,), (1,)), BF16)
    d_proj = attend_back(low, d_mixed, mixed_f, lse, cosine, sine, ids)
    grad_qkv_part = jnp.einsum("cer,rd->cde", d_proj, normed, preferred_element_type=F32).astype(BF16)
    d_one_part = jnp.einsum("cer,cde->rd", d_proj, qkv_full, preferred_element_type=F32)
    d_one_part = d_one_part.reshape(2, local, width)
    d_one = pick(d_one_part, c) + net.core(pick(d_one_part, 1 - c))
    grad_in = d_hidden + norm_back(d_one, normal_one, inverse_one, attn_norm_gain)
    grad_in = grad_in.astype(BF16)

    sums = lambda t: jnp.sum(t.astype(F32), axis=0)
    qkv_shift = jnp.sum(d_proj.astype(F32), axis=2)
    fc1_shift = sums_two[4]
    zero_qkv, zero_fc1 = jnp.zeros_like(qkv_shift), jnp.zeros_like(fc1_shift)
    small = jnp.concatenate(
        [
            sums(d_one * normal_one),
            sums(d_one),
            sums_two[0],
            sums_two[1],
            sums_two[2],
            sums_two[3],
            jnp.where(c == 0, qkv_shift, zero_qkv).reshape(-1),
            jnp.where(c == 1, qkv_shift, zero_qkv).reshape(-1),
        ]
        + [jnp.where((y == i) & (c == j), fc1_shift, zero_fc1) for i in range(2) for j in range(2)]
    )
    blocks = (net.lines, 2, rows, inner)
    attn_parts = jnp.concatenate(
        [grad_qkv_part.reshape((3,) + blocks), grad_proj_part.reshape((1,) + blocks)]
    )
    fc_parts = jnp.stack([grad_fc1_part, grad_fc2_part]).reshape(2, net.lines, 2, rows, quarter)
    attn_sum, fc_sum, grad_in_peer, small = settle(
        net.lines, attn_parts, fc_parts, grad_in, small.reshape(-1, width)
    )
    small = small.reshape(-1)
    input_grad = both(grad_in, grad_in_peer, y).astype(F32)
    grad_qkv, grad_proj = attn_sum[:3], attn_sum[3].T
    grad_fc1 = jnp.moveaxis(fc_sum[:, 0], 0, 1).reshape(rows, 2 * quarter)
    grad_fc2 = jnp.moveaxis(fc_sum[:, 1], 1, 2).reshape(2 * quarter, rows)

    vec = lambda i: small[i * width : (i + 1) * width]
    at = 6 * width
    qkv_shifts = small[at : at + 6 * inner].reshape(2, 3, inner)
    fc1_shifts = small[at + 6 * inner :].reshape(2, 2 * quarter)
    out_shape = tokens.shape
    return (
        block_output.reshape(out_shape),
        input_grad.reshape(out_shape),
        vec(0),
        vec(1),
        grad_qkv,
        pick(qkv_shifts, y),
        grad_proj,
        vec(2),
        vec(3),
        vec(4),
        grad_fc1,
        pick(fc1_shifts, y),
        grad_fc2,
        vec(5),
    )


def solution(mesh):
    slots = P(None, "shard", "ctx", None)
    placed = (
        slots,
        P(None, None, "shard", None),
        P(),
        P(),
        P(None, "shard", "tp"),
        P(None, "tp"),
        P("tp", "shard"),
        P(),
        P(),
        P(),
        P("shard", "tp"),
        P("tp"),
        P("tp", "shard"),
        P(),
        slots,
    )
    return jax.shard_map(
        functools.partial(per_device, shards=mesh.shape["shard"]),
        mesh=mesh,
        in_specs=placed,
        out_specs=(
            slots,
            slots,
            P(),
            P(),
            P(None, "shard", "tp"),
            P(None, "tp"),
            P("tp", "shard"),
            P(),
            P(),
            P(),
            P("shard", "tp"),
            P("tp"),
            P("tp", "shard"),
            P(),
        ),
        check_vma=False,
    )
```

```python
import functools
import math

import jax
import jax.numpy as jnp
from jax import lax
from jax.experimental import pallas as pl
from jax.experimental.pallas import tpu as pltpu
from jax.sharding import PartitionSpec as P

HDIM = 80
NORM_EPS = 1e-06
GELU = 1.702
ROPE_BASE = 10000.0
SCALE = 1.0 / math.sqrt(HDIM)
LOG2E = 1.0 / math.log(2.0)
NEG = -1e30
F32 = jnp.float32
BF16 = jnp.bfloat16
AXES = ("shard", "ctx", "tp")
QB = 256
AHEAD = 2
FIRST = 3
SLICE = 384
TILE = 256


def dg(left, right, dims, out=F32):
    return lax.dot_general(left, right, (dims, ((), ())), preferred_element_type=F32).astype(out)


def rope_rows(t, cosine, sine):
    half = t.shape[0] // 2
    first, second = t[:half], t[half:]
    return jnp.concatenate([first * cosine - second * sine, second * cosine + first * sine], axis=0)


def rope_rows_back(t, cosine, sine):
    half = t.shape[0] // 2
    first, second = t[:half], t[half:]
    return jnp.concatenate([first * cosine + second * sine, second * cosine - first * sine], axis=0)


def fill_bias(bias, idc_ref, idr_ref):
    @pl.when(pl.program_id(0) == 0)
    def _():
        bias[...] = jnp.where(idc_ref[...] == idr_ref[...], 0.0, NEG)


def at_step(h, action):
    pl.when(pl.program_id(0) == h)(action)


def spread(ticks, heads):
    plan = [[] for _ in range(heads)]
    for i, tick in enumerate(ticks):
        plan[min(i, heads - 1)].append(tick)
    return plan


def run_ticks(plan):
    for h, ticks in enumerate(plan):
        if ticks:
            at_step(h, lambda ticks=ticks: [tick() for tick in ticks] and None)


def attend_kernel(
    lines, heads, weights, normed, shift, cos_ref, sin_ref, idc_ref, idr_ref, w_own,
    low_ref, mixed_ref, outf_ref, lse_ref, part_ref, w_full,
    bias, proj_in, wv, rows_in, loads, own_sem, zs, zr, xs, xr,
):
    at = Place(lines)
    h = pl.program_id(0)
    gather = Gather(at, w_own, w_full, columns_of(w_own.shape[1]), own_sem, zs, zr, xs, xr)
    local = rows_in.shape[0] // 2
    copies = [
        pltpu.make_async_copy(weights, wv, loads.at[0]),
        pltpu.make_async_copy(normed.at[0], rows_in.at[pl.ds(0, local)], loads.at[1]),
        pltpu.make_async_copy(normed.at[1], rows_in.at[pl.ds(local, local)], loads.at[2]),
    ]

    @pl.when(h == 0)
    def _():
        for copy in copies:
            copy.start()
        at.greet()
        gather.start()
        for copy in copies:
            copy.wait()
        columns = shift[...].T
        for j in range(3):
            proj_in[j] = dg(wv[j], rows_in[...], ((0,), (1,))) + columns[:, j : j + 1]

    fill_bias(bias, idc_ref, idr_ref)
    cosine, sine = cos_ref[...], sin_ref[...]
    mine = pl.ds(pl.multiple_of(h * HDIM, HDIM), HDIM)
    query = rope_rows(proj_in[0, mine], cosine, sine).astype(BF16)
    key_f = rope_rows(proj_in[1, mine], cosine, sine)
    value = proj_in[2, mine].astype(BF16)
    low_ref[0] = query
    low_ref[1] = key_f.astype(BF16)
    low_ref[2] = value
    key_nat = key_f.T.astype(BF16)
    length = query.shape[1]
    factor = SCALE * LOG2E
    for start in range(0, length, QB):
        cols = slice(start, start + QB)
        logits = dg(key_nat, query[:, cols], ((1,), (0,))) + bias[:, cols]
        peak = jnp.max(logits, axis=0, keepdims=True)
        probs = jnp.exp2((logits - peak) * factor)
        total = jnp.sum(probs, axis=0, keepdims=True)
        mixed = dg(value, probs.astype(BF16), ((1,), (0,))) * (1.0 / total)
        mixed_ref[mine, cols] = mixed.astype(BF16)
        outf_ref[:, cols] = mixed
        lse_ref[0, :, cols] = peak * factor + jnp.log2(total)

    @pl.when(h == heads - 1)
    def _():
        def body(i, carry):
            r = pl.ds(pl.multiple_of(i * QB, QB), QB)
            part_ref[r] = dg(mixed_ref[:, r], wv[3], ((0,), (1,)), BF16)
            return carry

        lax.fori_loop(0, length // QB, body, 0)

    ticks = [functools.partial(gather.tick, i) for i in range(len(gather.pieces) + 1)]
    run_ticks(spread(ticks + [gather.drain], heads))


def attend(lines, weights, normed, shift, cosine, sine, ids, w_own):
    _, width, inner = weights.shape
    length = ids.shape[0]
    heads = inner // HDIM
    half = HDIM // 2
    head = lambda h: (0, h, 0)
    whole = lambda h: (0, 0)
    rows, quarter = w_own.shape
    anywhere = pl.BlockSpec(memory_space=pl.ANY)
    return pl.pallas_call(
        functools.partial(attend_kernel, lines, heads),
        grid=(heads,),
        in_specs=[
            anywhere,
            anywhere,
            pl.BlockSpec((8, inner), whole),
            pl.BlockSpec((half, length), whole),
            pl.BlockSpec((half, length), whole),
            pl.BlockSpec((length, 1), whole),
            pl.BlockSpec((1, length), whole),
            anywhere,
        ],
        out_specs=[
            pl.BlockSpec((3, HDIM, length), head),
            pl.BlockSpec((inner, length), whole),
            pl.BlockSpec((HDIM, length), lambda h: (h, 0)),
            pl.BlockSpec((1, 1, length), lambda h: (h, 0, 0)),
            pl.BlockSpec((length, width), whole),
            anywhere,
        ],
        out_shape=[
            jax.ShapeDtypeStruct((3, inner, length), BF16),
            jax.ShapeDtypeStruct((inner, length), BF16),
            jax.ShapeDtypeStruct((inner, length), F32),
            jax.ShapeDtypeStruct((heads, 1, length), F32),
            jax.ShapeDtypeStruct((length, width), BF16),
            jax.ShapeDtypeStruct((2 * lines * rows, quarter), BF16),
        ],
        scratch_shapes=[
            pltpu.VMEM((length, length), F32),
            pltpu.VMEM((3, inner, length), F32),
            pltpu.VMEM(weights.shape, BF16),
            pltpu.VMEM((length, width), BF16),
            pltpu.SemaphoreType.DMA((3,)),
        ]
        + gather_scratch(lines, quarter),
        compiler_params=pltpu.CompilerParams(
            collective_id=3, has_side_effects=True, vmem_limit_bytes=60 << 20
        ),
        cost_estimate=pl.CostEstimate(
            flops=4 * inner * length * length + 8 * inner * length * width,
            transcendentals=heads * length * length,
            bytes_accessed=26 * inner * length,
        ),
        name="attend",
    )(weights, normed, shift, cosine, sine, ids[:, None], ids[None, :], w_own)


def attend_back_kernel(
    lines, heads, low_ref, outf_ref, lse_ref, cos_ref, sin_ref, idc_ref, idr_ref,
    weights, normed, mixed, d_attn, w_grad, other, base,
    one_ref, qkv_grad, proj_grad, shift_ref, w_out, out_own, out_peer,
    bias, dq, dk, dv, d_mixed, d_proj, wv, rows_in, mixed_in, base_in, other_in, tile_buf, w_sum,
    loads, ys, yr, ts, *share_refs
):
    at = Place(lines)
    h = pl.program_id(0)
    share = Share(at, w_grad, w_sum, columns_of(w_grad.shape[1]), *share_refs)
    length, width = rows_in.shape
    local = length // 2

    def load_rows(source):
        return [
            pltpu.make_async_copy(source.at[i], rows_in.at[pl.ds(i * local, local)], loads.at[i])
            for i in range(2)
        ]

    mixed_copy = pltpu.make_async_copy(mixed, mixed_in, loads.at[2])
    weight_copy = pltpu.make_async_copy(weights, wv, loads.at[3])
    base_copy = pltpu.make_async_copy(base, base_in, loads.at[4])
    other_copy = remote(other, other_in, ys.at[0], yr.at[0], at.peer)
    out_copy = remote(out_own, out_peer, ys.at[1], yr.at[1], at.peer)

    @pl.when(h == 0)
    def _():
        for copy in load_rows(d_attn) + [mixed_copy, weight_copy, base_copy]:
            copy.start()
        at.greet()
        share.flow.start()
        other_copy.start()
        for copy in load_rows(d_attn) + [mixed_copy, weight_copy]:
            copy.wait()
        d_mixed[...] = dg(wv[3], rows_in[...], ((0,), (1,)), BF16)

        def body(i, carry):
            cols = pl.ds(pl.multiple_of(i * QB, QB), QB)
            proj_grad[cols] = dg(rows_in[:, cols], mixed_in[...], ((0,), (1,)), BF16)
            return carry

        lax.fori_loop(0, width // QB, body, 0)
        for copy in load_rows(normed):
            copy.start()

    fill_bias(bias, idc_ref, idr_ref)
    cosine, sine = cos_ref[...], sin_ref[...]
    mine = pl.ds(pl.multiple_of(h * HDIM, HDIM), HDIM)
    query, key = low_ref[0], low_ref[1]
    grad = d_mixed[mine]
    grad_f = grad.astype(F32)
    delta = jnp.sum(grad_f * outf_ref[...], axis=0, keepdims=True)
    nat = lambda t: t.astype(F32).T.astype(BF16)
    query_nat, key_nat, value_nat, grad_nat = nat(query), nat(key), nat(low_ref[2]), nat(grad)
    lse = lse_ref[0]
    factor = SCALE * LOG2E
    for start in range(0, length, QB):
        cols = slice(start, start + QB)
        logits = dg(key_nat, query[:, cols], ((1,), (0,)))
        probs = jnp.exp2(logits * factor + bias[:, cols] - lse[:, cols])
        d_probs = dg(value_nat, grad[:, cols], ((1,), (0,)))
        d_logits = (probs * (d_probs - delta[:, cols])).astype(BF16)
        part_v = dg(probs.astype(BF16), grad_nat[cols], ((1,), (0,)))
        part_k = dg(d_logits, query_nat[cols], ((1,), (0,)))
        dq[:, cols] = dg(key, d_logits, ((1,), (0,)))
        if start == 0:
            dv[...] = part_v
            dk[...] = part_k
        else:
            dv[...] += part_v
            dk[...] += part_k
    d_proj[0, mine] = rope_rows_back(dq[...] * SCALE, cosine, sine).astype(BF16)
    d_proj[1, mine] = rope_rows_back(dk[...].T * SCALE, cosine, sine).astype(BF16)
    d_proj[2, mine] = dv[...].T.astype(BF16)

    @pl.when(h == heads - 3)
    def _():
        other_copy.wait()
        base_copy.wait()
        out_own[...] = (base_in[...] + other_in[...].astype(F32)).astype(BF16)
        out_copy.start()

    ticks = [functools.partial(share.flow.tick, i) for i in range(len(share.pieces) + 1)]
    plan = spread(ticks, heads)
    run_ticks(plan[:-1])

    @pl.when(h == heads - 1)
    def _():
        for copy in load_rows(normed):
            copy.wait()
        one_rows = jnp.ones((8, length), BF16)

        def one_body(i, carry):
            r = pl.ds(pl.multiple_of(i * QB, QB), QB)
            total = dg(d_proj[0, :, r], wv[0], ((0,), (1,)))
            for j in range(1, 3):
                total += dg(d_proj[j, :, r], wv[j], ((0,), (1,)))
            one_ref[r] = total.astype(BF16)
            return carry

        lax.fori_loop(0, length // QB, one_body, 0)
        count = width // QB

        def copy_out(i):
            where = pl.ds(pl.multiple_of(lax.rem(i, count) * QB, QB), QB)
            slot = lax.rem(i, 2)
            return pltpu.make_async_copy(tile_buf.at[slot], qkv_grad.at[i // count, where], ts.at[slot])

        def grad_body(i, carry):
            cols = pl.ds(pl.multiple_of(lax.rem(i, count) * QB, QB), QB)

            @pl.when(i >= 2)
            def _():
                copy_out(i - 2).wait()

            tile_buf[lax.rem(i, 2)] = dg(rows_in[:, cols], d_proj[i // count], ((0,), (1,)), BF16)
            copy_out(i).start()
            return carry

        lax.fori_loop(0, 3 * count, grad_body, 0)
        for i in range(max(0, 3 * count - 2), 3 * count):
            copy_out(i).wait()
        for j in range(3):
            shift_ref[j] = dg(one_rows, d_proj[j], ((1,), (1,)))
        for tick in plan[-1]:
            tick()
        share.drain()
        w_out[...] = w_sum[...]
        out_copy.wait()


def attend_back(lines, low, outf, lse, cosine, sine, ids, weights, normed, mixed, d_attn, w_grad, other, base):
    _, inner, length = low.shape
    width = weights.shape[1]
    local = length // 2
    heads = inner // HDIM
    half = HDIM // 2
    w_rows, quarter = w_grad.shape
    rows = w_rows // (2 * lines)
    head = lambda h: (0, h, 0)
    whole = lambda h: (0, 0)
    cube = lambda h: (0, 0, 0)
    anywhere = pl.BlockSpec(memory_space=pl.ANY)
    dma = pltpu.SemaphoreType.DMA
    shape = jax.ShapeDtypeStruct
    return pl.pallas_call(
        functools.partial(attend_back_kernel, lines, heads),
        grid=(heads,),
        in_specs=[
            pl.BlockSpec((3, HDIM, length), head),
            pl.BlockSpec((HDIM, length), lambda h: (h, 0)),
            pl.BlockSpec((1, 1, length), lambda h: (h, 0, 0)),
            pl.BlockSpec((half, length), whole),
            pl.BlockSpec((half, length), whole),
            pl.BlockSpec((length, 1), whole),
            pl.BlockSpec((1, length), whole),
        ]
        + [anywhere] * 7,
        out_specs=[
            pl.BlockSpec((length, width), whole),
            anywhere,
            pl.BlockSpec((width, inner), whole),
            pl.BlockSpec((3, 8, inner), cube),
            pl.BlockSpec((2, rows, quarter), cube),
            pl.BlockSpec((local, width), whole),
            anywhere,
        ],
        out_shape=[
            shape((length, width), BF16),
            shape((3, width, inner), BF16),
            shape((width, inner), BF16),
            shape((3, 8, inner), F32),
            shape((2, rows, quarter), F32),
            shape((local, width), BF16),
            shape((local, width), BF16),
        ],
        scratch_shapes=[
            pltpu.VMEM((length, length), F32),
            pltpu.VMEM((HDIM, length), F32),
            pltpu.VMEM((length, HDIM), F32),
            pltpu.VMEM((length, HDIM), F32),
            pltpu.VMEM((inner, length), BF16),
            pltpu.VMEM((3, inner, length), BF16),
            pltpu.VMEM(weights.shape, BF16),
            pltpu.VMEM((length, width), BF16),
            pltpu.VMEM((inner, length), BF16),
            pltpu.VMEM((local, width), F32),
            pltpu.VMEM((local, width), BF16),
            pltpu.VMEM((2, QB, inner), BF16),
            pltpu.VMEM((2, rows, quarter), F32),
            dma((5,)), dma((2,)), dma((2,)), dma((2,)),
        ]
        + share_scratch(lines, rows, quarter),
        compiler_params=pltpu.CompilerParams(
            collective_id=4, has_side_effects=True, vmem_limit_bytes=63 << 20
        ),
        cost_estimate=pl.CostEstimate(
            flops=10 * inner * length * length + 20 * inner * length * width,
            transcendentals=heads * length * length,
            bytes_accessed=18 * inner * length,
        ),
        name="attend_back",
    )(low, outf, lse, cosine, sine, ids[:, None], ids[None, :], weights, normed, mixed, d_attn, w_grad, other, base)


def rope_tables(patch_row, patch_col):
    quarter = HDIM // 4
    frequency = ROPE_BASE ** (-2.0 * jnp.arange(quarter, dtype=F32) / (HDIM // 2))
    angles = jnp.concatenate(
        [
            frequency[:, None] * patch_row.astype(F32)[None, :],
            frequency[:, None] * patch_col.astype(F32)[None, :],
        ],
        axis=0,
    )
    return jnp.cos(angles), jnp.sin(angles)


MESH = pl.DeviceIdType.MESH


def remote(src, dst, send_sem, recv_sem, device):
    return pltpu.make_async_remote_copy(
        src_ref=src,
        dst_ref=dst,
        send_sem=send_sem,
        recv_sem=recv_sem,
        device_id=device,
        device_id_type=MESH,
    )


class Place:
    def __init__(self, lines):
        self.lines = lines
        self.s = lax.axis_index("shard")
        self.c = lax.axis_index("ctx")
        self.y = lax.axis_index("tp")
        self.line = self.s // 2
        self.side = lax.rem(self.s, 2)
        self.sib = (self.s, 1 - self.c, self.y)
        self.peer = (self.s, self.c, 1 - self.y)
        self.beside = (self.line * 2 + 1 - self.side, self.c, self.y)

    def ahead(self, k):
        return (lax.rem(self.line + k, self.lines) * 2 + self.side, self.c, self.y)

    def source(self, k):
        return lax.rem(self.line + self.lines - k, self.lines) * 2

    def greet(self):
        barrier = pltpu.get_barrier_semaphore()
        others = [self.sib, self.peer, self.beside] + [self.ahead(k) for k in range(1, self.lines)]
        for other in others:
            pl.semaphore_signal(barrier, inc=1, device_id=other, device_id_type=MESH)
        pl.semaphore_wait(barrier, len(others))


def norm_rows(values):
    center = values - jnp.mean(values, -1, keepdims=True)
    spread = jnp.mean(center * center, -1, keepdims=True)
    return center * lax.rsqrt(spread + NORM_EPS)


def collect_kernel(
    lines, pieces, block, tok, gain, shift, dy, qb,
    out, normed, dy_sib, qb_out,
    norm_buf, own_sem, zs, zr, xs, xr, ys, yr, ms, mr,
):
    at = Place(lines)
    diag = at.c == at.y

    def part(p, s):
        j, first, count, _ = pieces[p]
        rows = block.shape[1]
        return out.at[j, pl.ds(pl.multiple_of(s * rows, rows), rows), pl.ds(first, count)]

    def own(p):
        j, first, count, _ = pieces[p]
        return block.at[j, :, pl.ds(first, count)]

    def z_copy(p, k, src):
        return remote(src, part(p, at.s), zs.at[p, k], zr.at[p, k], at.ahead(k))

    def x_copy(p, k, src):
        return remote(src, part(p, at.source(k) + at.side), xs.at[p, k], xr.at[p, k], at.beside)

    def y_copy(p, i, src, s):
        return remote(src, part(p, s), ys.at[p, i], yr.at[p, i], at.peer)

    def near(k):
        return at.source(k) + at.side

    def far(k):
        return at.source(k) + 1 - at.side

    def z_wait(p, k):
        z_copy(p, k, part(p, near(k))).wait_recv()

    def x_wait(p, k):
        x_copy(p, k, part(p, far(k))).wait_recv()

    def y_wait(p, i, s):
        y_copy(p, i, part(p, s), s).wait_recv()

    late = [p for p in range(len(pieces)) if pieces[p][3]]
    early = [p for p in range(len(pieces)) if not pieces[p][3]]
    order = late + early
    at.greet()

    own_rows = pl.ds(pl.multiple_of(at.s * block.shape[1], block.shape[1]), block.shape[1])
    own_copy = pltpu.make_async_copy(block, out.at[:, own_rows], own_sem.at[0])
    bias_copy = pltpu.make_async_copy(qb, qb_out, own_sem.at[1])

    @pl.when(diag)
    def _():
        own_copy.start()
        bias_copy.start()
        remote(qb, qb_out, ms.at[0], mr.at[0], at.peer).start()
        for p in early:
            y_copy(p, 0, own(p), at.s).start()
        for p in order[:AHEAD]:
            for k in range(1, lines):
                z_copy(p, k, own(p)).start()

    dy_copy = remote(dy, dy_sib, ms.at[1], mr.at[1], at.sib)
    dy_copy.start()
    norm_buf[...] = (norm_rows(tok[...].astype(F32)) * gain[...] + shift[...]).astype(BF16)
    norm_copy = remote(norm_buf, normed.at[at.c], ms.at[2], mr.at[2], at.sib)
    norm_copy.start()
    norm_keep = pltpu.make_async_copy(norm_buf, normed.at[at.c], own_sem.at[2])
    norm_keep.start()

    @pl.when(diag)
    def _():
        for step in range(len(order) + 1):
            if step < len(order):
                p = order[step]
                if step + AHEAD < len(order):
                    for k in range(1, lines):
                        z_copy(order[step + AHEAD], k, own(order[step + AHEAD])).start()
                x_copy(p, 0, own(p)).start()
                if p in late:
                    y_copy(p, 0, own(p), at.s).start()
                for k in range(1, lines):
                    z_wait(p, k)
                    x_copy(p, k, part(p, near(k))).start()
                    if p in late:
                        y_copy(p, k, part(p, near(k)), near(k)).start()
            if step > 0:
                p = order[step - 1]
                for k in range(lines):
                    x_wait(p, k)
                    if p in late:
                        y_copy(p, lines + k, part(p, far(k)), far(k)).start()
        own_copy.wait()
        bias_copy.wait()
        remote(qb, qb_out, ms.at[0], mr.at[0], at.peer).wait_send()
        for p in order:
            for k in range(1, lines):
                z_copy(p, k, own(p)).wait_send()
            for k in range(lines):
                x_copy(p, k, part(p, near(k))).wait_send()
            y_copy(p, 0, own(p), at.s).wait_send()
            if p in late:
                for k in range(1, lines):
                    y_copy(p, k, part(p, near(k)), near(k)).wait_send()
                for k in range(lines):
                    y_copy(p, lines + k, part(p, far(k)), far(k)).wait_send()

    @pl.when(jnp.logical_not(diag))
    def _():
        for p in early:
            y_wait(p, 0, at.s)
            for k in range(1, lines):
                z_copy(p, k, part(p, at.s)).start()
            x_copy(p, 0, part(p, at.s)).start()
        for step in range(len(early) + 1):
            if step < len(early):
                p = early[step]
                for k in range(1, lines):
                    z_wait(p, k)
                    x_copy(p, k, part(p, near(k))).start()
            if step > 0:
                for k in range(lines):
                    x_wait(early[step - 1], k)
        for p in early:
            for k in range(1, lines):
                z_copy(p, k, part(p, at.s)).wait_send()
            for k in range(lines):
                x_copy(p, k, part(p, near(k))).wait_send()
        remote(qb, qb_out, ms.at[0], mr.at[0], at.peer).wait_recv()
        for p in late:
            for k in range(lines):
                y_wait(p, k, near(k))
                y_wait(p, lines + k, far(k))

    dy_copy.wait()
    norm_copy.wait_send()
    remote(norm_buf, normed.at[1 - at.c], ms.at[2], mr.at[2], at.sib).wait_recv()
    norm_keep.wait()


def collect(lines, block, tok, gain, shift, dy, qb):
    groups, rows, inner = block.shape
    local, width = tok.shape
    cut = (inner * 3 // 5) // 128 * 128
    pieces = [(j, f, n, i < 5) for i, (j, f, n) in enumerate((j, f, n) for j in range(4) for f, n in ((0, cut), (cut, inner - cut)))]
    n = len(pieces)
    anywhere = pl.BlockSpec(memory_space=pl.ANY)
    vmem = pl.BlockSpec(memory_space=pltpu.VMEM)
    dma = pltpu.SemaphoreType.DMA
    return pl.pallas_call(
        functools.partial(collect_kernel, lines, pieces),
        in_specs=[anywhere, vmem, vmem, vmem, anywhere, anywhere],
        out_specs=[anywhere] * 4,
        out_shape=[
            jax.ShapeDtypeStruct((groups, 2 * lines * rows, inner), BF16),
            jax.ShapeDtypeStruct((2, local, width), BF16),
            jax.ShapeDtypeStruct(dy.shape, BF16),
            jax.ShapeDtypeStruct(qb.shape, F32),
        ],
        scratch_shapes=[
            pltpu.VMEM((local, width), BF16),
            dma((3,)),
            dma((n, lines)),
            dma((n, lines)),
            dma((n, lines)),
            dma((n, lines)),
            dma((n, 2 * lines)),
            dma((n, 2 * lines)),
            dma((3,)),
            dma((3,)),
        ],
        compiler_params=pltpu.CompilerParams(
            collective_id=0, has_side_effects=True, vmem_limit_bytes=24 << 20
        ),
        name="collect",
    )(block, tok, gain[None], shift[None], dy, qb)


class Gather:
    def __init__(self, at, own, full, pieces, own_sem, zs, zr, xs, xr):
        self.at, self.own, self.full, self.pieces = at, own, full, pieces
        self.own_sem, self.zs, self.zr, self.xs, self.xr = own_sem, zs, zr, xs, xr
        self.rows = own.shape[0]

    def part(self, p, s):
        start, count = self.pieces[p]
        return self.full.at[pl.ds(pl.multiple_of(s * self.rows, self.rows), self.rows), pl.ds(start, count)]

    def z_copy(self, p, k):
        start, count = self.pieces[p]
        src = self.own.at[:, pl.ds(start, count)]
        return remote(src, self.part(p, self.at.s), self.zs.at[p, k], self.zr.at[p, k], self.at.ahead(k))

    def x_copy(self, p, k):
        start, count = self.pieces[p]
        there = self.part(p, self.at.source(k) + self.at.side)
        src = self.own.at[:, pl.ds(start, count)] if k == 0 else there
        return remote(src, there, self.xs.at[p, k], self.xr.at[p, k], self.at.beside)

    def z_wait(self, p, k):
        there = self.part(p, self.at.source(k) + self.at.side)
        remote(there, there, self.zs.at[p, k], self.zr.at[p, k], self.at.ahead(k)).wait_recv()

    def x_wait(self, p, k):
        there = self.part(p, self.at.source(k) + 1 - self.at.side)
        remote(there, there, self.xs.at[p, k], self.xr.at[p, k], self.at.beside).wait_recv()

    def keep(self):
        there = self.full.at[pl.ds(pl.multiple_of(self.at.s * self.rows, self.rows), self.rows)]
        return pltpu.make_async_copy(self.own, there, self.own_sem)

    def begin(self, p):
        if p < len(self.pieces):
            for k in range(1, self.at.lines):
                self.z_copy(p, k).start()

    def start(self):
        self.keep().start()
        for p in range(AHEAD):
            self.begin(p)

    def tick(self, p):
        if p < len(self.pieces):
            self.begin(p + AHEAD)
            self.x_copy(p, 0).start()
            for k in range(1, self.at.lines):
                self.z_wait(p, k)
                self.x_copy(p, k).start()
        if 0 < p <= len(self.pieces):
            for k in range(self.at.lines):
                self.x_wait(p - 1, k)
        if p == len(self.pieces):
            self.keep().wait()

    def drain(self):
        for p in range(len(self.pieces)):
            for k in range(self.at.lines):
                self.x_copy(p, k).wait_send()
                if k > 0:
                    self.z_copy(p, k).wait_send()


class Scatter:
    def __init__(self, at, block, mine, xbuf, zin, xs, xr, zs, zr, load=None):
        self.at, self.block, self.mine, self.xbuf, self.zin = at, block, mine, xbuf, zin
        self.xs, self.xr, self.zs, self.zr, self.load = xs, xr, zs, zr, load

    def x_copy(self, row):
        src = self.block(row, 1 - self.at.side)
        return remote(src, self.xbuf.at[row], self.xs.at[row], self.xr.at[row], self.at.beside)

    def load_copy(self, row):
        return pltpu.make_async_copy(self.block(row, self.at.side), self.mine.at[row], self.load.at[row])

    def z_copy(self, k):
        row = lax.rem(self.at.line + k, self.at.lines)
        return remote(self.mine.at[row], self.zin.at[k], self.zs.at[k], self.zr.at[k], self.at.ahead(k))

    def start(self):
        for row in range(self.at.lines):
            self.x_copy(row).start()
            if self.load is not None:
                self.load_copy(row).start()

    def middle(self):
        for row in range(self.at.lines):
            self.x_copy(row).wait_recv()
            if self.load is not None:
                self.load_copy(row).wait()
                here = self.mine[row]
            else:
                here = self.block(row, self.at.side)[...]
            self.mine[row] = (here.astype(F32) + self.xbuf[row].astype(F32)).astype(BF16)
        for k in range(1, self.at.lines):
            self.z_copy(k).start()

    def finish(self):
        total = self.mine[self.at.line].astype(F32)
        for k in range(1, self.at.lines):
            self.z_copy(k).wait_recv()
            total += self.zin[k].astype(F32)
        return total

    def drain(self):
        for row in range(self.at.lines):
            self.x_copy(row).wait_send()
        for k in range(1, self.at.lines):
            self.z_copy(k).wait_send()


class Flow:
    def __init__(self, units, begin, done):
        self.units, self.begin, self.done = units, begin, done

    def start(self):
        for i in range(min(AHEAD, len(self.units))):
            self.begin(i)

    def tick(self, i):
        count = len(self.units)
        if i < count:
            self.units[i].middle()
            if i + AHEAD < count:
                self.begin(i + AHEAD)
        if 0 < i <= count:
            self.done(i - 1, self.units[i - 1].finish())

    def run(self):
        self.start()
        for i in range(len(self.units) + 1):
            self.tick(i)


class Share:
    def __init__(self, at, grad, out, pieces, mine, xbuf, zin, xs, xr, zs, zr, load, cs, cr):
        rows = out.shape[1]
        self.at, self.out, self.pieces, self.cs, self.cr = at, out, pieces, cs, cr

        def unit(i):
            start, count = pieces[i]

            def block(line, side):
                first = pl.multiple_of((2 * line + side) * rows, rows)
                return grad.at[pl.ds(first, rows), pl.ds(start, count)]

            cut = lambda ref: ref.at[:, :, pl.ds(start, count)]
            return Scatter(
                at, block, cut(mine), cut(xbuf), cut(zin), xs.at[i], xr.at[i], zs.at[i], zr.at[i], load.at[i]
            )

        units = [unit(i) for i in range(len(pieces))]
        self.flow = Flow(units, lambda i: units[i].start(), self.done)

    def share(self, i, core):
        start, count = self.pieces[i]
        here = self.out.at[core, :, pl.ds(start, count)]
        return remote(here, here, self.cs.at[i], self.cr.at[i], self.at.sib)

    def done(self, i, total):
        start, count = self.pieces[i]
        self.out[self.at.c, :, start : start + count] = total
        self.share(i, self.at.c).start()

    def drain(self):
        for i, unit in enumerate(self.flow.units):
            unit.drain()
            self.share(i, self.at.c).wait_send()
            self.share(i, 1 - self.at.c).wait_recv()


def columns_of(quarter):
    return [(start, 256) for start in range(0, quarter, 256)]


def share_scratch(lines, rows, quarter):
    n = len(columns_of(quarter))
    dma = pltpu.SemaphoreType.DMA
    slab = pltpu.VMEM((lines, rows, quarter), BF16)
    return [slab] * 3 + [dma((n, lines))] * 5 + [dma((n,))] * 2


def gather_scratch(lines, quarter):
    n = len(columns_of(quarter))
    dma = pltpu.SemaphoreType.DMA
    return [dma] + [dma((n, lines))] * 4


def settle_kernel(
    lines, pieces, qkv, proj, d_one, d_hid, tok, gain, vec,
    attn_out, grad_own, grad_peer, vec_out,
    here, mine, ax, ai, ay, al, one_in, vown, vbuf, vin,
    hs, axs, axr, azs, azr, ays, ayr, cs, cr, vs, vr, os, orr, ms, mr,
):
    at = Place(lines)
    diag = at.c == at.y
    first = [p for p in range(len(pieces)) if pieces[p][3]]
    last = [p for p in range(len(pieces)) if not pieces[p][3]]

    def cut(ref, p):
        _, start, count, _ = pieces[p]
        return ref.at[..., pl.ds(start, count)]

    def source(p):
        j = pieces[p][0]
        return cut(proj if j == 3 else qkv.at[j], p)

    def local_part(p):
        return cut(here.at[pieces[p][0]], p)

    class Direct(Scatter):
        def __init__(self, p):
            j = pieces[p][0]
            super().__init__(
                at, lambda line, side: local_part(p).at[line, side],
                cut(mine.at[j], p), cut(ax.at[j], p), cut(ai.at[j], p),
                axs.at[p], axr.at[p], azs.at[p], azr.at[p],
            )
            self.p = p

        def x_copy(self, row):
            src = source(self.p).at[row, 1 - at.side]
            return remote(src, self.xbuf.at[row], self.xs.at[row], self.xr.at[row], at.beside)

    def summed(p):
        j = pieces[p][0]
        return Scatter(
            at, lambda line, side: cut(ay.at[j, line, side], p),
            cut(mine.at[j], p), cut(ax.at[j], p), cut(ai.at[j], p),
            axs.at[p], axr.at[p], azs.at[p], azr.at[p],
        )

    def pair_copy(p, half):
        side = (1 - at.side, at.side)[half]
        there = cut(ay.at[pieces[p][0], :, side], p)
        return remote(source(p).at[:, side], there, ays.at[p, half], ayr.at[p, half], at.peer)

    def last_copy(p):
        j = pieces[p][0]
        return remote(cut(al.at[j, 0], p), cut(al.at[j, 1], p), ays.at[p, 0], ayr.at[p, 0], at.peer)

    def attn_share(p):
        there = cut(attn_out.at[pieces[p][0]], p)
        return remote(there, there, cs.at[p], cr.at[p], at.sib)

    order = last + first
    diag_units = [Direct(p) for p in last] + [summed(p) for p in first]
    off_units = [Direct(p) for p in last]

    def diag_begin(i):
        p = order[i]
        if p in first:
            j, start, count, _ = pieces[p]
            for half in range(2):
                pair_copy(p, half).wait_recv()
            for row in range(lines):
                for side in range(2):
                    both = local_part(p)[row, side].astype(F32) + cut(ay.at[j, row, side], p)[...].astype(F32)
                    ay[j, row, side, :, start : start + count] = both.astype(BF16)
        diag_units[i].start()

    def diag_done(i, total):
        p = order[i]
        j, start, count, _ = pieces[p]
        if p in last:
            last_copy(p).wait_recv()
            total = total + cut(al.at[j, 1], p)[...].astype(F32)
        attn_out[j, :, start : start + count] = total
        attn_share(p).start()

    def off_done(i, total):
        j, start, count, _ = pieces[last[i]]
        al[j, 0, :, start : start + count] = total.astype(BF16)
        last_copy(last[i]).start()

    diag_flow = Flow(diag_units, diag_begin, diag_done)
    off_flow = Flow(off_units, lambda i: off_units[i].start(), off_done)

    def ticks(begin, end):
        @pl.when(diag)
        def _():
            for i in range(begin, end):
                diag_flow.tick(i)

        @pl.when(jnp.logical_not(diag))
        def _():
            for i in range(begin, end):
                off_flow.tick(i)

    loads = [
        pltpu.make_async_copy(qkv, here.at[pl.ds(0, 3)], hs.at[0]),
        pltpu.make_async_copy(proj, here.at[3], hs.at[1]),
    ]
    for load in loads:
        load.start()
    at.greet()
    one_copy = remote(d_one.at[1 - at.c], one_in, os, orr, at.sib)
    one_copy.start()

    @pl.when(diag)
    def _():
        for i in range(min(AHEAD, len(last))):
            diag_units[i].start()

    @pl.when(jnp.logical_not(diag))
    def _():
        for p in first:
            for half in range(2):
                pair_copy(p, half).start()
        off_flow.start()

    one_copy.wait_recv()
    local = tok.shape[0]
    tile = TILE
    grad_copies = []
    sums = [jnp.zeros((1, tok.shape[1]), F32) for _ in range(2)]
    for q in range(local // tile):
        r = pl.ds(q * tile, tile)
        value = tok[r].astype(F32)
        center = value - jnp.mean(value, -1, keepdims=True)
        inverse = lax.rsqrt(jnp.mean(center * center, -1, keepdims=True) + NORM_EPS)
        normal = center * inverse
        grad = d_one[at.c, r].astype(F32) + one_in[r].astype(F32)
        grad_own[r] = (d_hid[r] + norm_back(grad, normal, inverse, gain[...])).astype(BF16)
        copy = remote(grad_own.at[r], grad_peer.at[r], ms.at[q], mr.at[q], at.peer)
        grad_copies.append(copy)
        for i, t in enumerate((grad * normal, grad)):
            sums[i] += jnp.sum(t, axis=0, keepdims=True)
    vown[...] = vec[...]
    for i in range(2):
        vown[i : i + 1] = sums[i]

    def small_copy(stage, device):
        src = vown if stage == 0 else vbuf.at[stage - 1]
        return remote(src, vin.at[stage], vs.at[stage], vr.at[stage], device)

    steps = [at.sib, at.peer, at.beside]

    def small_start(stage):
        small_copy(stage, steps[stage]).start()

    def small_add(stage):
        small_copy(stage, steps[stage]).wait_recv()
        before = vown[...] if stage == 0 else vbuf[stage - 1]
        vbuf[stage] = before + vin[stage]

    def line_copy(k):
        return remote(vbuf.at[2], vin.at[3 + at.line], vs.at[2 + k], vr.at[2 + k], at.ahead(k))

    def line_wait(k):
        there = vin.at[3 + at.source(k) // 2]
        remote(vbuf.at[2], there, vs.at[2 + k], vr.at[2 + k], at.ahead(k)).wait_recv()

    small_start(0)
    for load in loads:
        load.wait()
    total_ticks = len(order) + 1
    marks = [total_ticks * i // 5 for i in range(1, 5)]

    @pl.when(diag)
    def _():
        for i in range(len(last), min(AHEAD, len(order))):
            diag_begin(i)

    ticks(0, marks[0])
    for copy in grad_copies:
        copy.start()
    small_add(0)
    small_start(1)
    ticks(marks[0], marks[1])
    small_add(1)
    small_start(2)
    ticks(marks[1], marks[2])
    small_add(2)
    for k in range(1, lines):
        line_copy(k).start()
    vin[3 + at.line] = vbuf[2]
    ticks(marks[2], total_ticks)
    for k in range(1, lines):
        line_wait(k)
    total = vin[3]
    for row in range(1, lines):
        total = total + vin[3 + row]
    vec_out[...] = total

    @pl.when(diag)
    def _():
        for unit in diag_units:
            unit.drain()
        for p in order:
            attn_share(p).wait_send()

    @pl.when(jnp.logical_not(diag))
    def _():
        for unit in off_units:
            unit.drain()
        for p in last:
            last_copy(p).wait_send()
        for p in first:
            for half in range(2):
                pair_copy(p, half).wait_send()
        for p in order:
            attn_share(p).wait_recv()

    for stage in range(3):
        small_copy(stage, steps[stage]).wait_send()
    for k in range(1, lines):
        line_copy(k).wait_send()
    one_copy.wait_send()
    for copy in grad_copies:
        copy.wait()


def settle(lines, qkv, proj, d_one, d_hid, tok, gain, vec):
    _, _, _, rows, inner = qkv.shape
    local, width = tok.shape
    pieces = settle_pieces(inner)
    n = len(pieces)
    tiles = local // TILE
    anywhere = pl.BlockSpec(memory_space=pl.ANY)
    vmem = pl.BlockSpec(memory_space=pltpu.VMEM)
    dma = pltpu.SemaphoreType.DMA
    stage = (4, lines, rows, inner)
    return pl.pallas_call(
        functools.partial(settle_kernel, lines, pieces),
        in_specs=[anywhere] * 2 + [vmem] * 5,
        out_specs=[vmem, vmem, anywhere, vmem],
        out_shape=[
            jax.ShapeDtypeStruct((4, rows, inner), F32),
            jax.ShapeDtypeStruct((local, width), BF16),
            jax.ShapeDtypeStruct((local, width), BF16),
            jax.ShapeDtypeStruct(vec.shape, F32),
        ],
        scratch_shapes=[
            pltpu.VMEM((4, lines, 2, rows, inner), BF16),
            pltpu.VMEM(stage, BF16),
            pltpu.VMEM(stage, BF16),
            pltpu.VMEM(stage, BF16),
            pltpu.VMEM((4, lines, 2, rows, inner), BF16),
            pltpu.VMEM((4, 2, rows, inner), BF16),
            pltpu.VMEM((local, width), BF16),
            pltpu.VMEM(vec.shape, F32),
            pltpu.VMEM((3,) + vec.shape, F32),
            pltpu.VMEM((3 + lines,) + vec.shape, F32),
            dma((2,)),
            dma((n, lines)), dma((n, lines)), dma((n, lines)), dma((n, lines)), dma((n, 2)), dma((n, 2)),
            dma((n,)), dma((n,)), dma((2 + lines,)), dma((2 + lines,)),
            dma, dma, dma((tiles,)), dma((tiles,)),
        ],
        compiler_params=pltpu.CompilerParams(
            collective_id=1, has_side_effects=True, vmem_limit_bytes=60 << 20
        ),
        name="settle",
    )(qkv, proj, d_one, d_hid, tok, gain[None], vec)


def settle_pieces(inner):
    cuts = [(f, min(SLICE, inner - f)) for f in range(0, inner, SLICE)]
    every = [(j, f, n) for j in (3, 0, 1, 2) for f, n in cuts]
    return [(j, f, n, i >= len(every) - FIRST) for i, (j, f, n) in enumerate(every)]


def feed_kernel(
    lines, part, tok, proj_bias, gain, shift, b1, b2, w1_in, w2_own, dy_in, dy_sib,
    d_attn, d_hid, base, mlp_other, g1, g2, g2_out, vec,
    w1, w2, two, dy, act, dpre, hid, sbuf, rbuf, mbuf, ybuf, yin, acc, grad_tile, wide_tile,
    loads, ps, pr, ns, nr, ss, sr, ts, tr, ys, yr, os, dos, dor, gs, outs, keeps,
    own_sem, zs, zr, xs, xr, *share_refs,
):
    at = Place(lines)
    c, y = at.c, at.y
    local = hid.shape[0]
    tiles = local // TILE
    pieces = columns_of(w1.shape[1])
    gather = Gather(at, w2_own, w2, pieces, own_sem, zs, zr, xs, xr)
    share = Share(at, g2, g2_out, pieces, *share_refs)
    gather_ticks = [functools.partial(gather.tick, i) for i in range(len(pieces) + 1)]
    share_ticks = [functools.partial(share.flow.tick, i) for i in range(len(pieces) + 1)]

    def advance(ticks, count=1):
        for _ in range(count):
            if ticks:
                ticks.pop(0)()

    def rows(g, q):
        return pl.ds((g * tiles + q) * TILE, TILE)

    def group(g):
        return pl.ds(g * local, local)

    def near_rows(q):
        return pl.ds(q * TILE, TILE)

    copies = [
        pltpu.make_async_copy(tok, ybuf, loads.at[0]),
        pltpu.make_async_copy(part.at[c], yin, loads.at[1]),
        pltpu.make_async_copy(w1_in, w1, loads.at[2]),
        pltpu.make_async_copy(dy_in.at[y], dy.at[group(0)], loads.at[3]),
        pltpu.make_async_copy(dy_sib.at[y], dy.at[group(1)], loads.at[4]),
        pltpu.make_async_copy(dy_in.at[1 - y], dy.at[group(2)], loads.at[5]),
        pltpu.make_async_copy(dy_sib.at[1 - y], dy.at[group(3)], loads.at[6]),
    ]
    for copy in copies:
        copy.start()
    at.greet()
    part_copy = remote(part.at[1 - c], rbuf.at[0], ps, pr, at.sib)
    part_copy.start()
    gather.start()

    def two_sib(q):
        return remote(two.at[rows(0, q)], two.at[rows(1, q)], ns.at[0, q], nr.at[0, q], at.sib)

    def two_peer(q):
        return remote(two.at[rows(0, q)], two.at[rows(2, q)], ns.at[1, q], nr.at[1, q], at.peer)

    def two_pass(q):
        return remote(two.at[rows(2, q)], two.at[rows(3, q)], ns.at[2, q], nr.at[2, q], at.sib)

    copies[0].wait()
    copies[1].wait()
    part_copy.wait_recv()
    for q in range(tiles):
        r = near_rows(q)
        value = ybuf[r].astype(F32) + yin[r].astype(F32) + rbuf[0, r].astype(F32) + proj_bias[...]
        hid[r] = value
        two[rows(0, q)] = (norm_rows(value) * gain[...] + shift[...]).astype(BF16)
        two_peer(q).start()
        two_sib(q).start()

    def first_layer(start, count):
        def body(i, carry):
            r = pl.ds(pl.multiple_of((start + i) * TILE, TILE), TILE)
            pre = dg(two[r], w1[...], ((1,), (0,))) + b1[...]
            sig = jax.nn.sigmoid(GELU * pre)
            act[r] = (pre * sig).astype(BF16)
            dpre[r] = (sig + GELU * pre * sig * (1.0 - sig)).astype(BF16)
            return carry

        lax.fori_loop(0, count, body, 0)

    copies[2].wait()
    first_layer(0, tiles)
    advance(gather_ticks)
    for q in range(tiles):
        two_sib(q).wait_recv()
    first_layer(tiles, tiles)
    advance(gather_ticks)
    for q in range(tiles):
        two_peer(q).wait_recv()
        two_pass(q).start()
        first_layer(2 * tiles + q, 1)
        advance(gather_ticks)
    for q in range(tiles):
        two_pass(q).wait_recv()
    first_layer(3 * tiles, tiles)
    for copy in copies[3:]:
        copy.wait()

    def weight_grad(left, right, out):
        count = out.shape[0] // TILE

        def copy(i):
            slot = lax.rem(i, 2)
            where = pl.ds(pl.multiple_of(i * TILE, TILE), TILE)
            return pltpu.make_async_copy(grad_tile.at[slot], out.at[where], gs.at[slot])

        def body(i, carry):
            cols = pl.ds(pl.multiple_of(i * TILE, TILE), TILE)

            @pl.when(i >= 2)
            def _():
                copy(i - 2).wait()

            grad_tile[lax.rem(i, 2)] = dg(left[:, cols], right[...], ((0,), (0,))).astype(BF16)
            copy(i).start()
            return carry

        lax.fori_loop(0, count, body, 0)
        for i in range(max(0, count - 2), count):
            copy(i).wait()

    weight_grad(dy, act, g2)
    advance(gather_ticks, len(gather_ticks))
    share.flow.start()

    shift_sum = jnp.zeros((1, b1.shape[1]), F32)

    def to_norm(g, q):
        r = rows(g, q)
        low = (dg(dy[r], w2[...], ((1,), (0,))) * dpre[r].astype(F32)).astype(BF16)
        dpre[r] = low
        return dg(low, w1[...], ((1,), (1,))), jnp.sum(low.astype(F32), axis=0, keepdims=True)

    def swap(kind, q):
        r = near_rows(q)
        return remote(sbuf.at[kind, r], rbuf.at[kind, r], ss.at[kind, q], sr.at[kind, q], at.sib)

    def y_copy(q):
        r = near_rows(q)
        return remote(ybuf.at[r], yin.at[r], ys.at[q], yr.at[q], at.peer)

    for kind in range(2):
        for q in range(tiles):
            r = near_rows(q)
            value, total = to_norm(3 - 2 * kind, q)
            sbuf[kind, r] = value.astype(BF16)
            shift_sum += total
            swap(kind, q).start()
            value, total = to_norm(2 - 2 * kind, q)
            shift_sum += total
            swap(kind, q).wait_recv()
            value += rbuf[kind, r].astype(F32)
            if kind == 0:
                ybuf[r] = value.astype(BF16)
                y_copy(q).start()
            else:
                acc[r] = value
                advance(share_ticks)

    weight_grad(two, dpre, g1)
    advance(share_ticks)

    def swap_out(kind, q):
        r = near_rows(q)
        return remote(sbuf.at[kind, r], mbuf.at[kind, r], ts.at[kind, q], tr.at[kind, q], at.sib)

    def other_out(q):
        r = near_rows(q)
        return pltpu.make_async_copy(mbuf.at[0, r], mlp_other.at[r], outs.at[q])

    def base_out(q):
        return pltpu.make_async_copy(wide_tile.at[q % 2], base.at[near_rows(q)], keeps.at[q])

    for kind in range(2):
        for q in range(tiles):
            r = near_rows(q)
            swap(kind, q).wait_send()
            sbuf[kind, r] = dg(act[rows(3 - 2 * kind, q)], w2[...], ((1,), (1,)), BF16)
            swap_out(kind, q).start()
            value = dg(act[rows(2 - 2 * kind, q)], w2[...], ((1,), (1,)))
            swap_out(kind, q).wait_recv()
            value += mbuf[kind, r].astype(F32)
            if kind == 0:
                mbuf[0, r] = value.astype(BF16)
                other_out(q).start()
            else:
                if q >= 2:
                    base_out(q - 2).wait()
                wide_tile[q % 2] = hid[r] + value + b2[...]
                base_out(q).start()
        advance(share_ticks)

    def attn_copy(q):
        r = near_rows(q)
        return remote(ybuf.at[r], d_attn.at[c, r], dos.at[q], dor.at[q], at.sib)

    def attn_keep(q):
        r = near_rows(q)
        return pltpu.make_async_copy(ybuf.at[r], d_attn.at[c, r], os.at[q])

    def hid_keep(q):
        r = near_rows(q)
        return pltpu.make_async_copy(acc.at[r], d_hid.at[r], os.at[tiles + q])

    sums = [jnp.zeros((1, hid.shape[1]), F32) for _ in range(4)]
    for q in range(tiles):
        r = near_rows(q)
        y_copy(q).wait()
        grad = acc[r] + yin[r].astype(F32)
        value = hid[r]
        center = value - jnp.mean(value, -1, keepdims=True)
        inverse = lax.rsqrt(jnp.mean(center * center, -1, keepdims=True) + NORM_EPS)
        normal = center * inverse
        out_grad = dy[rows(0, q)].astype(F32)
        total = out_grad + norm_back(grad, normal, inverse, gain[...])
        low = total.astype(BF16)
        ybuf[r] = low
        attn_copy(q).start()
        attn_keep(q).start()
        acc[r] = total
        hid_keep(q).start()
        for i, t in enumerate((low.astype(F32), grad * normal, grad, out_grad)):
            sums[i] += jnp.sum(t, axis=0, keepdims=True)
    for i in range(4):
        vec[i : i + 1] = sums[i]
    vec[4:5] = shift_sum
    vec[5:8] = jnp.zeros((3, hid.shape[1]), F32)

    advance(share_ticks, len(share_ticks))
    share.drain()
    gather.drain()
    part_copy.wait_send()
    for q in range(tiles):
        two_sib(q).wait_send()
        two_peer(q).wait_send()
        two_pass(q).wait_send()
        other_out(q).wait()
        if q >= tiles - 2:
            base_out(q).wait()
        for kind in range(2):
            swap_out(kind, q).wait_send()
        attn_copy(q).wait_send()
        attn_keep(q).wait()
        hid_keep(q).wait()
        there = d_attn.at[1 - c, near_rows(q)]
        remote(there, there, dos.at[q], dor.at[q], at.sib).wait_recv()


def feed(lines, part, tok, proj_bias, gain, shift, b1, b2, w1, w2_own, dy, dy_sib):
    local, width = tok.shape
    rows, quarter = w2_own.shape
    tiles = local // TILE
    anywhere = pl.BlockSpec(memory_space=pl.ANY)
    vmem = pl.BlockSpec(memory_space=pltpu.VMEM)
    dma = pltpu.SemaphoreType.DMA
    slots = pltpu.VMEM((local, width), BF16)
    shape = jax.ShapeDtypeStruct
    return pl.pallas_call(
        functools.partial(feed_kernel, lines),
        in_specs=[anywhere] * 2 + [vmem] * 5 + [anywhere] * 4,
        out_specs=[anywhere] * 6 + [vmem] * 2,
        out_shape=[
            shape((2, local, width), BF16),
            shape((local, width), F32),
            shape((local, width), F32),
            shape((local, width), BF16),
            shape((width, quarter), BF16),
            shape((width, quarter), BF16),
            shape((2, rows, quarter), F32),
            shape((8, width), F32),
        ],
        scratch_shapes=[
            pltpu.VMEM((width, quarter), BF16),
            pltpu.VMEM((width, quarter), BF16),
            pltpu.VMEM((4 * local, width), BF16),
            pltpu.VMEM((4 * local, width), BF16),
            pltpu.VMEM((4 * local, quarter), BF16),
            pltpu.VMEM((4 * local, quarter), BF16),
            pltpu.VMEM((local, width), F32),
            pltpu.VMEM((2, local, width), BF16),
            pltpu.VMEM((2, local, width), BF16),
            pltpu.VMEM((2, local, width), BF16),
            slots,
            slots,
            pltpu.VMEM((local, width), F32),
            pltpu.VMEM((2, TILE, quarter), BF16),
            pltpu.VMEM((2, TILE, width), F32),
            dma((7,)), dma, dma,
            dma((3, tiles)), dma((3, tiles)),
            dma((2, tiles)), dma((2, tiles)), dma((2, tiles)), dma((2, tiles)),
            dma((tiles,)), dma((tiles,)), dma((2 * tiles,)), dma((tiles,)), dma((tiles,)), dma((2,)),
            dma((tiles,)), dma((tiles,)),
        ]
        + gather_scratch(lines, quarter)
        + share_scratch(lines, rows, quarter),
        compiler_params=pltpu.CompilerParams(
            collective_id=2, has_side_effects=True, vmem_limit_bytes=63 << 20
        ),
        name="feed",
    )(part, tok, proj_bias[None], gain[None], shift[None], b1[None], b2[None], w1, w2_own, dy, dy_sib)


def norm_back(grad_out, normal, inverse, gain):
    scaled = grad_out * gain
    return inverse * (
        scaled
        - jnp.mean(scaled, -1, keepdims=True)
        - normal * jnp.mean(scaled * normal, -1, keepdims=True)
    )


class Links:
    def __init__(self, shards):
        self.shards = shards
        self.lines = shards // 2
        self.s = lax.axis_index("shard")
        self.c = lax.axis_index("ctx")
        self.y = lax.axis_index("tp")
        self.line = self.s // 2
        self.side = self.s % 2
        self.diag = self.c == self.y

    def send(self, value, target, where=lambda c, y: True):
        flat = lambda s, c, y: (s * 2 + c) * 2 + y
        pairs = []
        for s in range(self.shards):
            for c in range(2):
                for y in range(2):
                    if where(c, y):
                        pairs.append((flat(s, c, y), flat(*target(s, c, y))))
        return lax.ppermute(value, AXES, pairs)

    def across(self, value, where=lambda c, y: True):
        return self.send(value, lambda s, c, y: (s, c, 1 - y), where)


def per_device(
    tokens,
    patch_meta,
    attn_norm_gain,
    attn_norm_bias,
    qkv_weight,
    qkv_bias,
    proj_weight,
    proj_bias,
    mlp_norm_gain,
    mlp_norm_bias,
    fc1_weight,
    fc1_bias,
    fc2_weight,
    fc2_bias,
    cotangent,
    *,
    shards,
):
    net = Links(shards)
    c, y = net.c, net.y
    local = tokens.shape[2]
    width = tokens.shape[3]
    full = patch_meta.shape[3]
    inner = qkv_weight.shape[2]
    rows = width // shards
    quarter = fc1_weight.shape[1] // 2
    pick = lambda t, i, d=0: lax.dynamic_index_in_dim(t, i, d, False)
    mine_or = lambda own, other: jnp.where(net.diag, own, other)

    def both(own, other, index):
        return jnp.where(index == 0, jnp.stack([own, other]), jnp.stack([other, own]))

    attn_block = jnp.concatenate([qkv_weight, proj_weight.T[None]], axis=0)
    grad_out = cotangent.reshape(2, local, width)
    tok = pick(tokens, y).reshape(local, width)
    attn_full, normed, grad_out_sib, bias_qkv = collect(
        net.lines, attn_block, tok, attn_norm_gain, attn_norm_bias, grad_out, qkv_bias
    )
    fc1_block = lax.dynamic_slice_in_dim(fc1_weight, c * quarter, quarter, 1)
    fc2_block = lax.dynamic_slice_in_dim(fc2_weight, c * quarter, quarter, 0).T
    bias_fc1 = lax.dynamic_slice_in_dim(fc1_bias, c * quarter, quarter, 0)

    meta = pick(patch_meta, y, 1).reshape(3, full)
    ids = meta[0]
    cosine, sine = rope_tables(meta[1], meta[2])
    shift = jnp.pad(bias_qkv, ((0, 5), (0, 0)))
    low, mixed, mixed_f, lse, attn_part, fc1_full = attend(
        net.lines, attn_full, normed, shift, cosine, sine, ids, fc1_block
    )
    attn_part = attn_part.reshape(2, local, width)
    d_attn, d_hidden, base, mlp_other, grad_fc1_part, _, fc2_sum, sums_two = feed(
        net.lines, attn_part, tok, proj_bias, mlp_norm_gain, mlp_norm_bias, bias_fc1, fc2_bias,
        fc1_full, fc2_block, grad_out, grad_out_sib,
    )
    d_one_part, grad_qkv_part, grad_proj_part, qkv_shift, fc1_sum, out_own, out_peer = attend_back(
        net.lines, low, mixed_f, lse, cosine, sine, ids, attn_full, normed, mixed, d_attn,
        grad_fc1_part, mlp_other, base,
    )
    d_one_part = d_one_part.reshape(2, local, width)
    qkv_shift = qkv_shift[:, 0]
    block_output = both(out_own, out_peer, y)

    fc1_shift = sums_two[4]
    zero_qkv, zero_fc1 = jnp.zeros_like(qkv_shift), jnp.zeros_like(fc1_shift)
    small = jnp.concatenate(
        [
            jnp.zeros((2 * width,), F32),
            sums_two[0],
            sums_two[1],
            sums_two[2],
            sums_two[3],
            jnp.where(c == 0, qkv_shift, zero_qkv).reshape(-1),
            jnp.where(c == 1, qkv_shift, zero_qkv).reshape(-1),
        ]
        + [jnp.where((y == i) & (c == j), fc1_shift, zero_fc1) for i in range(2) for j in range(2)]
    )
    blocks = (net.lines, 2, rows, inner)
    attn_sum, grad_in, grad_in_peer, small = settle(
        net.lines, grad_qkv_part.reshape((3,) + blocks), grad_proj_part.reshape(blocks), d_one_part,
        d_hidden, tok, attn_norm_gain, small.reshape(-1, width),
    )
    small = small.reshape(-1)
    input_grad = both(grad_in, grad_in_peer, y).astype(F32)
    grad_qkv, grad_proj = attn_sum[:3], attn_sum[3].T
    grad_fc1 = jnp.moveaxis(fc1_sum, 0, 1).reshape(rows, 2 * quarter)
    grad_fc2 = jnp.moveaxis(fc2_sum, 1, 2).reshape(2 * quarter, rows)

    vec = lambda i: small[i * width : (i + 1) * width]
    at = 6 * width
    qkv_shifts = small[at : at + 6 * inner].reshape(2, 3, inner)
    fc1_shifts = small[at + 6 * inner :].reshape(2, 2 * quarter)
    out_shape = tokens.shape
    return (
        block_output.reshape(out_shape),
        input_grad.reshape(out_shape),
        vec(0),
        vec(1),
        grad_qkv,
        pick(qkv_shifts, y),
        grad_proj,
        vec(2),
        vec(3),
        vec(4),
        grad_fc1,
        pick(fc1_shifts, y),
        grad_fc2,
        vec(5),
    )


def solution(mesh):
    slots = P(None, "shard", "ctx", None)
    placed = (
        slots,
        P(None, None, "shard", None),
        P(),
        P(),
        P(None, "shard", "tp"),
        P(None, "tp"),
        P("tp", "shard"),
        P(),
        P(),
        P(),
        P("shard", "tp"),
        P("tp"),
        P("tp", "shard"),
        P(),
        slots,
    )
    return jax.shard_map(
        functools.partial(per_device, shards=mesh.shape["shard"]),
        mesh=mesh,
        in_specs=placed,
        out_specs=(
            slots,
            slots,
            P(),
            P(),
            P(None, "shard", "tp"),
            P(None, "tp"),
            P("tp", "shard"),
            P(),
            P(),
            P(),
            P("shard", "tp"),
            P("tp"),
            P("tp", "shard"),
            P(),
        ),
        check_vma=False,
    )
```

```python
import functools
import math

import jax
import jax.numpy as jnp
from jax import lax
from jax.experimental import pallas as pl
from jax.experimental.pallas import tpu as pltpu
from jax.sharding import PartitionSpec as P

HDIM = 80
NORM_EPS = 1e-06
GELU = 1.702
ROPE_BASE = 10000.0
SCALE = 1.0 / math.sqrt(HDIM)
LOG2E = 1.0 / math.log(2.0)
NEG = -1e30
F32 = jnp.float32
BF16 = jnp.bfloat16
AXES = ("shard", "ctx", "tp")
QB = 256
AHEAD = 2
KEPT = 3
FIRST = 4
SLICE = 384
TILE = 256


def dg(left, right, dims, out=F32):
    return lax.dot_general(left, right, (dims, ((), ())), preferred_element_type=F32).astype(out)


def rope_rows(t, cosine, sine):
    half = t.shape[0] // 2
    first, second = t[:half], t[half:]
    return jnp.concatenate([first * cosine - second * sine, second * cosine + first * sine], axis=0)


def rope_rows_back(t, cosine, sine):
    half = t.shape[0] // 2
    first, second = t[:half], t[half:]
    return jnp.concatenate([first * cosine + second * sine, second * cosine - first * sine], axis=0)


def fill_bias(bias, idc_ref, idr_ref):
    @pl.when(pl.program_id(0) == 0)
    def _():
        bias[...] = jnp.where(idc_ref[...] == idr_ref[...], 0.0, NEG)


def at_step(h, action):
    @pl.when(pl.program_id(0) == h)
    def _():
        action()


def spread(ticks, heads):
    plan = [[] for _ in range(heads)]
    for i, tick in enumerate(ticks):
        plan[i * (heads - 1) // max(1, len(ticks) - 1)].append(tick)
    return plan


def run_ticks(plan):
    for h, ticks in enumerate(plan):
        if ticks:
            at_step(h, lambda ticks=ticks: [tick() for tick in ticks])


def attend_kernel(
    lines, heads, weights, normed, shift, cos_ref, sin_ref, idc_ref, idr_ref, w_own,
    low_ref, mixed_ref, outf_ref, lse_ref, part_ref, w_full,
    bias, proj_in, wv, rows_in, loads, own_sem, zs, zr, xs, xr,
):
    at = Place(lines)
    h = pl.program_id(0)
    gather = Gather(at, w_own, w_full, columns_of(w_own.shape[1]), own_sem, zs, zr, xs, xr)
    local = rows_in.shape[0] // 2
    copies = [
        pltpu.make_async_copy(weights, wv, loads.at[0]),
        pltpu.make_async_copy(normed.at[0], rows_in.at[pl.ds(0, local)], loads.at[1]),
        pltpu.make_async_copy(normed.at[1], rows_in.at[pl.ds(local, local)], loads.at[2]),
    ]

    @pl.when(h == 0)
    def _():
        for copy in copies:
            copy.start()
        at.greet()
        gather.start()
        for copy in copies:
            copy.wait()
        columns = shift[...].T
        for j in range(3):
            proj_in[j] = dg(wv[j], rows_in[...], ((0,), (1,))) + columns[:, j : j + 1]

    fill_bias(bias, idc_ref, idr_ref)
    cosine, sine = cos_ref[...], sin_ref[...]
    mine = pl.ds(pl.multiple_of(h * HDIM, HDIM), HDIM)
    query = rope_rows(proj_in[0, mine], cosine, sine).astype(BF16)
    key_f = rope_rows(proj_in[1, mine], cosine, sine)
    value = proj_in[2, mine].astype(BF16)
    low_ref[0] = query
    low_ref[1] = key_f.astype(BF16)
    low_ref[2] = value
    key_nat = key_f.T.astype(BF16)
    length = query.shape[1]
    factor = SCALE * LOG2E
    for start in range(0, length, QB):
        cols = slice(start, start + QB)
        logits = dg(key_nat, query[:, cols], ((1,), (0,))) + bias[:, cols]
        peak = jnp.max(logits, axis=0, keepdims=True)
        probs = jnp.exp2((logits - peak) * factor)
        total = jnp.sum(probs, axis=0, keepdims=True)
        mixed = dg(value, probs.astype(BF16), ((1,), (0,))) * (1.0 / total)
        mixed_ref[mine, cols] = mixed.astype(BF16)
        outf_ref[:, cols] = mixed
        lse_ref[0, :, cols] = peak * factor + jnp.log2(total)

    ticks = [functools.partial(gather.tick, i) for i in range(len(gather.pieces))]
    run_ticks(spread(ticks, heads))

    @pl.when(h == heads - 1)
    def _():
        def body(i, carry):
            r = pl.ds(pl.multiple_of(i * QB, QB), QB)
            part_ref[r] = dg(mixed_ref[:, r], wv[3], ((0,), (1,)), BF16)
            return carry

        lax.fori_loop(0, length // QB, body, 0)
        gather.finish()
        gather.drain()


def attend(lines, weights, normed, shift, cosine, sine, ids, w_own):
    _, width, inner = weights.shape
    length = ids.shape[0]
    heads = inner // HDIM
    half = HDIM // 2
    head = lambda h: (0, h, 0)
    whole = lambda h: (0, 0)
    rows, quarter = w_own.shape
    anywhere = pl.BlockSpec(memory_space=pl.ANY)
    return pl.pallas_call(
        functools.partial(attend_kernel, lines, heads),
        grid=(heads,),
        in_specs=[
            anywhere,
            anywhere,
            pl.BlockSpec((8, inner), whole),
            pl.BlockSpec((half, length), whole),
            pl.BlockSpec((half, length), whole),
            pl.BlockSpec((length, 1), whole),
            pl.BlockSpec((1, length), whole),
            anywhere,
        ],
        out_specs=[
            pl.BlockSpec((3, HDIM, length), head),
            pl.BlockSpec((inner, length), whole),
            pl.BlockSpec((HDIM, length), lambda h: (h, 0)),
            pl.BlockSpec((1, 1, length), lambda h: (h, 0, 0)),
            pl.BlockSpec((length, width), whole),
            anywhere,
        ],
        out_shape=[
            jax.ShapeDtypeStruct((3, inner, length), BF16),
            jax.ShapeDtypeStruct((inner, length), BF16),
            jax.ShapeDtypeStruct((inner, length), F32),
            jax.ShapeDtypeStruct((heads, 1, length), F32),
            jax.ShapeDtypeStruct((length, width), BF16),
            jax.ShapeDtypeStruct((2 * lines * rows, quarter), BF16),
        ],
        scratch_shapes=[
            pltpu.VMEM((length, length), F32),
            pltpu.VMEM((3, inner, length), F32),
            pltpu.VMEM(weights.shape, BF16),
            pltpu.VMEM((length, width), BF16),
            pltpu.SemaphoreType.DMA((3,)),
        ]
        + gather_scratch(lines, quarter),
        compiler_params=pltpu.CompilerParams(
            collective_id=3, has_side_effects=True, vmem_limit_bytes=63 << 20
        ),
        cost_estimate=pl.CostEstimate(
            flops=4 * inner * length * length + 8 * inner * length * width,
            transcendentals=heads * length * length,
            bytes_accessed=26 * inner * length,
        ),
        name="attend",
    )(weights, normed, shift, cosine, sine, ids[:, None], ids[None, :], w_own)


def attend_back_kernel(
    lines, heads, low_ref, outf_ref, lse_ref, cos_ref, sin_ref, idc_ref, idr_ref,
    weights, normed, mixed, d_attn, w_grad, w_grad_two, other, base,
    one_ref, qkv_grad, proj_grad, shift_ref, w_out, out_own, out_peer,
    bias, dq, dk, dv, d_mixed, d_proj, wv, rows_in, mixed_in, base_in, other_in, tile_buf, w_sum,
    loads, ys, yr, ts, *share_refs
):
    at = Place(lines)
    h = pl.program_id(0)
    slices = [(w_grad,) + piece for piece in columns_of(w_grad.shape[1])]
    slices = [(w_grad_two,) + piece for piece in columns_of(w_grad.shape[1])[KEPT:]] + slices
    share = Share(at, slices, w_sum, *share_refs)
    length, width = rows_in.shape
    local = length // 2

    def load_rows(source):
        return [
            pltpu.make_async_copy(source.at[i], rows_in.at[pl.ds(i * local, local)], loads.at[i])
            for i in range(2)
        ]

    mixed_copy = pltpu.make_async_copy(mixed, mixed_in, loads.at[2])
    weight_copy = pltpu.make_async_copy(weights, wv, loads.at[3])
    base_copy = pltpu.make_async_copy(base, base_in, loads.at[4])
    chunk = local // 2
    chunks = [pl.ds(q * chunk, chunk) for q in range(2)]
    other_copies = [
        remote(other.at[r], other_in.at[r], ys.at[0, q], yr.at[0, q], at.peer) for q, r in enumerate(chunks)
    ]
    out_copies = [
        remote(out_own.at[r], out_peer.at[r], ys.at[1, q], yr.at[1, q], at.peer) for q, r in enumerate(chunks)
    ]

    @pl.when(h == 0)
    def _():
        for copy in load_rows(d_attn) + [mixed_copy, weight_copy, base_copy]:
            copy.start()
        at.greet()
        share.flow.start()
        other_copies[0].start()
        for copy in load_rows(d_attn) + [mixed_copy, weight_copy]:
            copy.wait()
        d_mixed[...] = dg(wv[3], rows_in[...], ((0,), (1,)), BF16)

        def body(i, carry):
            cols = pl.ds(pl.multiple_of(i * QB, QB), QB)
            proj_grad[cols] = dg(rows_in[:, cols], mixed_in[...], ((0,), (1,)), BF16)
            return carry

        lax.fori_loop(0, width // QB, body, 0)
        other_copies[1].start()
        for copy in load_rows(normed):
            copy.start()

    fill_bias(bias, idc_ref, idr_ref)
    cosine, sine = cos_ref[...], sin_ref[...]
    mine = pl.ds(pl.multiple_of(h * HDIM, HDIM), HDIM)
    query, key = low_ref[0], low_ref[1]
    grad = d_mixed[mine]
    grad_f = grad.astype(F32)
    delta = jnp.sum(grad_f * outf_ref[...], axis=0, keepdims=True)
    nat = lambda t: t.astype(F32).T.astype(BF16)
    query_nat, key_nat, value_nat, grad_nat = nat(query), nat(key), nat(low_ref[2]), nat(grad)
    lse = lse_ref[0]
    factor = SCALE * LOG2E
    for start in range(0, length, QB):
        cols = slice(start, start + QB)
        logits = dg(key_nat, query[:, cols], ((1,), (0,)))
        probs = jnp.exp2(logits * factor + bias[:, cols] - lse[:, cols])
        d_probs = dg(value_nat, grad[:, cols], ((1,), (0,)))
        d_logits = (probs * (d_probs - delta[:, cols])).astype(BF16)
        part_v = dg(probs.astype(BF16), grad_nat[cols], ((1,), (0,)))
        part_k = dg(d_logits, query_nat[cols], ((1,), (0,)))
        dq[:, cols] = dg(key, d_logits, ((1,), (0,)))
        if start == 0:
            dv[...] = part_v
            dk[...] = part_k
        else:
            dv[...] += part_v
            dk[...] += part_k
    d_proj[0, mine] = rope_rows_back(dq[...] * SCALE, cosine, sine).astype(BF16)
    d_proj[1, mine] = rope_rows_back(dk[...].T * SCALE, cosine, sine).astype(BF16)
    d_proj[2, mine] = dv[...].T.astype(BF16)

    def out_rows(q):
        r = chunks[q]
        other_copies[q].wait()
        out_own[r] = (base_in[r] + other_in[r].astype(F32)).astype(BF16)
        out_copies[q].start()

    @pl.when(h == 1)
    def _():
        base_copy.wait()
        out_rows(0)

    @pl.when(h == heads // 2)
    def _():
        out_rows(1)

    ticks = share.flow.ticks()
    early = min(len(ticks), heads // 2 + 1)
    for i in range(early):
        at_step(max(0, 2 * i - 1), ticks[i])
    ticks = ticks[early:]

    @pl.when(h == heads - 1)
    def _():
        for copy in load_rows(normed):
            copy.wait()
        one_rows = jnp.ones((8, length), BF16)

        def one_body(i, carry):
            r = pl.ds(pl.multiple_of(i * QB, QB), QB)
            total = dg(d_proj[0, :, r], wv[0], ((0,), (1,)))
            for j in range(1, 3):
                total += dg(d_proj[j, :, r], wv[j], ((0,), (1,)))
            one_ref[r] = total.astype(BF16)
            return carry

        lax.fori_loop(0, length // QB, one_body, 0)
        for tick in ticks[:1]:
            tick()
        count = width // QB

        def copy_out(i):
            where = pl.ds(pl.multiple_of(lax.rem(i, count) * QB, QB), QB)
            slot = lax.rem(i, 2)
            return pltpu.make_async_copy(tile_buf.at[slot], qkv_grad.at[i // count, where], ts.at[slot])

        def grad_body(i, carry):
            cols = pl.ds(pl.multiple_of(lax.rem(i, count) * QB, QB), QB)

            @pl.when(i >= 2)
            def _():
                copy_out(i - 2).wait()

            tile_buf[lax.rem(i, 2)] = dg(rows_in[:, cols], d_proj[i // count], ((0,), (1,)), BF16)
            copy_out(i).start()
            return carry

        lax.fori_loop(0, 3 * count, grad_body, 0)
        for i in range(max(0, 3 * count - 2), 3 * count):
            copy_out(i).wait()
        for j in range(3):
            shift_ref[j] = dg(one_rows, d_proj[j], ((1,), (1,)))
        for tick in ticks[1:]:
            tick()
        share.drain()
        w_out[...] = w_sum[...]
        for copy in out_copies:
            copy.wait()


def attend_back(lines, low, outf, lse, cosine, sine, ids, *arrays):
    weights, w_grad = arrays[0], arrays[4]
    _, inner, length = low.shape
    width = weights.shape[1]
    local = length // 2
    heads = inner // HDIM
    half = HDIM // 2
    w_rows, quarter = w_grad.shape
    rows = w_rows // (2 * lines)
    pieces = columns_of(quarter)[KEPT:] + columns_of(quarter)
    columns = sum(count for _, count in pieces)
    head = lambda h: (0, h, 0)
    whole = lambda h: (0, 0)
    cube = lambda h: (0, 0, 0)
    anywhere = pl.BlockSpec(memory_space=pl.ANY)
    dma = pltpu.SemaphoreType.DMA
    shape = jax.ShapeDtypeStruct
    return pl.pallas_call(
        functools.partial(attend_back_kernel, lines, heads),
        grid=(heads,),
        in_specs=[
            pl.BlockSpec((3, HDIM, length), head),
            pl.BlockSpec((HDIM, length), lambda h: (h, 0)),
            pl.BlockSpec((1, 1, length), lambda h: (h, 0, 0)),
            pl.BlockSpec((half, length), whole),
            pl.BlockSpec((half, length), whole),
            pl.BlockSpec((length, 1), whole),
            pl.BlockSpec((1, length), whole),
        ]
        + [anywhere] * 8,
        out_specs=[
            pl.BlockSpec((length, width), whole),
            anywhere,
            pl.BlockSpec((width, inner), whole),
            pl.BlockSpec((3, 8, inner), cube),
            pl.BlockSpec((2, rows, columns), cube),
            pl.BlockSpec((local, width), whole),
            anywhere,
        ],
        out_shape=[
            shape((length, width), BF16),
            shape((3, width, inner), BF16),
            shape((width, inner), BF16),
            shape((3, 8, inner), F32),
            shape((2, rows, columns), F32),
            shape((local, width), BF16),
            shape((local, width), BF16),
        ],
        scratch_shapes=[
            pltpu.VMEM((length, length), F32),
            pltpu.VMEM((HDIM, length), F32),
            pltpu.VMEM((length, HDIM), F32),
            pltpu.VMEM((length, HDIM), F32),
            pltpu.VMEM((inner, length), BF16),
            pltpu.VMEM((3, inner, length), BF16),
            pltpu.VMEM(weights.shape, BF16),
            pltpu.VMEM((length, width), BF16),
            pltpu.VMEM((inner, length), BF16),
            pltpu.VMEM((local, width), F32),
            pltpu.VMEM((local, width), BF16),
            pltpu.VMEM((2, QB, inner), BF16),
            pltpu.VMEM((2, rows, columns), F32),
            dma((5,)), dma((2, 2)), dma((2, 2)), dma((2,)),
        ]
        + share_scratch(lines, rows, pieces),
        compiler_params=pltpu.CompilerParams(
            collective_id=4, has_side_effects=True, vmem_limit_bytes=63 << 20
        ),
        cost_estimate=pl.CostEstimate(
            flops=10 * inner * length * length + 20 * inner * length * width,
            transcendentals=heads * length * length,
            bytes_accessed=18 * inner * length,
        ),
        name="attend_back",
    )(low, outf, lse, cosine, sine, ids[:, None], ids[None, :], *arrays)


def rope_tables(patch_row, patch_col):
    quarter = HDIM // 4
    frequency = ROPE_BASE ** (-2.0 * jnp.arange(quarter, dtype=F32) / (HDIM // 2))
    angles = jnp.concatenate(
        [
            frequency[:, None] * patch_row.astype(F32)[None, :],
            frequency[:, None] * patch_col.astype(F32)[None, :],
        ],
        axis=0,
    )
    return jnp.cos(angles), jnp.sin(angles)


MESH = pl.DeviceIdType.MESH


def remote(src, dst, send_sem, recv_sem, device):
    return pltpu.make_async_remote_copy(
        src_ref=src,
        dst_ref=dst,
        send_sem=send_sem,
        recv_sem=recv_sem,
        device_id=device,
        device_id_type=MESH,
    )


class Place:
    def __init__(self, lines):
        self.lines = lines
        self.s = lax.axis_index("shard")
        self.c = lax.axis_index("ctx")
        self.y = lax.axis_index("tp")
        self.line = self.s // 2
        self.side = lax.rem(self.s, 2)
        self.sib = (self.s, 1 - self.c, self.y)
        self.peer = (self.s, self.c, 1 - self.y)
        self.beside = (self.line * 2 + 1 - self.side, self.c, self.y)

    def ahead(self, k):
        return (lax.rem(self.line + k, self.lines) * 2 + self.side, self.c, self.y)

    def source(self, k):
        return lax.rem(self.line + self.lines - k, self.lines) * 2

    def greet(self):
        barrier = pltpu.get_barrier_semaphore()
        others = [self.sib, self.peer, self.beside] + [self.ahead(k) for k in range(1, self.lines)]
        for other in others:
            pl.semaphore_signal(barrier, inc=1, device_id=other, device_id_type=MESH)
        pl.semaphore_wait(barrier, len(others))


def norm_rows(values):
    center = values - jnp.mean(values, -1, keepdims=True)
    spread = jnp.mean(center * center, -1, keepdims=True)
    return center * lax.rsqrt(spread + NORM_EPS)


def collect_kernel(
    lines, pieces, block, tok, gain, shift, dy, qb,
    out, normed, dy_sib, qb_out,
    norm_buf, own_sem, zs, zr, xs, xr, ys, yr, ms, mr,
):
    at = Place(lines)
    diag = at.c == at.y

    def part(p, s):
        j, first, count, _ = pieces[p]
        rows = block.shape[1]
        return out.at[j, pl.ds(pl.multiple_of(s * rows, rows), rows), pl.ds(first, count)]

    def own(p):
        j, first, count, _ = pieces[p]
        return block.at[j, :, pl.ds(first, count)]

    def z_copy(p, k, src):
        return remote(src, part(p, at.s), zs.at[p, k], zr.at[p, k], at.ahead(k))

    def x_copy(p, k, src):
        return remote(src, part(p, at.source(k) + at.side), xs.at[p, k], xr.at[p, k], at.beside)

    def y_copy(p, i, src, s):
        return remote(src, part(p, s), ys.at[p, i], yr.at[p, i], at.peer)

    def near(k):
        return at.source(k) + at.side

    def far(k):
        return at.source(k) + 1 - at.side

    def z_wait(p, k):
        z_copy(p, k, part(p, near(k))).wait_recv()

    def x_wait(p, k):
        x_copy(p, k, part(p, far(k))).wait_recv()

    def y_wait(p, i, s):
        y_copy(p, i, part(p, s), s).wait_recv()

    late = [p for p in range(len(pieces)) if pieces[p][3]]
    early = [p for p in range(len(pieces)) if not pieces[p][3]]
    order = late + early
    at.greet()

    own_rows = pl.ds(pl.multiple_of(at.s * block.shape[1], block.shape[1]), block.shape[1])
    own_copy = pltpu.make_async_copy(block, out.at[:, own_rows], own_sem.at[0])
    bias_copy = pltpu.make_async_copy(qb, qb_out, own_sem.at[1])

    @pl.when(diag)
    def _():
        own_copy.start()
        bias_copy.start()
        remote(qb, qb_out, ms.at[0], mr.at[0], at.peer).start()
        for p in early:
            y_copy(p, 0, own(p), at.s).start()
        for p in order[:AHEAD]:
            for k in range(1, lines):
                z_copy(p, k, own(p)).start()

    dy_copy = remote(dy, dy_sib, ms.at[1], mr.at[1], at.sib)
    dy_copy.start()
    norm_buf[...] = (norm_rows(tok[...].astype(F32)) * gain[...] + shift[...]).astype(BF16)
    norm_copy = remote(norm_buf, normed.at[at.c], ms.at[2], mr.at[2], at.sib)
    norm_copy.start()
    norm_keep = pltpu.make_async_copy(norm_buf, normed.at[at.c], own_sem.at[2])
    norm_keep.start()

    @pl.when(diag)
    def _():
        for step in range(len(order) + 1):
            if step < len(order):
                p = order[step]
                if step + AHEAD < len(order):
                    for k in range(1, lines):
                        z_copy(order[step + AHEAD], k, own(order[step + AHEAD])).start()
                x_copy(p, 0, own(p)).start()
                if p in late:
                    y_copy(p, 0, own(p), at.s).start()
                for k in range(1, lines):
                    z_wait(p, k)
                    x_copy(p, k, part(p, near(k))).start()
                    if p in late:
                        y_copy(p, k, part(p, near(k)), near(k)).start()
            if step > 0:
                p = order[step - 1]
                for k in range(lines):
                    x_wait(p, k)
                    if p in late:
                        y_copy(p, lines + k, part(p, far(k)), far(k)).start()
        own_copy.wait()
        bias_copy.wait()
        remote(qb, qb_out, ms.at[0], mr.at[0], at.peer).wait_send()
        for p in order:
            for k in range(1, lines):
                z_copy(p, k, own(p)).wait_send()
            for k in range(lines):
                x_copy(p, k, part(p, near(k))).wait_send()
            y_copy(p, 0, own(p), at.s).wait_send()
            if p in late:
                for k in range(1, lines):
                    y_copy(p, k, part(p, near(k)), near(k)).wait_send()
                for k in range(lines):
                    y_copy(p, lines + k, part(p, far(k)), far(k)).wait_send()

    @pl.when(jnp.logical_not(diag))
    def _():
        for p in early:
            y_wait(p, 0, at.s)
            for k in range(1, lines):
                z_copy(p, k, part(p, at.s)).start()
            x_copy(p, 0, part(p, at.s)).start()
        for step in range(len(early) + 1):
            if step < len(early):
                p = early[step]
                for k in range(1, lines):
                    z_wait(p, k)
                    x_copy(p, k, part(p, near(k))).start()
            if step > 0:
                for k in range(lines):
                    x_wait(early[step - 1], k)
        for p in early:
            for k in range(1, lines):
                z_copy(p, k, part(p, at.s)).wait_send()
            for k in range(lines):
                x_copy(p, k, part(p, near(k))).wait_send()
        remote(qb, qb_out, ms.at[0], mr.at[0], at.peer).wait_recv()
        for p in late:
            for k in range(lines):
                y_wait(p, k, near(k))
                y_wait(p, lines + k, far(k))

    dy_copy.wait()
    norm_copy.wait_send()
    remote(norm_buf, normed.at[1 - at.c], ms.at[2], mr.at[2], at.sib).wait_recv()
    norm_keep.wait()


def collect(lines, block, tok, gain, shift, dy, qb):
    groups, rows, inner = block.shape
    local, width = tok.shape
    cut = (inner * 3 // 5) // 128 * 128
    pieces = [(j, f, n, i < 5) for i, (j, f, n) in enumerate((j, f, n) for j in range(4) for f, n in ((0, cut), (cut, inner - cut)))]
    n = len(pieces)
    anywhere = pl.BlockSpec(memory_space=pl.ANY)
    vmem = pl.BlockSpec(memory_space=pltpu.VMEM)
    dma = pltpu.SemaphoreType.DMA
    return pl.pallas_call(
        functools.partial(collect_kernel, lines, pieces),
        in_specs=[anywhere, vmem, vmem, vmem, anywhere, anywhere],
        out_specs=[anywhere] * 4,
        out_shape=[
            jax.ShapeDtypeStruct((groups, 2 * lines * rows, inner), BF16),
            jax.ShapeDtypeStruct((2, local, width), BF16),
            jax.ShapeDtypeStruct(dy.shape, BF16),
            jax.ShapeDtypeStruct(qb.shape, F32),
        ],
        scratch_shapes=[
            pltpu.VMEM((local, width), BF16),
            dma((3,)),
            dma((n, lines)),
            dma((n, lines)),
            dma((n, lines)),
            dma((n, lines)),
            dma((n, 2 * lines)),
            dma((n, 2 * lines)),
            dma((3,)),
            dma((3,)),
        ],
        compiler_params=pltpu.CompilerParams(
            collective_id=0, has_side_effects=True, vmem_limit_bytes=63 << 20
        ),
        name="collect",
    )(block, tok, gain[None], shift[None], dy, qb)


class Gather:
    def __init__(self, at, own, full, pieces, own_sem, zs, zr, xs, xr):
        self.at, self.own, self.full, self.pieces = at, own, full, pieces
        self.own_sem, self.zs, self.zr, self.xs, self.xr = own_sem, zs, zr, xs, xr
        self.rows = own.shape[0]

    def part(self, p, s):
        start, count = self.pieces[p]
        return self.full.at[pl.ds(pl.multiple_of(s * self.rows, self.rows), self.rows), pl.ds(start, count)]

    def z_copy(self, p, k):
        start, count = self.pieces[p]
        src = self.own.at[:, pl.ds(start, count)]
        return remote(src, self.part(p, self.at.s), self.zs.at[p, k], self.zr.at[p, k], self.at.ahead(k))

    def x_copy(self, p, k):
        start, count = self.pieces[p]
        there = self.part(p, self.at.source(k) + self.at.side)
        src = self.own.at[:, pl.ds(start, count)] if k == 0 else there
        return remote(src, there, self.xs.at[p, k], self.xr.at[p, k], self.at.beside)

    def z_wait(self, p, k):
        there = self.part(p, self.at.source(k) + self.at.side)
        remote(there, there, self.zs.at[p, k], self.zr.at[p, k], self.at.ahead(k)).wait_recv()

    def x_wait(self, p, k):
        there = self.part(p, self.at.source(k) + 1 - self.at.side)
        remote(there, there, self.xs.at[p, k], self.xr.at[p, k], self.at.beside).wait_recv()

    def keep(self):
        there = self.full.at[pl.ds(pl.multiple_of(self.at.s * self.rows, self.rows), self.rows)]
        return pltpu.make_async_copy(self.own, there, self.own_sem)

    def begin(self, p):
        if p < len(self.pieces):
            for k in range(1, self.at.lines):
                self.z_copy(p, k).start()

    def start(self):
        self.keep().start()
        for p in range(AHEAD):
            self.begin(p)
        for p in range(len(self.pieces)):
            self.x_copy(p, 0).start()

    def tick(self, p):
        self.begin(p + AHEAD)
        for k in range(1, self.at.lines):
            self.z_wait(p, k)
            self.x_copy(p, k).start()

    def finish(self):
        for p in range(len(self.pieces)):
            for k in range(self.at.lines):
                self.x_wait(p, k)
        self.keep().wait()

    def drain(self):
        for p in range(len(self.pieces)):
            for k in range(self.at.lines):
                self.x_copy(p, k).wait_send()
                if k > 0:
                    self.z_copy(p, k).wait_send()


class Scatter:
    def __init__(self, at, block, mine, xbuf, zin, xs, xr, zs, zr, load=None):
        self.at, self.block, self.mine, self.xbuf, self.zin = at, block, mine, xbuf, zin
        self.xs, self.xr, self.zs, self.zr, self.load = xs, xr, zs, zr, load

    def x_copy(self, row):
        src = self.block(row, 1 - self.at.side)
        return remote(src, self.xbuf.at[row], self.xs.at[row], self.xr.at[row], self.at.beside)

    def load_copy(self, row):
        return pltpu.make_async_copy(self.block(row, self.at.side), self.mine.at[row], self.load.at[row])

    def z_copy(self, k):
        row = lax.rem(self.at.line + k, self.at.lines)
        return remote(self.mine.at[row], self.zin.at[k], self.zs.at[k], self.zr.at[k], self.at.ahead(k))

    def start(self):
        for row in range(self.at.lines):
            self.x_copy(row).start()
            if self.load is not None:
                self.load_copy(row).start()

    def middle(self):
        for row in range(self.at.lines):
            self.x_copy(row).wait_recv()
            if self.load is not None:
                self.load_copy(row).wait()
                here = self.mine[row]
            else:
                here = self.block(row, self.at.side)[...]
            self.mine[row] = (here.astype(F32) + self.xbuf[row].astype(F32)).astype(BF16)
        for k in range(1, self.at.lines):
            self.z_copy(k).start()

    def finish(self):
        total = self.mine[self.at.line].astype(F32)
        for k in range(1, self.at.lines):
            self.z_copy(k).wait_recv()
            total += self.zin[k].astype(F32)
        return total

    def drain(self):
        for row in range(self.at.lines):
            self.x_copy(row).wait_send()
        for k in range(1, self.at.lines):
            self.z_copy(k).wait_send()


class Flow:
    def __init__(self, units, begin, done, lag=1):
        self.units, self.begin, self.done, self.lag = units, begin, done, lag

    def start(self):
        for i in range(min(AHEAD, len(self.units))):
            self.begin(i)

    def tick(self, i):
        count = len(self.units)
        if i < count:
            self.units[i].middle()
            if i + AHEAD < count:
                self.begin(i + AHEAD)
        if 0 <= i - self.lag < count:
            self.done(i - self.lag, self.units[i - self.lag].finish())

    def ticks(self):
        return [functools.partial(self.tick, i) for i in range(len(self.units) + self.lag)]


class Share:
    def __init__(self, at, slices, out, mine, xbuf, zin, xs, xr, zs, zr, load, cs, cr):
        rows = out.shape[1]
        self.at, self.out, self.cs, self.cr = at, out, cs, cr
        self.places, units, total = [], [], 0
        for i, (grad, start, count) in enumerate(slices):

            def block(line, side, grad=grad, start=start, count=count):
                first = pl.multiple_of((2 * line + side) * rows, rows)
                return grad.at[pl.ds(first, rows), pl.ds(start, count)]

            cut = lambda ref: ref.at[:, :, pl.ds(total, count)]
            units.append(
                Scatter(
                    at, block, cut(mine), cut(xbuf), cut(zin), xs.at[i], xr.at[i], zs.at[i], zr.at[i], load.at[i]
                )
            )
            self.places.append((total, count))
            total += count
        self.flow = Flow(units, lambda i: units[i].start(), self.done, lag=2)

    def share(self, i, core):
        start, count = self.places[i]
        here = self.out.at[core, :, pl.ds(start, count)]
        return remote(here, here, self.cs.at[i], self.cr.at[i], self.at.sib)

    def done(self, i, total):
        start, count = self.places[i]
        self.out[self.at.c, :, start : start + count] = total
        self.share(i, self.at.c).start()

    def drain(self):
        for i, unit in enumerate(self.flow.units):
            unit.drain()
            self.share(i, self.at.c).wait_send()
            self.share(i, 1 - self.at.c).wait_recv()


def columns_of(quarter):
    return [(start, 256) for start in range(0, quarter, 256)]


def share_scratch(lines, rows, pieces):
    n = len(pieces)
    dma = pltpu.SemaphoreType.DMA
    slab = pltpu.VMEM((lines, rows, sum(count for _, count in pieces)), BF16)
    return [slab] * 3 + [dma((n, lines))] * 5 + [dma((n,))] * 2


def gather_scratch(lines, quarter):
    n = len(columns_of(quarter))
    dma = pltpu.SemaphoreType.DMA
    return [dma] + [dma((n, lines))] * 4


def settle_kernel(
    lines, pieces, qkv, proj, d_one, d_hid, tok, gain, vec,
    attn_out, grad_own, grad_peer, vec_out,
    here, mine, ax, ai, ay, al, one_in, vown, vbuf, vin,
    hs, axs, axr, azs, azr, ays, ayr, cs, cr, vs, vr, os, orr, ms, mr,
):
    at = Place(lines)
    diag = at.c == at.y
    first = [p for p in range(len(pieces)) if pieces[p][3]]
    last = [p for p in range(len(pieces)) if not pieces[p][3]]

    def cut(ref, p):
        _, start, count, _ = pieces[p]
        return ref.at[..., pl.ds(start, count)]

    def source(p):
        j = pieces[p][0]
        return cut(proj if j == 3 else qkv.at[j], p)

    def local_part(p):
        return cut(here.at[pieces[p][0]], p)

    class Direct(Scatter):
        def __init__(self, p):
            j = pieces[p][0]
            super().__init__(
                at, lambda line, side: local_part(p).at[line, side],
                cut(mine.at[j], p), cut(ax.at[j], p), cut(ai.at[j], p),
                axs.at[p], axr.at[p], azs.at[p], azr.at[p],
            )
            self.p = p

        def x_copy(self, row):
            src = source(self.p).at[row, 1 - at.side]
            return remote(src, self.xbuf.at[row], self.xs.at[row], self.xr.at[row], at.beside)

    def summed(p):
        j = pieces[p][0]
        return Scatter(
            at, lambda line, side: cut(ay.at[j, line, side], p),
            cut(mine.at[j], p), cut(ax.at[j], p), cut(ai.at[j], p),
            axs.at[p], axr.at[p], azs.at[p], azr.at[p],
        )

    def pair_copy(p, half):
        side = (1 - at.side, at.side)[half]
        there = cut(ay.at[pieces[p][0], :, side], p)
        return remote(source(p).at[:, side], there, ays.at[p, half], ayr.at[p, half], at.peer)

    def last_copy(p):
        j = pieces[p][0]
        return remote(cut(al.at[j, 0], p), cut(al.at[j, 1], p), ays.at[p, 0], ayr.at[p, 0], at.peer)

    def attn_share(p):
        there = cut(attn_out.at[pieces[p][0]], p)
        return remote(there, there, cs.at[p], cr.at[p], at.sib)

    order = last + first
    diag_units = [Direct(p) for p in last] + [summed(p) for p in first]
    off_units = [Direct(p) for p in last]

    def diag_begin(i):
        p = order[i]
        if p in first:
            j, start, count, _ = pieces[p]
            for half in range(2):
                pair_copy(p, half).wait_recv()
            for row in range(lines):
                for side in range(2):
                    both = local_part(p)[row, side].astype(F32) + cut(ay.at[j, row, side], p)[...].astype(F32)
                    ay[j, row, side, :, start : start + count] = both.astype(BF16)
        diag_units[i].start()

    def diag_done(i, total):
        p = order[i]
        j, start, count, _ = pieces[p]
        attn_out[j, :, start : start + count] = total
        if p in first:
            attn_share(p).start()

    def off_done(i, total):
        j, start, count, _ = pieces[last[i]]
        al[j, 0, :, start : start + count] = total.astype(BF16)
        last_copy(last[i]).start()

    diag_flow = Flow(diag_units, diag_begin, diag_done)
    off_flow = Flow(off_units, lambda i: off_units[i].start(), off_done)

    def ticks(begin, end):
        @pl.when(diag)
        def _():
            for i in range(begin, end):
                diag_flow.tick(i)

        @pl.when(jnp.logical_not(diag))
        def _():
            for i in range(begin, end):
                off_flow.tick(i)

    loads = [
        pltpu.make_async_copy(qkv, here.at[pl.ds(0, 3)], hs.at[0]),
        pltpu.make_async_copy(proj, here.at[3], hs.at[1]),
    ]
    for load in loads:
        load.start()
    at.greet()
    one_copy = remote(d_one.at[1 - at.c], one_in, os, orr, at.sib)
    one_copy.start()

    @pl.when(diag)
    def _():
        for i in range(min(AHEAD, len(last))):
            diag_units[i].start()

    @pl.when(jnp.logical_not(diag))
    def _():
        for p in first:
            for half in range(2):
                pair_copy(p, half).start()
        off_flow.start()

    one_copy.wait_recv()
    local = tok.shape[0]
    tile = TILE // 2
    grad_copies = []
    sums = [jnp.zeros((1, tok.shape[1]), F32) for _ in range(2)]
    for q in range(local // tile):
        r = pl.ds(q * tile, tile)
        value = tok[r].astype(F32)
        center = value - jnp.mean(value, -1, keepdims=True)
        inverse = lax.rsqrt(jnp.mean(center * center, -1, keepdims=True) + NORM_EPS)
        normal = center * inverse
        grad = d_one[at.c, r].astype(F32) + one_in[r].astype(F32)
        grad_own[r] = (d_hid[r] + norm_back(grad, normal, inverse, gain[...])).astype(BF16)
        copy = remote(grad_own.at[r], grad_peer.at[r], ms.at[q], mr.at[q], at.peer)
        grad_copies.append(copy)
        for i, t in enumerate((grad * normal, grad)):
            sums[i] += jnp.sum(t, axis=0, keepdims=True)
    vown[...] = vec[...]
    for i in range(2):
        vown[i : i + 1] = sums[i]

    def small_copy(stage, device):
        src = vown if stage == 0 else vbuf.at[stage - 1]
        return remote(src, vin.at[stage], vs.at[stage], vr.at[stage], device)

    steps = [at.sib, at.peer, at.beside]

    def small_start(stage):
        small_copy(stage, steps[stage]).start()

    def small_add(stage):
        small_copy(stage, steps[stage]).wait_recv()
        before = vown[...] if stage == 0 else vbuf[stage - 1]
        vbuf[stage] = before + vin[stage]

    def line_copy(k):
        return remote(vbuf.at[2], vin.at[3 + at.line], vs.at[2 + k], vr.at[2 + k], at.ahead(k))

    def line_wait(k):
        there = vin.at[3 + at.source(k) // 2]
        remote(vbuf.at[2], there, vs.at[2 + k], vr.at[2 + k], at.ahead(k)).wait_recv()

    small_start(0)
    for load in loads:
        load.wait()
    total_ticks = len(order) + 1
    small_add(0)
    small_start(1)
    for i in range(total_ticks):
        ticks(i, i + 1)
        if i >= 1 and grad_copies[i - 1 : i]:
            grad_copies[i - 1].start()
        if i == total_ticks // 2:
            small_add(1)
            small_start(2)
        if i == total_ticks - 2:
            small_add(2)
            for k in range(1, lines):
                line_copy(k).start()
            vin[3 + at.line] = vbuf[2]

    @pl.when(diag)
    def _():
        for p in last:
            j, start, count, _ = pieces[p]
            last_copy(p).wait_recv()
            attn_out[j, :, start : start + count] += cut(al.at[j, 1], p)[...].astype(F32)
            attn_share(p).start()

    for k in range(1, lines):
        line_wait(k)
    total = vin[3]
    for row in range(1, lines):
        total = total + vin[3 + row]
    vec_out[...] = total

    @pl.when(diag)
    def _():
        for unit in diag_units:
            unit.drain()
        for p in order:
            attn_share(p).wait_send()

    @pl.when(jnp.logical_not(diag))
    def _():
        for unit in off_units:
            unit.drain()
        for p in last:
            last_copy(p).wait_send()
        for p in first:
            for half in range(2):
                pair_copy(p, half).wait_send()
        for p in order:
            attn_share(p).wait_recv()

    for stage in range(3):
        small_copy(stage, steps[stage]).wait_send()
    for k in range(1, lines):
        line_copy(k).wait_send()
    one_copy.wait_send()
    for copy in grad_copies:
        copy.wait()


def settle(lines, qkv, proj, d_one, d_hid, tok, gain, vec):
    _, _, _, rows, inner = qkv.shape
    local, width = tok.shape
    pieces = settle_pieces(inner)
    n = len(pieces)
    tiles = local // TILE * 2
    anywhere = pl.BlockSpec(memory_space=pl.ANY)
    vmem = pl.BlockSpec(memory_space=pltpu.VMEM)
    dma = pltpu.SemaphoreType.DMA
    stage = (4, lines, rows, inner)
    return pl.pallas_call(
        functools.partial(settle_kernel, lines, pieces),
        in_specs=[anywhere] * 2 + [vmem] * 5,
        out_specs=[vmem, vmem, anywhere, vmem],
        out_shape=[
            jax.ShapeDtypeStruct((4, rows, inner), F32),
            jax.ShapeDtypeStruct((local, width), BF16),
            jax.ShapeDtypeStruct((local, width), BF16),
            jax.ShapeDtypeStruct(vec.shape, F32),
        ],
        scratch_shapes=[
            pltpu.VMEM((4, lines, 2, rows, inner), BF16),
            pltpu.VMEM(stage, BF16),
            pltpu.VMEM(stage, BF16),
            pltpu.VMEM(stage, BF16),
            pltpu.VMEM((4, lines, 2, rows, inner), BF16),
            pltpu.VMEM((4, 2, rows, inner), BF16),
            pltpu.VMEM((local, width), BF16),
            pltpu.VMEM(vec.shape, F32),
            pltpu.VMEM((3,) + vec.shape, F32),
            pltpu.VMEM((3 + lines,) + vec.shape, F32),
            dma((2,)),
            dma((n, lines)), dma((n, lines)), dma((n, lines)), dma((n, lines)), dma((n, 2)), dma((n, 2)),
            dma((n,)), dma((n,)), dma((2 + lines,)), dma((2 + lines,)),
            dma, dma, dma((tiles,)), dma((tiles,)),
        ],
        compiler_params=pltpu.CompilerParams(
            collective_id=1, has_side_effects=True, vmem_limit_bytes=63 << 20
        ),
        name="settle",
    )(qkv, proj, d_one, d_hid, tok, gain[None], vec)


def settle_pieces(inner):
    cuts = [(f, min(SLICE, inner - f)) for f in range(0, inner, SLICE)]
    every = [(j, f, n) for j in (3, 0, 1, 2) for f, n in cuts]
    return [(j, f, n, i >= len(every) - FIRST) for i, (j, f, n) in enumerate(every)]


def feed_kernel(
    lines, part, tok, proj_bias, gain, shift, b1, b2, w1_in, w2_own, dy_in, dy_sib,
    d_attn, d_hid, base, mlp_other, g1, g2, g2_out, vec,
    w1, w2, two, dy, act, dpre, hid, sbuf, rbuf, mbuf, ybuf, yin, acc, grad_tile, wide_tile,
    loads, ps, pr, ns, nr, ss, sr, ts, tr, ys, yr, os, dos, dor, gs, outs, keeps,
    own_sem, zs, zr, xs, xr, *share_refs,
):
    at = Place(lines)
    c, y = at.c, at.y
    local = hid.shape[0]
    tiles = local // TILE
    pieces = columns_of(w1.shape[1])
    gather = Gather(at, w2_own, w2, pieces, own_sem, zs, zr, xs, xr)
    share = Share(at, [(g2,) + piece for piece in pieces[:KEPT]], g2_out, *share_refs)
    gather_ticks = [functools.partial(gather.tick, i) for i in range(len(pieces))]
    share_ticks = share.flow.ticks()

    def advance(ticks, count=1):
        for _ in range(count):
            if ticks:
                ticks.pop(0)()

    def rows(g, q):
        return pl.ds((g * tiles + q) * TILE, TILE)

    def group(g):
        return pl.ds(g * local, local)

    def near_rows(q):
        return pl.ds(q * TILE, TILE)

    copies = [
        pltpu.make_async_copy(tok, ybuf, loads.at[0]),
        pltpu.make_async_copy(part.at[c], yin, loads.at[1]),
        pltpu.make_async_copy(w1_in, w1, loads.at[2]),
        pltpu.make_async_copy(dy_in.at[y], dy.at[group(0)], loads.at[3]),
        pltpu.make_async_copy(dy_sib.at[y], dy.at[group(1)], loads.at[4]),
        pltpu.make_async_copy(dy_in.at[1 - y], dy.at[group(2)], loads.at[5]),
        pltpu.make_async_copy(dy_sib.at[1 - y], dy.at[group(3)], loads.at[6]),
    ]
    for copy in copies:
        copy.start()
    at.greet()
    part_copy = remote(part.at[1 - c], rbuf.at[0], ps, pr, at.sib)
    part_copy.start()
    gather.start()

    def two_sib(q):
        return remote(two.at[rows(0, q)], two.at[rows(1, q)], ns.at[0, q], nr.at[0, q], at.sib)

    def two_peer(q):
        return remote(two.at[rows(0, q)], two.at[rows(2, q)], ns.at[1, q], nr.at[1, q], at.peer)

    def two_pass(q):
        return remote(two.at[rows(2, q)], two.at[rows(3, q)], ns.at[2, q], nr.at[2, q], at.sib)

    copies[0].wait()
    copies[1].wait()
    part_copy.wait_recv()
    for q in range(tiles):
        r = near_rows(q)
        value = ybuf[r].astype(F32) + yin[r].astype(F32) + rbuf[0, r].astype(F32) + proj_bias[...]
        hid[r] = value
        two[rows(0, q)] = (norm_rows(value) * gain[...] + shift[...]).astype(BF16)
        two_peer(q).start()
        two_sib(q).start()

    def first_layer(start, count):
        def body(i, carry):
            r = pl.ds(pl.multiple_of((start + i) * TILE, TILE), TILE)
            pre = dg(two[r], w1[...], ((1,), (0,))) + b1[...]
            sig = jax.nn.sigmoid(GELU * pre)
            act[r] = (pre * sig).astype(BF16)
            dpre[r] = (sig + GELU * pre * sig * (1.0 - sig)).astype(BF16)
            return carry

        lax.fori_loop(0, count, body, 0)

    copies[2].wait()
    first_layer(0, tiles)
    advance(gather_ticks)
    for q in range(tiles):
        two_sib(q).wait_recv()
    first_layer(tiles, tiles)
    advance(gather_ticks)
    for q in range(tiles):
        two_peer(q).wait_recv()
        two_pass(q).start()
        first_layer(2 * tiles + q, 1)
        advance(gather_ticks)
    for q in range(tiles):
        two_pass(q).wait_recv()
    first_layer(3 * tiles, tiles)
    for copy in copies[3:]:
        copy.wait()

    def weight_grad(left, right, out):
        count = out.shape[0] // TILE

        def copy(i):
            slot = lax.rem(i, 2)
            where = pl.ds(pl.multiple_of(i * TILE, TILE), TILE)
            return pltpu.make_async_copy(grad_tile.at[slot], out.at[where], gs.at[slot])

        def body(i, carry):
            cols = pl.ds(pl.multiple_of(i * TILE, TILE), TILE)

            @pl.when(i >= 2)
            def _():
                copy(i - 2).wait()

            grad_tile[lax.rem(i, 2)] = dg(left[:, cols], right[...], ((0,), (0,))).astype(BF16)
            copy(i).start()
            return carry

        lax.fori_loop(0, count, body, 0)
        for i in range(max(0, count - 2), count):
            copy(i).wait()

    advance(gather_ticks, len(gather_ticks))
    weight_grad(dy, act, g2)
    gather.finish()
    share.flow.start()

    shift_sum = jnp.zeros((1, b1.shape[1]), F32)

    def to_norm(g, q):
        r = rows(g, q)
        low = (dg(dy[r], w2[...], ((1,), (0,))) * dpre[r].astype(F32)).astype(BF16)
        dpre[r] = low
        return dg(low, w1[...], ((1,), (1,))), jnp.sum(low.astype(F32), axis=0, keepdims=True)

    def swap(kind, q):
        r = near_rows(q)
        return remote(sbuf.at[kind, r], rbuf.at[kind, r], ss.at[kind, q], sr.at[kind, q], at.sib)

    def y_copy(q):
        r = near_rows(q)
        return remote(ybuf.at[r], yin.at[r], ys.at[q], yr.at[q], at.peer)

    for kind in range(2):
        for q in range(tiles):
            r = near_rows(q)
            value, total = to_norm(3 - 2 * kind, q)
            sbuf[kind, r] = value.astype(BF16)
            shift_sum += total
            swap(kind, q).start()
            value, total = to_norm(2 - 2 * kind, q)
            shift_sum += total
            swap(kind, q).wait_recv()
            value += rbuf[kind, r].astype(F32)
            if kind == 0:
                ybuf[r] = value.astype(BF16)
                y_copy(q).start()
            else:
                acc[r] = value
                advance(share_ticks)

    weight_grad(two, dpre, g1)
    advance(share_ticks)

    def swap_out(kind, q):
        r = near_rows(q)
        return remote(sbuf.at[kind, r], mbuf.at[kind, r], ts.at[kind, q], tr.at[kind, q], at.sib)

    def other_out(q):
        r = near_rows(q)
        return pltpu.make_async_copy(mbuf.at[0, r], mlp_other.at[r], outs.at[q])

    def base_out(q):
        return pltpu.make_async_copy(wide_tile.at[q % 2], base.at[near_rows(q)], keeps.at[q])

    for kind in range(2):
        for q in range(tiles):
            r = near_rows(q)
            swap(kind, q).wait_send()
            sbuf[kind, r] = dg(act[rows(3 - 2 * kind, q)], w2[...], ((1,), (1,)), BF16)
            swap_out(kind, q).start()
            value = dg(act[rows(2 - 2 * kind, q)], w2[...], ((1,), (1,)))
            swap_out(kind, q).wait_recv()
            value += mbuf[kind, r].astype(F32)
            if kind == 0:
                mbuf[0, r] = value.astype(BF16)
                other_out(q).start()
            else:
                if q >= 2:
                    base_out(q - 2).wait()
                wide_tile[q % 2] = hid[r] + value + b2[...]
                base_out(q).start()
        advance(share_ticks)

    def attn_copy(q):
        r = near_rows(q)
        return remote(ybuf.at[r], d_attn.at[c, r], dos.at[q], dor.at[q], at.sib)

    def attn_keep(q):
        r = near_rows(q)
        return pltpu.make_async_copy(ybuf.at[r], d_attn.at[c, r], os.at[q])

    def hid_keep(q):
        r = near_rows(q)
        return pltpu.make_async_copy(acc.at[r], d_hid.at[r], os.at[tiles + q])

    sums = [jnp.zeros((1, hid.shape[1]), F32) for _ in range(4)]
    for q in range(tiles):
        r = near_rows(q)
        y_copy(q).wait()
        grad = acc[r] + yin[r].astype(F32)
        value = hid[r]
        center = value - jnp.mean(value, -1, keepdims=True)
        inverse = lax.rsqrt(jnp.mean(center * center, -1, keepdims=True) + NORM_EPS)
        normal = center * inverse
        out_grad = dy[rows(0, q)].astype(F32)
        total = out_grad + norm_back(grad, normal, inverse, gain[...])
        low = total.astype(BF16)
        ybuf[r] = low
        attn_copy(q).start()
        attn_keep(q).start()
        acc[r] = total
        hid_keep(q).start()
        for i, t in enumerate((low.astype(F32), grad * normal, grad, out_grad)):
            sums[i] += jnp.sum(t, axis=0, keepdims=True)
    for i in range(4):
        vec[i : i + 1] = sums[i]
    vec[4:5] = shift_sum
    vec[5:8] = jnp.zeros((3, hid.shape[1]), F32)

    advance(share_ticks, len(share_ticks))
    share.drain()
    gather.drain()
    part_copy.wait_send()
    for q in range(tiles):
        two_sib(q).wait_send()
        two_peer(q).wait_send()
        two_pass(q).wait_send()
        other_out(q).wait()
        if q >= tiles - 2:
            base_out(q).wait()
        for kind in range(2):
            swap_out(kind, q).wait_send()
        attn_copy(q).wait_send()
        attn_keep(q).wait()
        hid_keep(q).wait()
        there = d_attn.at[1 - c, near_rows(q)]
        remote(there, there, dos.at[q], dor.at[q], at.sib).wait_recv()


def feed(lines, part, tok, proj_bias, gain, shift, b1, b2, w1, w2_own, dy, dy_sib):
    local, width = tok.shape
    rows, quarter = w2_own.shape
    kept = columns_of(quarter)[:KEPT]
    tiles = local // TILE
    anywhere = pl.BlockSpec(memory_space=pl.ANY)
    vmem = pl.BlockSpec(memory_space=pltpu.VMEM)
    dma = pltpu.SemaphoreType.DMA
    slots = pltpu.VMEM((local, width), BF16)
    shape = jax.ShapeDtypeStruct
    return pl.pallas_call(
        functools.partial(feed_kernel, lines),
        in_specs=[anywhere] * 2 + [vmem] * 5 + [anywhere] * 4,
        out_specs=[anywhere] * 6 + [vmem] * 2,
        out_shape=[
            shape((2, local, width), BF16),
            shape((local, width), F32),
            shape((local, width), F32),
            shape((local, width), BF16),
            shape((width, quarter), BF16),
            shape((width, quarter), BF16),
            shape((2, rows, sum(n for _, n in kept)), F32),
            shape((8, width), F32),
        ],
        scratch_shapes=[
            pltpu.VMEM((width, quarter), BF16),
            pltpu.VMEM((width, quarter), BF16),
            pltpu.VMEM((4 * local, width), BF16),
            pltpu.VMEM((4 * local, width), BF16),
            pltpu.VMEM((4 * local, quarter), BF16),
            pltpu.VMEM((4 * local, quarter), BF16),
            pltpu.VMEM((local, width), F32),
            pltpu.VMEM((2, local, width), BF16),
            pltpu.VMEM((2, local, width), BF16),
            pltpu.VMEM((2, local, width), BF16),
            slots,
            slots,
            pltpu.VMEM((local, width), F32),
            pltpu.VMEM((2, TILE, quarter), BF16),
            pltpu.VMEM((2, TILE, width), F32),
            dma((7,)), dma, dma,
            dma((3, tiles)), dma((3, tiles)),
            dma((2, tiles)), dma((2, tiles)), dma((2, tiles)), dma((2, tiles)),
            dma((tiles,)), dma((tiles,)), dma((2 * tiles,)), dma((tiles,)), dma((tiles,)), dma((2,)),
            dma((tiles,)), dma((tiles,)),
        ]
        + gather_scratch(lines, quarter)
        + share_scratch(lines, rows, kept),
        compiler_params=pltpu.CompilerParams(
            collective_id=2, has_side_effects=True, vmem_limit_bytes=63 << 20
        ),
        name="feed",
    )(part, tok, proj_bias[None], gain[None], shift[None], b1[None], b2[None], w1, w2_own, dy, dy_sib)


def norm_back(grad_out, normal, inverse, gain):
    scaled = grad_out * gain
    return inverse * (
        scaled
        - jnp.mean(scaled, -1, keepdims=True)
        - normal * jnp.mean(scaled * normal, -1, keepdims=True)
    )


class Links:
    def __init__(self, shards):
        self.shards = shards
        self.lines = shards // 2
        self.s = lax.axis_index("shard")
        self.c = lax.axis_index("ctx")
        self.y = lax.axis_index("tp")
        self.line = self.s // 2
        self.side = self.s % 2
        self.diag = self.c == self.y

    def send(self, value, target, where=lambda c, y: True):
        flat = lambda s, c, y: (s * 2 + c) * 2 + y
        pairs = []
        for s in range(self.shards):
            for c in range(2):
                for y in range(2):
                    if where(c, y):
                        pairs.append((flat(s, c, y), flat(*target(s, c, y))))
        return lax.ppermute(value, AXES, pairs)

    def across(self, value, where=lambda c, y: True):
        return self.send(value, lambda s, c, y: (s, c, 1 - y), where)


def per_device(
    tokens,
    patch_meta,
    attn_norm_gain,
    attn_norm_bias,
    qkv_weight,
    qkv_bias,
    proj_weight,
    proj_bias,
    mlp_norm_gain,
    mlp_norm_bias,
    fc1_weight,
    fc1_bias,
    fc2_weight,
    fc2_bias,
    cotangent,
    *,
    shards,
):
    net = Links(shards)
    c, y = net.c, net.y
    local = tokens.shape[2]
    width = tokens.shape[3]
    full = patch_meta.shape[3]
    inner = qkv_weight.shape[2]
    rows = width // shards
    quarter = fc1_weight.shape[1] // 2
    pick = lambda t, i, d=0: lax.dynamic_index_in_dim(t, i, d, False)
    mine_or = lambda own, other: jnp.where(net.diag, own, other)

    def both(own, other, index):
        return jnp.where(index == 0, jnp.stack([own, other]), jnp.stack([other, own]))

    attn_block = jnp.concatenate([qkv_weight, proj_weight.T[None]], axis=0)
    grad_out = cotangent.reshape(2, local, width)
    tok = pick(tokens, y).reshape(local, width)
    attn_full, normed, grad_out_sib, bias_qkv = collect(
        net.lines, attn_block, tok, attn_norm_gain, attn_norm_bias, grad_out, qkv_bias
    )
    fc1_block = lax.dynamic_slice_in_dim(fc1_weight, c * quarter, quarter, 1)
    fc2_block = lax.dynamic_slice_in_dim(fc2_weight, c * quarter, quarter, 0).T
    bias_fc1 = lax.dynamic_slice_in_dim(fc1_bias, c * quarter, quarter, 0)

    meta = pick(patch_meta, y, 1).reshape(3, full)
    ids = meta[0]
    cosine, sine = rope_tables(meta[1], meta[2])
    shift = jnp.pad(bias_qkv, ((0, 5), (0, 0)))
    low, mixed, mixed_f, lse, attn_part, fc1_full = attend(
        net.lines, attn_full, normed, shift, cosine, sine, ids, fc1_block
    )
    attn_part = attn_part.reshape(2, local, width)
    d_attn, d_hidden, base, mlp_other, grad_fc1_part, grad_fc2_part, fc2_sum, sums_two = feed(
        net.lines, attn_part, tok, proj_bias, mlp_norm_gain, mlp_norm_bias, bias_fc1, fc2_bias,
        fc1_full, fc2_block, grad_out, grad_out_sib,
    )
    d_one_part, grad_qkv_part, grad_proj_part, qkv_shift, fc1_sum, out_own, out_peer = attend_back(
        net.lines, low, mixed_f, lse, cosine, sine, ids, attn_full, normed, mixed, d_attn,
        grad_fc1_part, grad_fc2_part, mlp_other, base,
    )
    late = fc1_sum.shape[2] - quarter
    fc2_sum = jnp.concatenate([fc2_sum, fc1_sum[:, :, :late]], axis=2)
    fc1_sum = fc1_sum[:, :, late:]
    d_one_part = d_one_part.reshape(2, local, width)
    qkv_shift = qkv_shift[:, 0]
    block_output = both(out_own, out_peer, y)

    fc1_shift = sums_two[4]
    zero_qkv, zero_fc1 = jnp.zeros_like(qkv_shift), jnp.zeros_like(fc1_shift)
    small = jnp.concatenate(
        [
            jnp.zeros((2 * width,), F32),
            sums_two[0],
            sums_two[1],
            sums_two[2],
            sums_two[3],
            jnp.where(c == 0, qkv_shift, zero_qkv).reshape(-1),
            jnp.where(c == 1, qkv_shift, zero_qkv).reshape(-1),
        ]
        + [jnp.where((y == i) & (c == j), fc1_shift, zero_fc1) for i in range(2) for j in range(2)]
    )
    blocks = (net.lines, 2, rows, inner)
    attn_sum, grad_in, grad_in_peer, small = settle(
        net.lines, grad_qkv_part.reshape((3,) + blocks), grad_proj_part.reshape(blocks), d_one_part,
        d_hidden, tok, attn_norm_gain, small.reshape(-1, width),
    )
    small = small.reshape(-1)
    input_grad = both(grad_in, grad_in_peer, y).astype(F32)
    grad_qkv, grad_proj = attn_sum[:3], attn_sum[3].T
    grad_fc1 = jnp.moveaxis(fc1_sum, 0, 1).reshape(rows, 2 * quarter)
    grad_fc2 = jnp.moveaxis(fc2_sum, 1, 2).reshape(2 * quarter, rows)

    vec = lambda i: small[i * width : (i + 1) * width]
    at = 6 * width
    qkv_shifts = small[at : at + 6 * inner].reshape(2, 3, inner)
    fc1_shifts = small[at + 6 * inner :].reshape(2, 2 * quarter)
    out_shape = tokens.shape
    return (
        block_output.reshape(out_shape),
        input_grad.reshape(out_shape),
        vec(0),
        vec(1),
        grad_qkv,
        pick(qkv_shifts, y),
        grad_proj,
        vec(2),
        vec(3),
        vec(4),
        grad_fc1,
        pick(fc1_shifts, y),
        grad_fc2,
        vec(5),
    )


def solution(mesh):
    slots = P(None, "shard", "ctx", None)
    placed = (
        slots,
        P(None, None, "shard", None),
        P(),
        P(),
        P(None, "shard", "tp"),
        P(None, "tp"),
        P("tp", "shard"),
        P(),
        P(),
        P(),
        P("shard", "tp"),
        P("tp"),
        P("tp", "shard"),
        P(),
        slots,
    )
    return jax.shard_map(
        functools.partial(per_device, shards=mesh.shape["shard"]),
        mesh=mesh,
        in_specs=placed,
        out_specs=(
            slots,
            slots,
            P(),
            P(),
            P(None, "shard", "tp"),
            P(None, "tp"),
            P("tp", "shard"),
            P(),
            P(),
            P(),
            P("shard", "tp"),
            P("tp"),
            P("tp", "shard"),
            P(),
        ),
        check_vma=False,
    )
```

```python
import functools
import math

import jax
import jax.numpy as jnp
from jax import lax
from jax.experimental import pallas as pl
from jax.experimental.pallas import tpu as pltpu
from jax.sharding import PartitionSpec as P

HDIM = 80
NORM_EPS = 1e-06
GELU = 1.702
ROPE_BASE = 10000.0
SCALE = 1.0 / math.sqrt(HDIM)
LOG2E = 1.0 / math.log(2.0)
NEG = -1e30
F32 = jnp.float32
BF16 = jnp.bfloat16
AXES = ("shard", "ctx", "tp")
QB = 512
AHEAD = 2
LEAD = 1
KEPT = 3
FIRST = 4
SLICE = 384
TILE = 256


def dg(left, right, dims, out=F32):
    return lax.dot_general(left, right, (dims, ((), ())), preferred_element_type=F32).astype(out)


def rope_rows(t, cosine, sine):
    half = t.shape[0] // 2
    first, second = t[:half], t[half:]
    return jnp.concatenate([first * cosine - second * sine, second * cosine + first * sine], axis=0)


def rope_rows_back(t, cosine, sine):
    half = t.shape[0] // 2
    first, second = t[:half], t[half:]
    return jnp.concatenate([first * cosine + second * sine, second * cosine - first * sine], axis=0)


def fill_bias(bias, idc_ref, idr_ref):
    @pl.when(pl.program_id(0) == 0)
    def _():
        bias[...] = jnp.where(idc_ref[...] == idr_ref[...], 0.0, NEG)


def at_step(h, action):
    @pl.when(pl.program_id(0) == h)
    def _():
        action()


def spread(ticks, heads):
    plan = [[] for _ in range(heads)]
    for i, tick in enumerate(ticks):
        plan[i * (heads - 1) // max(1, len(ticks) - 1)].append(tick)
    return plan


def run_ticks(plan):
    for h, ticks in enumerate(plan):
        if ticks:
            at_step(h, lambda ticks=ticks: [tick() for tick in ticks])


def attend_kernel(
    lines, heads, weights, normed, shift, cos_ref, sin_ref, idc_ref, idr_ref, w_own,
    low_ref, mixed_ref, outf_ref, lse_ref, part_ref, w_full,
    bias, proj_in, wv, rows_in, loads, own_sem, zs, zr, xs, xr,
):
    at = Place(lines)
    h = pl.program_id(0)
    gather = Gather(at, w_own, w_full, columns_of(w_own.shape[1]), own_sem, zs, zr, xs, xr)
    local = rows_in.shape[0] // 2
    copies = [
        pltpu.make_async_copy(weights, wv, loads.at[0]),
        pltpu.make_async_copy(normed.at[0], rows_in.at[pl.ds(0, local)], loads.at[1]),
        pltpu.make_async_copy(normed.at[1], rows_in.at[pl.ds(local, local)], loads.at[2]),
    ]

    @pl.when(h == 0)
    def _():
        for copy in copies:
            copy.start()
        at.greet()
        gather.start()
        for copy in copies:
            copy.wait()
        columns = shift[...].T
        for j in range(3):
            proj_in[j] = dg(wv[j], rows_in[...], ((0,), (1,))) + columns[:, j : j + 1]

    fill_bias(bias, idc_ref, idr_ref)
    cosine, sine = cos_ref[...], sin_ref[...]
    mine = pl.ds(pl.multiple_of(h * HDIM, HDIM), HDIM)
    query = rope_rows(proj_in[0, mine], cosine, sine).astype(BF16)
    key_f = rope_rows(proj_in[1, mine], cosine, sine)
    value = proj_in[2, mine].astype(BF16)
    low_ref[0] = query
    low_ref[1] = key_f.astype(BF16)
    low_ref[2] = value
    key_nat = key_f.T.astype(BF16)
    length = query.shape[1]
    factor = SCALE * LOG2E
    for start in range(0, length, QB):
        cols = slice(start, start + QB)
        logits = dg(key_nat, query[:, cols], ((1,), (0,))) + bias[:, cols]
        peak = jnp.max(logits, axis=0, keepdims=True)
        probs = jnp.exp2((logits - peak) * factor)
        total = jnp.sum(probs, axis=0, keepdims=True)
        mixed = dg(value, probs.astype(BF16), ((1,), (0,))) * (1.0 / total)
        mixed_ref[mine, cols] = mixed.astype(BF16)
        outf_ref[:, cols] = mixed
        lse_ref[0, :, cols] = peak * factor + jnp.log2(total)

    ticks = [functools.partial(gather.tick, i) for i in range(len(gather.pieces))]
    run_ticks(spread(ticks, heads))

    @pl.when(h == heads - 1)
    def _():
        def body(i, carry):
            r = pl.ds(pl.multiple_of(i * TILE, TILE), TILE)
            part_ref[r] = dg(mixed_ref[:, r], wv[3], ((0,), (1,)), BF16)
            return carry

        lax.fori_loop(0, length // TILE, body, 0)
        gather.finish()
        gather.drain()


def attend(lines, weights, normed, shift, cosine, sine, ids, w_own):
    _, width, inner = weights.shape
    length = ids.shape[0]
    heads = inner // HDIM
    half = HDIM // 2
    head = lambda h: (0, h, 0)
    whole = lambda h: (0, 0)
    rows, quarter = w_own.shape
    anywhere = pl.BlockSpec(memory_space=pl.ANY)
    return pl.pallas_call(
        functools.partial(attend_kernel, lines, heads),
        grid=(heads,),
        in_specs=[
            anywhere,
            anywhere,
            pl.BlockSpec((8, inner), whole),
            pl.BlockSpec((half, length), whole),
            pl.BlockSpec((half, length), whole),
            pl.BlockSpec((length, 1), whole),
            pl.BlockSpec((1, length), whole),
            anywhere,
        ],
        out_specs=[
            pl.BlockSpec((3, HDIM, length), head),
            pl.BlockSpec((inner, length), whole),
            pl.BlockSpec((HDIM, length), lambda h: (h, 0)),
            pl.BlockSpec((1, 1, length), lambda h: (h, 0, 0)),
            pl.BlockSpec((length, width), whole),
            anywhere,
        ],
        out_shape=[
            jax.ShapeDtypeStruct((3, inner, length), BF16),
            jax.ShapeDtypeStruct((inner, length), BF16),
            jax.ShapeDtypeStruct((inner, length), F32),
            jax.ShapeDtypeStruct((heads, 1, length), F32),
            jax.ShapeDtypeStruct((length, width), BF16),
            jax.ShapeDtypeStruct((2 * lines * rows, quarter), BF16),
        ],
        scratch_shapes=[
            pltpu.VMEM((length, length), F32),
            pltpu.VMEM((3, inner, length), F32),
            pltpu.VMEM(weights.shape, BF16),
            pltpu.VMEM((length, width), BF16),
            pltpu.SemaphoreType.DMA((3,)),
        ]
        + gather_scratch(lines, quarter),
        compiler_params=pltpu.CompilerParams(
            collective_id=3, has_side_effects=True, vmem_limit_bytes=63 << 20
        ),
        cost_estimate=pl.CostEstimate(
            flops=4 * inner * length * length + 8 * inner * length * width,
            transcendentals=heads * length * length,
            bytes_accessed=26 * inner * length,
        ),
        name="attend",
    )(weights, normed, shift, cosine, sine, ids[:, None], ids[None, :], w_own)


def attend_back_kernel(
    lines, heads, low_ref, outf_ref, lse_ref, cos_ref, sin_ref, idc_ref, idr_ref,
    weights, normed, mixed, d_attn, w_grad, w_grad_two, other, base,
    one_ref, qkv_grad, proj_grad, shift_ref, w_out, out_full,
    bias, dq, dk, dv, d_mixed, d_proj, wv, rows_in, mixed_in, base_in, other_in, out_low, tile_buf, w_sum,
    loads, ys, yr, ks, ts, *share_refs
):
    at = Place(lines)
    h = pl.program_id(0)
    slices = [(w_grad,) + piece for piece in columns_of(w_grad.shape[1])]
    slices = [(w_grad_two,) + piece for piece in columns_of(w_grad.shape[1])[KEPT:]] + slices
    share = Share(at, slices, w_sum, *share_refs)
    length, width = rows_in.shape
    local = length // 2

    def load_rows(source):
        return [
            pltpu.make_async_copy(source.at[i], rows_in.at[pl.ds(i * local, local)], loads.at[i])
            for i in range(2)
        ]

    mixed_copy = pltpu.make_async_copy(mixed, mixed_in, loads.at[2])
    weight_copy = pltpu.make_async_copy(weights, wv, loads.at[3])
    base_copy = pltpu.make_async_copy(base, base_in, loads.at[4])
    chunk = local // 4
    chunks = [pl.ds(q * chunk, chunk) for q in range(4)]
    other_copies = [
        remote(other.at[r], other_in.at[r], ys.at[0, q], yr.at[0, q], at.peer) for q, r in enumerate(chunks)
    ]
    out_copies = [
        remote(out_low.at[r], out_full.at[at.y, r], ys.at[1, q], yr.at[1, q], at.peer)
        for q, r in enumerate(chunks)
    ]
    out_keeps = [
        pltpu.make_async_copy(out_low.at[r], out_full.at[at.y, r], ks.at[q]) for q, r in enumerate(chunks)
    ]

    @pl.when(h == 0)
    def _():
        for copy in load_rows(d_attn) + [mixed_copy, weight_copy, base_copy]:
            copy.start()
        at.greet()
        share.flow.start()
        for copy in other_copies:
            copy.start()
        for copy in load_rows(d_attn) + [mixed_copy, weight_copy]:
            copy.wait()
        d_mixed[...] = dg(wv[3], rows_in[...], ((0,), (1,)), BF16)

        def body(i, carry):
            cols = pl.ds(pl.multiple_of(i * TILE, TILE), TILE)
            proj_grad[cols] = dg(rows_in[:, cols], mixed_in[...], ((0,), (1,)), BF16)
            return carry

        lax.fori_loop(0, width // TILE, body, 0)
        for copy in load_rows(normed):
            copy.start()

    fill_bias(bias, idc_ref, idr_ref)
    cosine, sine = cos_ref[...], sin_ref[...]
    mine = pl.ds(pl.multiple_of(h * HDIM, HDIM), HDIM)
    query, key = low_ref[0], low_ref[1]
    grad = d_mixed[mine]
    grad_f = grad.astype(F32)
    delta = jnp.sum(grad_f * outf_ref[...], axis=0, keepdims=True)
    nat = lambda t: t.astype(F32).T.astype(BF16)
    query_nat, key_nat, value_nat, grad_nat = nat(query), nat(key), nat(low_ref[2]), nat(grad)
    lse = lse_ref[0]
    factor = SCALE * LOG2E
    for start in range(0, length, QB):
        cols = slice(start, start + QB)
        logits = dg(key_nat, query[:, cols], ((1,), (0,)))
        probs = jnp.exp2(logits * factor + bias[:, cols] - lse[:, cols])
        d_probs = dg(value_nat, grad[:, cols], ((1,), (0,)))
        d_logits = (probs * (d_probs - delta[:, cols])).astype(BF16)
        part_v = dg(probs.astype(BF16), grad_nat[cols], ((1,), (0,)))
        part_k = dg(d_logits, query_nat[cols], ((1,), (0,)))
        dq[:, cols] = dg(key, d_logits, ((1,), (0,)))
        if start == 0:
            dv[...] = part_v
            dk[...] = part_k
        else:
            dv[...] += part_v
            dk[...] += part_k
    d_proj[0, mine] = rope_rows_back(dq[...] * SCALE, cosine, sine).astype(BF16)
    d_proj[1, mine] = rope_rows_back(dk[...].T * SCALE, cosine, sine).astype(BF16)
    d_proj[2, mine] = dv[...].T.astype(BF16)

    def out_rows(q):
        r = chunks[q]
        if q == 0:
            base_copy.wait()
        other_copies[q].wait()
        out_low[r] = (base_in[r] + other_in[r].astype(F32)).astype(BF16)
        out_copies[q].start()
        out_keeps[q].start()

    for q, step in enumerate((0, 1, 3, 5)):
        at_step(step, functools.partial(out_rows, q))

    ticks = share.flow.ticks()
    early = min(len(ticks), heads // 2 + 1)
    for i in range(early):
        at_step(max(0, 2 * i - 1), ticks[i])
    ticks = ticks[early:]

    @pl.when(h == heads - 1)
    def _():
        for copy in load_rows(normed):
            copy.wait()
        one_rows = jnp.ones((8, length), BF16)

        def one_body(i, carry):
            r = pl.ds(pl.multiple_of(i * TILE, TILE), TILE)
            total = dg(d_proj[0, :, r], wv[0], ((0,), (1,)))
            for j in range(1, 3):
                total += dg(d_proj[j, :, r], wv[j], ((0,), (1,)))
            one_ref[r] = total.astype(BF16)
            return carry

        lax.fori_loop(0, length // TILE, one_body, 0)
        for tick in ticks[:1]:
            tick()
        count = width // TILE

        def copy_out(i):
            where = pl.ds(pl.multiple_of(lax.rem(i, count) * TILE, TILE), TILE)
            slot = lax.rem(i, 2)
            return pltpu.make_async_copy(tile_buf.at[slot], qkv_grad.at[i // count, where], ts.at[slot])

        def grad_body(i, carry):
            cols = pl.ds(pl.multiple_of(lax.rem(i, count) * TILE, TILE), TILE)

            @pl.when(i >= 2)
            def _():
                copy_out(i - 2).wait()

            tile_buf[lax.rem(i, 2)] = dg(rows_in[:, cols], d_proj[i // count], ((0,), (1,)), BF16)
            copy_out(i).start()
            return carry

        lax.fori_loop(0, 3 * count, grad_body, 0)
        for i in range(max(0, 3 * count - 2), 3 * count):
            copy_out(i).wait()
        for j in range(3):
            shift_ref[j] = dg(one_rows, d_proj[j], ((1,), (1,)))
        for tick in ticks[1:]:
            tick()
        share.drain()
        w_out[...] = w_sum[...]
        for q, r in enumerate(chunks):
            out_copies[q].wait_send()
            there = out_full.at[1 - at.y, r]
            remote(there, there, ys.at[1, q], yr.at[1, q], at.peer).wait_recv()
            out_keeps[q].wait()


def attend_back(lines, low, outf, lse, cosine, sine, ids, *arrays):
    weights, w_grad = arrays[0], arrays[4]
    _, inner, length = low.shape
    width = weights.shape[1]
    local = length // 2
    heads = inner // HDIM
    half = HDIM // 2
    w_rows, quarter = w_grad.shape
    rows = w_rows // (2 * lines)
    pieces = columns_of(quarter)[KEPT:] + columns_of(quarter)
    columns = sum(count for _, count in pieces)
    head = lambda h: (0, h, 0)
    whole = lambda h: (0, 0)
    cube = lambda h: (0, 0, 0)
    anywhere = pl.BlockSpec(memory_space=pl.ANY)
    dma = pltpu.SemaphoreType.DMA
    shape = jax.ShapeDtypeStruct
    return pl.pallas_call(
        functools.partial(attend_back_kernel, lines, heads),
        grid=(heads,),
        in_specs=[
            pl.BlockSpec((3, HDIM, length), head),
            pl.BlockSpec((HDIM, length), lambda h: (h, 0)),
            pl.BlockSpec((1, 1, length), lambda h: (h, 0, 0)),
            pl.BlockSpec((half, length), whole),
            pl.BlockSpec((half, length), whole),
            pl.BlockSpec((length, 1), whole),
            pl.BlockSpec((1, length), whole),
        ]
        + [anywhere] * 8,
        out_specs=[
            pl.BlockSpec((length, width), whole),
            anywhere,
            pl.BlockSpec((width, inner), whole),
            pl.BlockSpec((3, 8, inner), cube),
            pl.BlockSpec((2, rows, columns), cube),
            anywhere,
        ],
        out_shape=[
            shape((length, width), BF16),
            shape((3, width, inner), BF16),
            shape((width, inner), BF16),
            shape((3, 8, inner), F32),
            shape((2, rows, columns), F32),
            shape((2, local, width), BF16),
        ],
        scratch_shapes=[
            pltpu.VMEM((length, length), F32),
            pltpu.VMEM((HDIM, length), F32),
            pltpu.VMEM((length, HDIM), F32),
            pltpu.VMEM((length, HDIM), F32),
            pltpu.VMEM((inner, length), BF16),
            pltpu.VMEM((3, inner, length), BF16),
            pltpu.VMEM(weights.shape, BF16),
            pltpu.VMEM((length, width), BF16),
            pltpu.VMEM((inner, length), BF16),
            pltpu.VMEM((local, width), F32),
            pltpu.VMEM((local, width), BF16),
            pltpu.VMEM((local, width), BF16),
            pltpu.VMEM((2, TILE, inner), BF16),
            pltpu.VMEM((2, rows, columns), F32),
            dma((5,)), dma((2, 4)), dma((2, 4)), dma((4,)), dma((2,)),
        ]
        + share_scratch(lines, rows, pieces),
        compiler_params=pltpu.CompilerParams(
            collective_id=4, has_side_effects=True, vmem_limit_bytes=63 << 20
        ),
        cost_estimate=pl.CostEstimate(
            flops=10 * inner * length * length + 20 * inner * length * width,
            transcendentals=heads * length * length,
            bytes_accessed=18 * inner * length,
        ),
        name="attend_back",
    )(low, outf, lse, cosine, sine, ids[:, None], ids[None, :], *arrays)


def rope_tables(patch_row, patch_col):
    quarter = HDIM // 4
    frequency = ROPE_BASE ** (-2.0 * jnp.arange(quarter, dtype=F32) / (HDIM // 2))
    angles = jnp.concatenate(
        [
            frequency[:, None] * patch_row.astype(F32)[None, :],
            frequency[:, None] * patch_col.astype(F32)[None, :],
        ],
        axis=0,
    )
    return jnp.cos(angles), jnp.sin(angles)


MESH = pl.DeviceIdType.MESH


def remote(src, dst, send_sem, recv_sem, device):
    return pltpu.make_async_remote_copy(
        src_ref=src,
        dst_ref=dst,
        send_sem=send_sem,
        recv_sem=recv_sem,
        device_id=device,
        device_id_type=MESH,
    )


class Place:
    def __init__(self, lines):
        self.lines = lines
        self.s = lax.axis_index("shard")
        self.c = lax.axis_index("ctx")
        self.y = lax.axis_index("tp")
        self.line = self.s // 2
        self.side = lax.rem(self.s, 2)
        self.sib = (self.s, 1 - self.c, self.y)
        self.peer = (self.s, self.c, 1 - self.y)
        self.beside = (self.line * 2 + 1 - self.side, self.c, self.y)

    def ahead(self, k):
        return (lax.rem(self.line + k, self.lines) * 2 + self.side, self.c, self.y)

    def source(self, k):
        return lax.rem(self.line + self.lines - k, self.lines) * 2

    def greet(self):
        barrier = pltpu.get_barrier_semaphore()
        others = [self.sib, self.peer, self.beside] + [self.ahead(k) for k in range(1, self.lines)]
        for other in others:
            pl.semaphore_signal(barrier, inc=1, device_id=other, device_id_type=MESH)
        pl.semaphore_wait(barrier, len(others))


def norm_rows(values):
    center = values - jnp.mean(values, -1, keepdims=True)
    spread = jnp.mean(center * center, -1, keepdims=True)
    return center * lax.rsqrt(spread + NORM_EPS)


def collect_kernel(
    lines, pieces, block, tok, gain, shift, dy, qb,
    out, normed, dy_sib, qb_out,
    norm_buf, own_sem, zs, zr, xs, xr, ys, yr, ms, mr,
):
    at = Place(lines)
    diag = at.c == at.y

    def part(p, s):
        j, first, count, _ = pieces[p]
        rows = block.shape[1]
        return out.at[j, pl.ds(pl.multiple_of(s * rows, rows), rows), pl.ds(first, count)]

    def own(p):
        j, first, count, _ = pieces[p]
        return block.at[j, :, pl.ds(first, count)]

    def z_copy(p, k, src):
        return remote(src, part(p, at.s), zs.at[p, k], zr.at[p, k], at.ahead(k))

    def x_copy(p, k, src):
        return remote(src, part(p, at.source(k) + at.side), xs.at[p, k], xr.at[p, k], at.beside)

    def y_copy(p, i, src, s):
        return remote(src, part(p, s), ys.at[p, i], yr.at[p, i], at.peer)

    def near(k):
        return at.source(k) + at.side

    def far(k):
        return at.source(k) + 1 - at.side

    def z_wait(p, k):
        z_copy(p, k, part(p, near(k))).wait_recv()

    def x_wait(p, k):
        x_copy(p, k, part(p, far(k))).wait_recv()

    def y_wait(p, i, s):
        y_copy(p, i, part(p, s), s).wait_recv()

    late = [p for p in range(len(pieces)) if pieces[p][3]]
    early = [p for p in range(len(pieces)) if not pieces[p][3]]
    order = late + early
    at.greet()

    own_rows = pl.ds(pl.multiple_of(at.s * block.shape[1], block.shape[1]), block.shape[1])
    own_copy = pltpu.make_async_copy(block, out.at[:, own_rows], own_sem.at[0])
    bias_copy = pltpu.make_async_copy(qb, qb_out, own_sem.at[1])

    @pl.when(diag)
    def _():
        own_copy.start()
        bias_copy.start()
        remote(qb, qb_out, ms.at[0], mr.at[0], at.peer).start()
        for p in early:
            y_copy(p, 0, own(p), at.s).start()
        for p in order[:LEAD]:
            for k in range(1, lines):
                z_copy(p, k, own(p)).start()

    dy_copy = remote(dy, dy_sib, ms.at[1], mr.at[1], at.sib)
    dy_copy.start()
    norm_buf[...] = (norm_rows(tok[...].astype(F32)) * gain[...] + shift[...]).astype(BF16)
    norm_copy = remote(norm_buf, normed.at[at.c], ms.at[2], mr.at[2], at.sib)
    norm_copy.start()
    norm_keep = pltpu.make_async_copy(norm_buf, normed.at[at.c], own_sem.at[2])
    norm_keep.start()

    @pl.when(diag)
    def _():
        for step in range(len(order) + 1):
            if step < len(order):
                p = order[step]
                if step + LEAD < len(order):
                    for k in range(1, lines):
                        z_copy(order[step + LEAD], k, own(order[step + LEAD])).start()
                x_copy(p, 0, own(p)).start()
                if p in late:
                    y_copy(p, 0, own(p), at.s).start()
                for k in range(1, lines):
                    z_wait(p, k)
                    x_copy(p, k, part(p, near(k))).start()
                    if p in late:
                        y_copy(p, k, part(p, near(k)), near(k)).start()
            if step > 0:
                p = order[step - 1]
                for k in range(lines):
                    x_wait(p, k)
                    if p in late:
                        y_copy(p, lines + k, part(p, far(k)), far(k)).start()
        own_copy.wait()
        bias_copy.wait()
        remote(qb, qb_out, ms.at[0], mr.at[0], at.peer).wait_send()
        for p in order:
            for k in range(1, lines):
                z_copy(p, k, own(p)).wait_send()
            for k in range(lines):
                x_copy(p, k, part(p, near(k))).wait_send()
            y_copy(p, 0, own(p), at.s).wait_send()
            if p in late:
                for k in range(1, lines):
                    y_copy(p, k, part(p, near(k)), near(k)).wait_send()
                for k in range(lines):
                    y_copy(p, lines + k, part(p, far(k)), far(k)).wait_send()

    @pl.when(jnp.logical_not(diag))
    def _():
        for p in early:
            y_wait(p, 0, at.s)
            for k in range(1, lines):
                z_copy(p, k, part(p, at.s)).start()
            x_copy(p, 0, part(p, at.s)).start()
        for step in range(len(early) + 1):
            if step < len(early):
                p = early[step]
                for k in range(1, lines):
                    z_wait(p, k)
                    x_copy(p, k, part(p, near(k))).start()
            if step > 0:
                for k in range(lines):
                    x_wait(early[step - 1], k)
        for p in early:
            for k in range(1, lines):
                z_copy(p, k, part(p, at.s)).wait_send()
            for k in range(lines):
                x_copy(p, k, part(p, near(k))).wait_send()
        remote(qb, qb_out, ms.at[0], mr.at[0], at.peer).wait_recv()
        for p in late:
            for k in range(lines):
                y_wait(p, k, near(k))
                y_wait(p, lines + k, far(k))

    dy_copy.wait()
    norm_copy.wait_send()
    remote(norm_buf, normed.at[1 - at.c], ms.at[2], mr.at[2], at.sib).wait_recv()
    norm_keep.wait()


def collect(lines, block, tok, gain, shift, dy, qb):
    groups, rows, inner = block.shape
    local, width = tok.shape
    cut = (inner * 3 // 5) // 128 * 128
    pieces = [(j, f, n, i < 5) for i, (j, f, n) in enumerate((j, f, n) for j in range(4) for f, n in ((0, cut), (cut, inner - cut)))]
    n = len(pieces)
    anywhere = pl.BlockSpec(memory_space=pl.ANY)
    vmem = pl.BlockSpec(memory_space=pltpu.VMEM)
    dma = pltpu.SemaphoreType.DMA
    return pl.pallas_call(
        functools.partial(collect_kernel, lines, pieces),
        in_specs=[anywhere, vmem, vmem, vmem, anywhere, anywhere],
        out_specs=[anywhere] * 4,
        out_shape=[
            jax.ShapeDtypeStruct((groups, 2 * lines * rows, inner), BF16),
            jax.ShapeDtypeStruct((2, local, width), BF16),
            jax.ShapeDtypeStruct(dy.shape, BF16),
            jax.ShapeDtypeStruct(qb.shape, F32),
        ],
        scratch_shapes=[
            pltpu.VMEM((local, width), BF16),
            dma((3,)),
            dma((n, lines)),
            dma((n, lines)),
            dma((n, lines)),
            dma((n, lines)),
            dma((n, 2 * lines)),
            dma((n, 2 * lines)),
            dma((3,)),
            dma((3,)),
        ],
        compiler_params=pltpu.CompilerParams(
            collective_id=0, has_side_effects=True, vmem_limit_bytes=63 << 20
        ),
        name="collect",
    )(block, tok, gain[None], shift[None], dy, qb)


class Gather:
    def __init__(self, at, own, full, pieces, own_sem, zs, zr, xs, xr):
        self.at, self.own, self.full, self.pieces = at, own, full, pieces
        self.own_sem, self.zs, self.zr, self.xs, self.xr = own_sem, zs, zr, xs, xr
        self.rows = own.shape[0]

    def part(self, p, s):
        start, count = self.pieces[p]
        return self.full.at[pl.ds(pl.multiple_of(s * self.rows, self.rows), self.rows), pl.ds(start, count)]

    def z_copy(self, p, k):
        start, count = self.pieces[p]
        src = self.own.at[:, pl.ds(start, count)]
        return remote(src, self.part(p, self.at.s), self.zs.at[p, k], self.zr.at[p, k], self.at.ahead(k))

    def x_copy(self, p, k):
        start, count = self.pieces[p]
        there = self.part(p, self.at.source(k) + self.at.side)
        src = self.own.at[:, pl.ds(start, count)] if k == 0 else there
        return remote(src, there, self.xs.at[p, k], self.xr.at[p, k], self.at.beside)

    def z_wait(self, p, k):
        there = self.part(p, self.at.source(k) + self.at.side)
        remote(there, there, self.zs.at[p, k], self.zr.at[p, k], self.at.ahead(k)).wait_recv()

    def x_wait(self, p, k):
        there = self.part(p, self.at.source(k) + 1 - self.at.side)
        remote(there, there, self.xs.at[p, k], self.xr.at[p, k], self.at.beside).wait_recv()

    def keep(self):
        there = self.full.at[pl.ds(pl.multiple_of(self.at.s * self.rows, self.rows), self.rows)]
        return pltpu.make_async_copy(self.own, there, self.own_sem)

    def begin(self, p):
        if p < len(self.pieces):
            for k in range(1, self.at.lines):
                self.z_copy(p, k).start()

    def start(self):
        self.keep().start()
        for p in range(AHEAD):
            self.begin(p)
        for p in range(len(self.pieces)):
            self.x_copy(p, 0).start()

    def tick(self, p):
        self.begin(p + AHEAD)
        for k in range(1, self.at.lines):
            self.z_wait(p, k)
            self.x_copy(p, k).start()

    def finish(self):
        for p in range(len(self.pieces)):
            for k in range(self.at.lines):
                self.x_wait(p, k)
        self.keep().wait()

    def drain(self):
        for p in range(len(self.pieces)):
            for k in range(self.at.lines):
                self.x_copy(p, k).wait_send()
                if k > 0:
                    self.z_copy(p, k).wait_send()


class Scatter:
    def __init__(self, at, block, mine, xbuf, zin, xs, xr, zs, zr, load=None):
        self.at, self.block, self.mine, self.xbuf, self.zin = at, block, mine, xbuf, zin
        self.xs, self.xr, self.zs, self.zr, self.load = xs, xr, zs, zr, load

    def x_copy(self, row):
        src = self.block(row, 1 - self.at.side)
        return remote(src, self.xbuf.at[row], self.xs.at[row], self.xr.at[row], self.at.beside)

    def load_copy(self, row):
        return pltpu.make_async_copy(self.block(row, self.at.side), self.mine.at[row], self.load.at[row])

    def z_copy(self, k):
        row = lax.rem(self.at.line + k, self.at.lines)
        return remote(self.mine.at[row], self.zin.at[k], self.zs.at[k], self.zr.at[k], self.at.ahead(k))

    def start(self):
        for row in range(self.at.lines):
            self.x_copy(row).start()
            if self.load is not None:
                self.load_copy(row).start()

    def middle(self):
        for row in range(self.at.lines):
            self.x_copy(row).wait_recv()
            if self.load is not None:
                self.load_copy(row).wait()
                here = self.mine[row]
            else:
                here = self.block(row, self.at.side)[...]
            self.mine[row] = (here.astype(F32) + self.xbuf[row].astype(F32)).astype(BF16)
        for k in range(1, self.at.lines):
            self.z_copy(k).start()

    def finish(self):
        total = self.mine[self.at.line].astype(F32)
        for k in range(1, self.at.lines):
            self.z_copy(k).wait_recv()
            total += self.zin[k].astype(F32)
        return total

    def drain(self):
        for row in range(self.at.lines):
            self.x_copy(row).wait_send()
        for k in range(1, self.at.lines):
            self.z_copy(k).wait_send()


class Flow:
    def __init__(self, units, begin, done, lag=1):
        self.units, self.begin, self.done, self.lag = units, begin, done, lag

    def start(self):
        for i in range(min(AHEAD, len(self.units))):
            self.begin(i)

    def tick(self, i):
        count = len(self.units)
        if i < count:
            self.units[i].middle()
            if i + AHEAD < count:
                self.begin(i + AHEAD)
        if 0 <= i - self.lag < count:
            self.done(i - self.lag, self.units[i - self.lag].finish())

    def ticks(self):
        return [functools.partial(self.tick, i) for i in range(len(self.units) + self.lag)]


class Share:
    def __init__(self, at, slices, out, mine, xbuf, zin, xs, xr, zs, zr, load, cs, cr):
        rows = out.shape[1]
        self.at, self.out, self.cs, self.cr = at, out, cs, cr
        self.places, units, total = [], [], 0
        for i, (grad, start, count) in enumerate(slices):

            def block(line, side, grad=grad, start=start, count=count):
                first = pl.multiple_of((2 * line + side) * rows, rows)
                return grad.at[pl.ds(first, rows), pl.ds(start, count)]

            cut = lambda ref: ref.at[:, :, pl.ds(total, count)]
            units.append(
                Scatter(
                    at, block, cut(mine), cut(xbuf), cut(zin), xs.at[i], xr.at[i], zs.at[i], zr.at[i], load.at[i]
                )
            )
            self.places.append((total, count))
            total += count
        self.flow = Flow(units, lambda i: units[i].start(), self.done, lag=2)

    def share(self, i, core):
        start, count = self.places[i]
        here = self.out.at[core, :, pl.ds(start, count)]
        return remote(here, here, self.cs.at[i], self.cr.at[i], self.at.sib)

    def done(self, i, total):
        start, count = self.places[i]
        self.out[self.at.c, :, start : start + count] = total
        self.share(i, self.at.c).start()

    def drain(self):
        for i, unit in enumerate(self.flow.units):
            unit.drain()
            self.share(i, self.at.c).wait_send()
            self.share(i, 1 - self.at.c).wait_recv()


def columns_of(quarter):
    return [(start, 256) for start in range(0, quarter, 256)]


def share_scratch(lines, rows, pieces):
    n = len(pieces)
    dma = pltpu.SemaphoreType.DMA
    slab = pltpu.VMEM((lines, rows, sum(count for _, count in pieces)), BF16)
    return [slab] * 3 + [dma((n, lines))] * 5 + [dma((n,))] * 2


def gather_scratch(lines, quarter):
    n = len(columns_of(quarter))
    dma = pltpu.SemaphoreType.DMA
    return [dma] + [dma((n, lines))] * 4


def settle_kernel(
    lines, pieces, qkv, proj, d_one, d_hid, tok, gain, vec,
    attn_out, grad_full, vec_out,
    grad_own, here, mine, ax, ai, ay, al, one_in, vown, vbuf, vin,
    hs, axs, axr, azs, azr, ays, ayr, cs, cr, vs, vr, os, orr, ms, mr, ks,
):
    at = Place(lines)
    diag = at.c == at.y
    first = [p for p in range(len(pieces)) if pieces[p][3]]
    last = [p for p in range(len(pieces)) if not pieces[p][3]]

    def cut(ref, p):
        _, start, count, _ = pieces[p]
        return ref.at[..., pl.ds(start, count)]

    def source(p):
        j = pieces[p][0]
        return cut(proj if j == 3 else qkv.at[j], p)

    def local_part(p):
        return cut(here.at[pieces[p][0]], p)

    class Direct(Scatter):
        def __init__(self, p):
            j = pieces[p][0]
            super().__init__(
                at, lambda line, side: local_part(p).at[line, side],
                cut(mine.at[j], p), cut(ax.at[j], p), cut(ai.at[j], p),
                axs.at[p], axr.at[p], azs.at[p], azr.at[p],
            )
            self.p = p

        def x_copy(self, row):
            src = source(self.p).at[row, 1 - at.side]
            return remote(src, self.xbuf.at[row], self.xs.at[row], self.xr.at[row], at.beside)

    def summed(p):
        j = pieces[p][0]
        return Scatter(
            at, lambda line, side: cut(ay.at[j, line, side], p),
            cut(mine.at[j], p), cut(ax.at[j], p), cut(ai.at[j], p),
            axs.at[p], axr.at[p], azs.at[p], azr.at[p],
        )

    def pair_copy(p, half):
        side = (1 - at.side, at.side)[half]
        there = cut(ay.at[pieces[p][0], :, side], p)
        return remote(source(p).at[:, side], there, ays.at[p, half], ayr.at[p, half], at.peer)

    def last_copy(p):
        j = pieces[p][0]
        return remote(cut(al.at[j, 0], p), cut(al.at[j, 1], p), ays.at[p, 0], ayr.at[p, 0], at.peer)

    def attn_share(p):
        there = cut(attn_out.at[pieces[p][0]], p)
        return remote(there, there, cs.at[p], cr.at[p], at.sib)

    order = last + first
    diag_units = [Direct(p) for p in last] + [summed(p) for p in first]
    off_units = [Direct(p) for p in last]

    def diag_begin(i):
        p = order[i]
        if p in first:
            j, start, count, _ = pieces[p]
            for half in range(2):
                pair_copy(p, half).wait_recv()
            for row in range(lines):
                for side in range(2):
                    both = local_part(p)[row, side].astype(F32) + cut(ay.at[j, row, side], p)[...].astype(F32)
                    ay[j, row, side, :, start : start + count] = both.astype(BF16)
        diag_units[i].start()

    def diag_done(i, total):
        p = order[i]
        j, start, count, _ = pieces[p]
        attn_out[j, :, start : start + count] = total
        if p in first:
            attn_share(p).start()

    def off_done(i, total):
        j, start, count, _ = pieces[last[i]]
        al[j, 0, :, start : start + count] = total.astype(BF16)
        last_copy(last[i]).start()

    diag_flow = Flow(diag_units, diag_begin, diag_done)
    off_flow = Flow(off_units, lambda i: off_units[i].start(), off_done)

    def ticks(begin, end):
        @pl.when(diag)
        def _():
            for i in range(begin, end):
                diag_flow.tick(i)

        @pl.when(jnp.logical_not(diag))
        def _():
            for i in range(begin, end):
                off_flow.tick(i)

    loads = [
        pltpu.make_async_copy(qkv, here.at[pl.ds(0, 3)], hs.at[0]),
        pltpu.make_async_copy(proj, here.at[3], hs.at[1]),
    ]
    for load in loads:
        load.start()
    at.greet()
    one_copy = remote(d_one.at[1 - at.c], one_in, os, orr, at.sib)
    one_copy.start()

    @pl.when(diag)
    def _():
        for i in range(min(AHEAD, len(last))):
            diag_units[i].start()

    @pl.when(jnp.logical_not(diag))
    def _():
        for p in first:
            for half in range(2):
                pair_copy(p, half).start()
        off_flow.start()

    one_copy.wait_recv()
    local = tok.shape[0]
    tile = TILE // 2
    grad_copies, grad_keeps = [], []
    sums = [jnp.zeros((1, tok.shape[1]), F32) for _ in range(2)]
    for q in range(local // tile):
        r = pl.ds(q * tile, tile)
        value = tok[r].astype(F32)
        center = value - jnp.mean(value, -1, keepdims=True)
        inverse = lax.rsqrt(jnp.mean(center * center, -1, keepdims=True) + NORM_EPS)
        normal = center * inverse
        grad = d_one[at.c, r].astype(F32) + one_in[r].astype(F32)
        grad_own[r] = (d_hid[r] + norm_back(grad, normal, inverse, gain[...])).astype(BF16)
        copy = remote(grad_own.at[r], grad_full.at[at.y, r], ms.at[q], mr.at[q], at.peer)
        keep = pltpu.make_async_copy(grad_own.at[r], grad_full.at[at.y, r], ks.at[q])
        keep.start()
        grad_keeps.append(keep)
        grad_copies.append(copy)
        for i, t in enumerate((grad * normal, grad)):
            sums[i] += jnp.sum(t, axis=0, keepdims=True)
    vown[...] = vec[...]
    for i in range(2):
        vown[i : i + 1] = sums[i]

    def small_copy(stage, device):
        src = vown if stage == 0 else vbuf.at[stage - 1]
        return remote(src, vin.at[stage], vs.at[stage], vr.at[stage], device)

    steps = [at.sib, at.peer, at.beside]

    def small_start(stage):
        small_copy(stage, steps[stage]).start()

    def small_add(stage):
        small_copy(stage, steps[stage]).wait_recv()
        before = vown[...] if stage == 0 else vbuf[stage - 1]
        vbuf[stage] = before + vin[stage]

    def line_copy(k):
        return remote(vbuf.at[2], vin.at[3 + at.line], vs.at[2 + k], vr.at[2 + k], at.ahead(k))

    def line_wait(k):
        there = vin.at[3 + at.source(k) // 2]
        remote(vbuf.at[2], there, vs.at[2 + k], vr.at[2 + k], at.ahead(k)).wait_recv()

    small_start(0)
    for load in loads:
        load.wait()
    total_ticks = len(order) + 1
    small_add(0)
    small_start(1)
    for i in range(total_ticks):
        ticks(i, i + 1)
        if i >= 1 and grad_copies[i - 1 : i]:
            grad_copies[i - 1].start()
        if i == total_ticks // 2:
            small_add(1)
            small_start(2)
        if i == total_ticks - 2:
            small_add(2)
            for k in range(1, lines):
                line_copy(k).start()
            vin[3 + at.line] = vbuf[2]

    @pl.when(diag)
    def _():
        for p in last:
            j, start, count, _ = pieces[p]
            last_copy(p).wait_recv()
            attn_out[j, :, start : start + count] += cut(al.at[j, 1], p)[...].astype(F32)
            attn_share(p).start()

    for k in range(1, lines):
        line_wait(k)
    total = vin[3]
    for row in range(1, lines):
        total = total + vin[3 + row]
    vec_out[...] = total

    @pl.when(diag)
    def _():
        for unit in diag_units:
            unit.drain()
        for p in order:
            attn_share(p).wait_send()

    @pl.when(jnp.logical_not(diag))
    def _():
        for unit in off_units:
            unit.drain()
        for p in last:
            last_copy(p).wait_send()
        for p in first:
            for half in range(2):
                pair_copy(p, half).wait_send()
        for p in order:
            attn_share(p).wait_recv()

    for stage in range(3):
        small_copy(stage, steps[stage]).wait_send()
    for k in range(1, lines):
        line_copy(k).wait_send()
    one_copy.wait_send()
    for q, copy in enumerate(grad_copies):
        copy.wait_send()
        there = grad_full.at[1 - at.y, pl.ds(q * tile, tile)]
        remote(there, there, ms.at[q], mr.at[q], at.peer).wait_recv()
        grad_keeps[q].wait()


def settle(lines, qkv, proj, d_one, d_hid, tok, gain, vec):
    _, _, _, rows, inner = qkv.shape
    local, width = tok.shape
    pieces = settle_pieces(inner)
    n = len(pieces)
    tiles = local // TILE * 2
    anywhere = pl.BlockSpec(memory_space=pl.ANY)
    vmem = pl.BlockSpec(memory_space=pltpu.VMEM)
    dma = pltpu.SemaphoreType.DMA
    stage = (4, lines, rows, inner)
    return pl.pallas_call(
        functools.partial(settle_kernel, lines, pieces),
        in_specs=[anywhere] * 2 + [vmem] * 5,
        out_specs=[vmem, anywhere, vmem],
        out_shape=[
            jax.ShapeDtypeStruct((4, rows, inner), F32),
            jax.ShapeDtypeStruct((2, local, width), BF16),
            jax.ShapeDtypeStruct(vec.shape, F32),
        ],
        scratch_shapes=[
            pltpu.VMEM((local, width), BF16),
            pltpu.VMEM((4, lines, 2, rows, inner), BF16),
            pltpu.VMEM(stage, BF16),
            pltpu.VMEM(stage, BF16),
            pltpu.VMEM(stage, BF16),
            pltpu.VMEM((4, lines, 2, rows, inner), BF16),
            pltpu.VMEM((4, 2, rows, inner), BF16),
            pltpu.VMEM((local, width), BF16),
            pltpu.VMEM(vec.shape, F32),
            pltpu.VMEM((3,) + vec.shape, F32),
            pltpu.VMEM((3 + lines,) + vec.shape, F32),
            dma((2,)),
            dma((n, lines)), dma((n, lines)), dma((n, lines)), dma((n, lines)), dma((n, 2)), dma((n, 2)),
            dma((n,)), dma((n,)), dma((2 + lines,)), dma((2 + lines,)),
            dma, dma, dma((tiles,)), dma((tiles,)), dma((tiles,)),
        ],
        compiler_params=pltpu.CompilerParams(
            collective_id=1, has_side_effects=True, vmem_limit_bytes=63 << 20
        ),
        name="settle",
    )(qkv, proj, d_one, d_hid, tok, gain[None], vec)


def settle_pieces(inner):
    cuts = [(f, min(SLICE, inner - f)) for f in range(0, inner, SLICE)]
    every = [(j, f, n) for j in (3, 0, 1, 2) for f, n in cuts]
    return [(j, f, n, i >= len(every) - FIRST) for i, (j, f, n) in enumerate(every)]


def feed_kernel(
    lines, part, tok, params, w1_in, w2_own, dy_in, dy_sib,
    d_attn, d_hid, base, mlp_other, g1, g2, g2_out, vec,
    w1, w2, two, dy, act, dpre, hid, sbuf, rbuf, mbuf, ybuf, yin, acc, grad_tile, wide_tile,
    loads, ps, pr, ns, nr, ss, sr, ts, tr, ys, yr, os, dos, dor, gs, outs, keeps,
    own_sem, zs, zr, xs, xr, *share_refs,
):
    at = Place(lines)
    proj_bias, gain, shift, b1, b2 = [params.at[pl.ds(i, 1)] for i in range(5)]
    c, y = at.c, at.y
    local = hid.shape[0]
    tiles = local // TILE
    pieces = columns_of(w1.shape[1])
    gather = Gather(at, w2_own, w2, pieces, own_sem, zs, zr, xs, xr)
    share = Share(at, [(g2,) + piece for piece in pieces[:KEPT]], g2_out, *share_refs)
    gather_ticks = [functools.partial(gather.tick, i) for i in range(len(pieces))]
    share_ticks = share.flow.ticks()

    def advance(ticks, count=1):
        for _ in range(count):
            if ticks:
                ticks.pop(0)()

    def rows(g, q):
        return pl.ds((g * tiles + q) * TILE, TILE)

    def group(g):
        return pl.ds(g * local, local)

    def near_rows(q):
        return pl.ds(q * TILE, TILE)

    copies = [
        pltpu.make_async_copy(tok, ybuf, loads.at[0]),
        pltpu.make_async_copy(part.at[c], yin, loads.at[1]),
        pltpu.make_async_copy(w1_in, w1, loads.at[2]),
        pltpu.make_async_copy(dy_in.at[y], dy.at[group(0)], loads.at[3]),
        pltpu.make_async_copy(dy_sib.at[y], dy.at[group(1)], loads.at[4]),
        pltpu.make_async_copy(dy_in.at[1 - y], dy.at[group(2)], loads.at[5]),
        pltpu.make_async_copy(dy_sib.at[1 - y], dy.at[group(3)], loads.at[6]),
    ]
    for copy in copies:
        copy.start()
    at.greet()
    part_copy = remote(part.at[1 - c], rbuf.at[0], ps, pr, at.sib)
    part_copy.start()
    gather.start()

    def two_sib(q):
        return remote(two.at[rows(0, q)], two.at[rows(1, q)], ns.at[0, q], nr.at[0, q], at.sib)

    def two_peer(q):
        return remote(two.at[rows(0, q)], two.at[rows(2, q)], ns.at[1, q], nr.at[1, q], at.peer)

    def two_pass(q):
        return remote(two.at[rows(2, q)], two.at[rows(3, q)], ns.at[2, q], nr.at[2, q], at.sib)

    copies[0].wait()
    copies[1].wait()
    part_copy.wait_recv()
    for q in range(tiles):
        r = near_rows(q)
        value = ybuf[r].astype(F32) + yin[r].astype(F32) + rbuf[0, r].astype(F32) + proj_bias[...]
        hid[r] = value
        two[rows(0, q)] = (norm_rows(value) * gain[...] + shift[...]).astype(BF16)
        two_peer(q).start()
        two_sib(q).start()

    def first_layer(start, count):
        def body(i, carry):
            r = pl.ds(pl.multiple_of((start + i) * TILE, TILE), TILE)
            pre = dg(two[r], w1[...], ((1,), (0,))) + b1[...]
            sig = jax.nn.sigmoid(GELU * pre)
            act[r] = (pre * sig).astype(BF16)
            dpre[r] = (sig + GELU * pre * sig * (1.0 - sig)).astype(BF16)
            return carry

        lax.fori_loop(0, count, body, 0)

    copies[2].wait()
    first_layer(0, tiles)
    advance(gather_ticks)
    for q in range(tiles):
        two_sib(q).wait_recv()
    first_layer(tiles, tiles)
    advance(gather_ticks)
    for q in range(tiles):
        two_peer(q).wait_recv()
        two_pass(q).start()
        first_layer(2 * tiles + q, 1)
        advance(gather_ticks)
    for q in range(tiles):
        two_pass(q).wait_recv()
    first_layer(3 * tiles, tiles)
    for copy in copies[3:]:
        copy.wait()

    def weight_grad(left, right, out):
        count = out.shape[0] // TILE

        def copy(i):
            slot = lax.rem(i, 2)
            where = pl.ds(pl.multiple_of(i * TILE, TILE), TILE)
            return pltpu.make_async_copy(grad_tile.at[slot], out.at[where], gs.at[slot])

        def body(i, carry):
            cols = pl.ds(pl.multiple_of(i * TILE, TILE), TILE)

            @pl.when(i >= 2)
            def _():
                copy(i - 2).wait()

            grad_tile[lax.rem(i, 2)] = dg(left[:, cols], right[...], ((0,), (0,))).astype(BF16)
            copy(i).start()
            return carry

        lax.fori_loop(0, count, body, 0)
        for i in range(max(0, count - 2), count):
            copy(i).wait()

    advance(gather_ticks, len(gather_ticks))
    weight_grad(dy, act, g2)
    gather.finish()
    share.flow.start()

    shift_sum = jnp.zeros((1, b1.shape[1]), F32)

    def to_norm(g, q):
        r = rows(g, q)
        low = (dg(dy[r], w2[...], ((1,), (0,))) * dpre[r].astype(F32)).astype(BF16)
        dpre[r] = low
        return dg(low, w1[...], ((1,), (1,))), jnp.sum(low.astype(F32), axis=0, keepdims=True)

    def swap(kind, q):
        r = near_rows(q)
        return remote(sbuf.at[kind, r], rbuf.at[kind, r], ss.at[kind, q], sr.at[kind, q], at.sib)

    def y_copy(q):
        r = near_rows(q)
        return remote(ybuf.at[r], yin.at[r], ys.at[q], yr.at[q], at.peer)

    for kind in range(2):
        for q in range(tiles):
            r = near_rows(q)
            value, total = to_norm(3 - 2 * kind, q)
            sbuf[kind, r] = value.astype(BF16)
            shift_sum += total
            swap(kind, q).start()
            value, total = to_norm(2 - 2 * kind, q)
            shift_sum += total
            swap(kind, q).wait_recv()
            value += rbuf[kind, r].astype(F32)
            if kind == 0:
                ybuf[r] = value.astype(BF16)
                y_copy(q).start()
            else:
                acc[r] = value
                advance(share_ticks)

    weight_grad(two, dpre, g1)
    advance(share_ticks)

    def swap_out(kind, q):
        r = near_rows(q)
        return remote(sbuf.at[kind, r], mbuf.at[kind, r], ts.at[kind, q], tr.at[kind, q], at.sib)

    def other_out(q):
        r = near_rows(q)
        return pltpu.make_async_copy(mbuf.at[0, r], mlp_other.at[r], outs.at[q])

    def base_out(q):
        return pltpu.make_async_copy(wide_tile.at[q % 2], base.at[near_rows(q)], keeps.at[q])

    for kind in range(2):
        for q in range(tiles):
            r = near_rows(q)
            swap(kind, q).wait_send()
            sbuf[kind, r] = dg(act[rows(3 - 2 * kind, q)], w2[...], ((1,), (1,)), BF16)
            swap_out(kind, q).start()
            value = dg(act[rows(2 - 2 * kind, q)], w2[...], ((1,), (1,)))
            swap_out(kind, q).wait_recv()
            value += mbuf[kind, r].astype(F32)
            if kind == 0:
                mbuf[0, r] = value.astype(BF16)
                other_out(q).start()
            else:
                if q >= 2:
                    base_out(q - 2).wait()
                wide_tile[q % 2] = hid[r] + value + b2[...]
                base_out(q).start()
        advance(share_ticks)

    def attn_copy(q):
        r = near_rows(q)
        return remote(ybuf.at[r], d_attn.at[c, r], dos.at[q], dor.at[q], at.sib)

    def attn_keep(q):
        r = near_rows(q)
        return pltpu.make_async_copy(ybuf.at[r], d_attn.at[c, r], os.at[q])

    def hid_keep(q):
        r = near_rows(q)
        return pltpu.make_async_copy(acc.at[r], d_hid.at[r], os.at[tiles + q])

    sums = [jnp.zeros((1, hid.shape[1]), F32) for _ in range(4)]
    for q in range(tiles):
        r = near_rows(q)
        y_copy(q).wait()
        grad = acc[r] + yin[r].astype(F32)
        value = hid[r]
        center = value - jnp.mean(value, -1, keepdims=True)
        inverse = lax.rsqrt(jnp.mean(center * center, -1, keepdims=True) + NORM_EPS)
        normal = center * inverse
        out_grad = dy[rows(0, q)].astype(F32)
        total = out_grad + norm_back(grad, normal, inverse, gain[...])
        low = total.astype(BF16)
        ybuf[r] = low
        attn_copy(q).start()
        attn_keep(q).start()
        acc[r] = total
        hid_keep(q).start()
        for i, t in enumerate((low.astype(F32), grad * normal, grad, out_grad)):
            sums[i] += jnp.sum(t, axis=0, keepdims=True)
    for i in range(4):
        vec[i : i + 1] = sums[i]
    vec[4:5] = shift_sum
    vec[5:8] = jnp.zeros((3, hid.shape[1]), F32)

    advance(share_ticks, len(share_ticks))
    share.drain()
    gather.drain()
    part_copy.wait_send()
    for q in range(tiles):
        two_sib(q).wait_send()
        two_peer(q).wait_send()
        two_pass(q).wait_send()
        other_out(q).wait()
        if q >= tiles - 2:
            base_out(q).wait()
        for kind in range(2):
            swap_out(kind, q).wait_send()
        attn_copy(q).wait_send()
        attn_keep(q).wait()
        hid_keep(q).wait()
        there = d_attn.at[1 - c, near_rows(q)]
        remote(there, there, dos.at[q], dor.at[q], at.sib).wait_recv()


def feed(lines, part, tok, params, w1, w2_own, dy, dy_sib):
    local, width = tok.shape
    rows, quarter = w2_own.shape
    kept = columns_of(quarter)[:KEPT]
    tiles = local // TILE
    anywhere = pl.BlockSpec(memory_space=pl.ANY)
    vmem = pl.BlockSpec(memory_space=pltpu.VMEM)
    dma = pltpu.SemaphoreType.DMA
    slots = pltpu.VMEM((local, width), BF16)
    shape = jax.ShapeDtypeStruct
    return pl.pallas_call(
        functools.partial(feed_kernel, lines),
        in_specs=[anywhere] * 2 + [vmem] + [anywhere] * 4,
        out_specs=[anywhere] * 6 + [vmem] * 2,
        out_shape=[
            shape((2, local, width), BF16),
            shape((local, width), F32),
            shape((local, width), F32),
            shape((local, width), BF16),
            shape((width, quarter), BF16),
            shape((width, quarter), BF16),
            shape((2, rows, sum(n for _, n in kept)), F32),
            shape((8, width), F32),
        ],
        scratch_shapes=[
            pltpu.VMEM((width, quarter), BF16),
            pltpu.VMEM((width, quarter), BF16),
            pltpu.VMEM((4 * local, width), BF16),
            pltpu.VMEM((4 * local, width), BF16),
            pltpu.VMEM((4 * local, quarter), BF16),
            pltpu.VMEM((4 * local, quarter), BF16),
            pltpu.VMEM((local, width), F32),
            pltpu.VMEM((2, local, width), BF16),
            pltpu.VMEM((2, local, width), BF16),
            pltpu.VMEM((2, local, width), BF16),
            slots,
            slots,
            pltpu.VMEM((local, width), F32),
            pltpu.VMEM((2, TILE, quarter), BF16),
            pltpu.VMEM((2, TILE, width), F32),
            dma((7,)), dma, dma,
            dma((3, tiles)), dma((3, tiles)),
            dma((2, tiles)), dma((2, tiles)), dma((2, tiles)), dma((2, tiles)),
            dma((tiles,)), dma((tiles,)), dma((2 * tiles,)), dma((tiles,)), dma((tiles,)), dma((2,)),
            dma((tiles,)), dma((tiles,)),
        ]
        + gather_scratch(lines, quarter)
        + share_scratch(lines, rows, kept),
        compiler_params=pltpu.CompilerParams(
            collective_id=2, has_side_effects=True, vmem_limit_bytes=63 << 20
        ),
        name="feed",
    )(part, tok, params, w1, w2_own, dy, dy_sib)


def norm_back(grad_out, normal, inverse, gain):
    scaled = grad_out * gain
    return inverse * (
        scaled
        - jnp.mean(scaled, -1, keepdims=True)
        - normal * jnp.mean(scaled * normal, -1, keepdims=True)
    )


class Links:
    def __init__(self, shards):
        self.shards = shards
        self.lines = shards // 2
        self.s = lax.axis_index("shard")
        self.c = lax.axis_index("ctx")
        self.y = lax.axis_index("tp")
        self.line = self.s // 2
        self.side = self.s % 2
        self.diag = self.c == self.y

    def send(self, value, target, where=lambda c, y: True):
        flat = lambda s, c, y: (s * 2 + c) * 2 + y
        pairs = []
        for s in range(self.shards):
            for c in range(2):
                for y in range(2):
                    if where(c, y):
                        pairs.append((flat(s, c, y), flat(*target(s, c, y))))
        return lax.ppermute(value, AXES, pairs)

    def across(self, value, where=lambda c, y: True):
        return self.send(value, lambda s, c, y: (s, c, 1 - y), where)


def per_device(
    tokens,
    patch_meta,
    attn_norm_gain,
    attn_norm_bias,
    qkv_weight,
    qkv_bias,
    proj_weight,
    proj_bias,
    mlp_norm_gain,
    mlp_norm_bias,
    fc1_weight,
    fc1_bias,
    fc2_weight,
    fc2_bias,
    cotangent,
    *,
    shards,
):
    net = Links(shards)
    c, y = net.c, net.y
    local = tokens.shape[2]
    width = tokens.shape[3]
    full = patch_meta.shape[3]
    inner = qkv_weight.shape[2]
    rows = width // shards
    quarter = fc1_weight.shape[1] // 2
    pick = lambda t, i, d=0: lax.dynamic_index_in_dim(t, i, d, False)
    mine_or = lambda own, other: jnp.where(net.diag, own, other)

    def both(own, other, index):
        return jnp.where(index == 0, jnp.stack([own, other]), jnp.stack([other, own]))

    attn_block = jnp.concatenate([qkv_weight, proj_weight.T[None]], axis=0)
    grad_out = cotangent.reshape(2, local, width)
    tok = pick(tokens, y).reshape(local, width)
    attn_full, normed, grad_out_sib, bias_qkv = collect(
        net.lines, attn_block, tok, attn_norm_gain, attn_norm_bias, grad_out, qkv_bias
    )
    fc1_block = lax.dynamic_slice_in_dim(fc1_weight, c * quarter, quarter, 1)
    fc2_block = lax.dynamic_slice_in_dim(fc2_weight, c * quarter, quarter, 0).T
    bias_fc1 = lax.dynamic_slice_in_dim(fc1_bias, c * quarter, quarter, 0)

    meta = pick(patch_meta, y, 1).reshape(3, full)
    ids = meta[0]
    cosine, sine = rope_tables(meta[1], meta[2])
    shift = jnp.pad(bias_qkv, ((0, 5), (0, 0)))
    low, mixed, mixed_f, lse, attn_part, fc1_full = attend(
        net.lines, attn_full, normed, shift, cosine, sine, ids, fc1_block
    )
    attn_part = attn_part.reshape(2, local, width)
    params = jnp.stack([proj_bias, mlp_norm_gain, mlp_norm_bias, bias_fc1, fc2_bias])
    d_attn, d_hidden, base, mlp_other, grad_fc1_part, grad_fc2_part, fc2_sum, sums_two = feed(
        net.lines, attn_part, tok, params, fc1_full, fc2_block, grad_out, grad_out_sib,
    )
    d_one_part, grad_qkv_part, grad_proj_part, qkv_shift, fc1_sum, block_output = attend_back(
        net.lines, low, mixed_f, lse, cosine, sine, ids, attn_full, normed, mixed, d_attn,
        grad_fc1_part, grad_fc2_part, mlp_other, base,
    )
    late = fc1_sum.shape[2] - quarter
    fc2_sum = jnp.concatenate([fc2_sum, fc1_sum[:, :, :late]], axis=2)
    fc1_sum = fc1_sum[:, :, late:]
    d_one_part = d_one_part.reshape(2, local, width)
    qkv_shift = qkv_shift[:, 0]

    fc1_shift = sums_two[4]
    zero_qkv, zero_fc1 = jnp.zeros_like(qkv_shift), jnp.zeros_like(fc1_shift)
    small = jnp.concatenate(
        [
            jnp.zeros((2 * width,), F32),
            sums_two[0],
            sums_two[1],
            sums_two[2],
            sums_two[3],
            jnp.where(c == 0, qkv_shift, zero_qkv).reshape(-1),
            jnp.where(c == 1, qkv_shift, zero_qkv).reshape(-1),
        ]
        + [jnp.where((y == i) & (c == j), fc1_shift, zero_fc1) for i in range(2) for j in range(2)]
    )
    blocks = (net.lines, 2, rows, inner)
    attn_sum, input_grad, small = settle(
        net.lines, grad_qkv_part.reshape((3,) + blocks), grad_proj_part.reshape(blocks), d_one_part,
        d_hidden, tok, attn_norm_gain, small.reshape(-1, width),
    )
    small = small.reshape(-1)
    input_grad = input_grad.astype(F32)
    grad_qkv, grad_proj = attn_sum[:3], attn_sum[3].T
    grad_fc1 = jnp.moveaxis(fc1_sum, 0, 1).reshape(rows, 2 * quarter)
    grad_fc2 = jnp.moveaxis(fc2_sum, 1, 2).reshape(2 * quarter, rows)

    vec = lambda i: small[i * width : (i + 1) * width]
    at = 6 * width
    qkv_shifts = small[at : at + 6 * inner].reshape(2, 3, inner)
    fc1_shifts = small[at + 6 * inner :].reshape(2, 2 * quarter)
    out_shape = tokens.shape
    return (
        block_output.reshape(out_shape),
        input_grad.reshape(out_shape),
        vec(0),
        vec(1),
        grad_qkv,
        pick(qkv_shifts, y),
        grad_proj,
        vec(2),
        vec(3),
        vec(4),
        grad_fc1,
        pick(fc1_shifts, y),
        grad_fc2,
        vec(5),
    )


def solution(mesh):
    slots = P(None, "shard", "ctx", None)
    placed = (
        slots,
        P(None, None, "shard", None),
        P(),
        P(),
        P(None, "shard", "tp"),
        P(None, "tp"),
        P("tp", "shard"),
        P(),
        P(),
        P(),
        P("shard", "tp"),
        P("tp"),
        P("tp", "shard"),
        P(),
        slots,
    )
    return jax.shard_map(
        functools.partial(per_device, shards=mesh.shape["shard"]),
        mesh=mesh,
        in_specs=placed,
        out_specs=(
            slots,
            slots,
            P(),
            P(),
            P(None, "shard", "tp"),
            P(None, "tp"),
            P("tp", "shard"),
            P(),
            P(),
            P(),
            P("shard", "tp"),
            P("tp"),
            P("tp", "shard"),
            P(),
        ),
        check_vma=False,
    )
```

```python
import functools
import math

import jax
import jax.numpy as jnp
from jax import lax
from jax.experimental import pallas as pl
from jax.experimental.pallas import tpu as pltpu
from jax.sharding import PartitionSpec as P

HDIM = 80
NORM_EPS = 1e-06
GELU = 1.702
ROPE_BASE = 10000.0
SCALE = 1.0 / math.sqrt(HDIM)
LOG2E = 1.0 / math.log(2.0)
NEG = -1e30
F32 = jnp.float32
BF16 = jnp.bfloat16
AXES = ("shard", "ctx", "tp")
QB = 512
AHEAD = 2
LEAD = 1
KEPT = 4
FIRST = 4
SLICE = 384
TILE = 256


def dg(left, right, dims, out=F32):
    return lax.dot_general(left, right, (dims, ((), ())), preferred_element_type=F32).astype(out)


def rope_rows(t, cosine, sine):
    half = t.shape[0] // 2
    first, second = t[:half], t[half:]
    return jnp.concatenate([first * cosine - second * sine, second * cosine + first * sine], axis=0)


def rope_rows_back(t, cosine, sine):
    half = t.shape[0] // 2
    first, second = t[:half], t[half:]
    return jnp.concatenate([first * cosine + second * sine, second * cosine - first * sine], axis=0)


def fill_bias(bias, idc_ref, idr_ref):
    @pl.when(pl.program_id(0) == 0)
    def _():
        bias[...] = jnp.where(idc_ref[...] == idr_ref[...], 0.0, NEG)


def at_step(h, action):
    @pl.when(pl.program_id(0) == h)
    def _():
        action()


def spread(ticks, heads):
    plan = [[] for _ in range(heads)]
    for i, tick in enumerate(ticks):
        plan[i * (heads - 1) // max(1, len(ticks) - 1)].append(tick)
    return plan


def run_ticks(plan):
    for h, ticks in enumerate(plan):
        if ticks:
            at_step(h, lambda ticks=ticks: [tick() for tick in ticks])


def attend_kernel(
    lines, heads, weights, normed, shift, cos_ref, sin_ref, idc_ref, idr_ref, w_own,
    low_ref, mixed_ref, outf_ref, lse_ref, part_ref, w_full,
    bias, proj_in, wv, rows_in, loads, own_sem, zs, zr, xs, xr,
):
    at = Place(lines)
    h = pl.program_id(0)
    gather = Gather(at, w_own, w_full, columns_of(w_own.shape[1]), own_sem, zs, zr, xs, xr)
    local = rows_in.shape[0] // 2
    copies = [
        pltpu.make_async_copy(weights, wv, loads.at[0]),
        pltpu.make_async_copy(normed.at[0], rows_in.at[pl.ds(0, local)], loads.at[1]),
        pltpu.make_async_copy(normed.at[1], rows_in.at[pl.ds(local, local)], loads.at[2]),
    ]

    @pl.when(h == 0)
    def _():
        for copy in copies:
            copy.start()
        at.greet()
        gather.start()
        for copy in copies:
            copy.wait()
        columns = shift[...].T
        for j in range(3):
            proj_in[j] = dg(wv[j], rows_in[...], ((0,), (1,))) + columns[:, j : j + 1]

    fill_bias(bias, idc_ref, idr_ref)
    cosine, sine = cos_ref[...], sin_ref[...]
    mine = pl.ds(pl.multiple_of(h * HDIM, HDIM), HDIM)
    query = rope_rows(proj_in[0, mine], cosine, sine).astype(BF16)
    key_f = rope_rows(proj_in[1, mine], cosine, sine)
    value = proj_in[2, mine].astype(BF16)
    low_ref[0] = query
    low_ref[1] = key_f.astype(BF16)
    low_ref[2] = value
    key_nat = key_f.T.astype(BF16)
    length = query.shape[1]
    factor = SCALE * LOG2E
    for start in range(0, length, QB):
        cols = slice(start, start + QB)
        logits = dg(key_nat, query[:, cols], ((1,), (0,))) + bias[:, cols]
        peak = jnp.max(logits, axis=0, keepdims=True)
        probs = jnp.exp2((logits - peak) * factor)
        total = jnp.sum(probs, axis=0, keepdims=True)
        mixed = dg(value, probs.astype(BF16), ((1,), (0,))) * (1.0 / total)
        mixed_ref[mine, cols] = mixed.astype(BF16)
        outf_ref[:, cols] = mixed
        lse_ref[0, :, cols] = peak * factor + jnp.log2(total)

    ticks = [functools.partial(gather.tick, i) for i in range(len(gather.pieces))]
    run_ticks(spread(ticks, heads))

    @pl.when(h == heads - 1)
    def _():
        def body(i, carry):
            r = pl.ds(pl.multiple_of(i * TILE, TILE), TILE)
            part_ref[r] = dg(mixed_ref[:, r], wv[3], ((0,), (1,)), BF16)
            return carry

        lax.fori_loop(0, length // TILE, body, 0)
        gather.finish()
        gather.drain()


def attend(lines, weights, normed, shift, cosine, sine, ids, w_own):
    _, width, inner = weights.shape
    length = ids.shape[0]
    heads = inner // HDIM
    half = HDIM // 2
    head = lambda h: (0, h, 0)
    whole = lambda h: (0, 0)
    rows, quarter = w_own.shape
    anywhere = pl.BlockSpec(memory_space=pl.ANY)
    return pl.pallas_call(
        functools.partial(attend_kernel, lines, heads),
        grid=(heads,),
        in_specs=[
            anywhere,
            anywhere,
            pl.BlockSpec((8, inner), whole),
            pl.BlockSpec((half, length), whole),
            pl.BlockSpec((half, length), whole),
            pl.BlockSpec((length, 1), whole),
            pl.BlockSpec((1, length), whole),
            anywhere,
        ],
        out_specs=[
            pl.BlockSpec((3, HDIM, length), head),
            pl.BlockSpec((inner, length), whole),
            pl.BlockSpec((HDIM, length), lambda h: (h, 0)),
            pl.BlockSpec((1, 1, length), lambda h: (h, 0, 0)),
            pl.BlockSpec((length, width), whole),
            anywhere,
        ],
        out_shape=[
            jax.ShapeDtypeStruct((3, inner, length), BF16),
            jax.ShapeDtypeStruct((inner, length), BF16),
            jax.ShapeDtypeStruct((inner, length), F32),
            jax.ShapeDtypeStruct((heads, 1, length), F32),
            jax.ShapeDtypeStruct((length, width), BF16),
            jax.ShapeDtypeStruct((2 * lines * rows, quarter), BF16),
        ],
        scratch_shapes=[
            pltpu.VMEM((length, length), F32),
            pltpu.VMEM((3, inner, length), F32),
            pltpu.VMEM(weights.shape, BF16),
            pltpu.VMEM((length, width), BF16),
            pltpu.SemaphoreType.DMA((3,)),
        ]
        + gather_scratch(lines, quarter),
        compiler_params=pltpu.CompilerParams(
            collective_id=3, has_side_effects=True, vmem_limit_bytes=63 << 20
        ),
        cost_estimate=pl.CostEstimate(
            flops=4 * inner * length * length + 8 * inner * length * width,
            transcendentals=heads * length * length,
            bytes_accessed=26 * inner * length,
        ),
        name="attend",
    )(weights, normed, shift, cosine, sine, ids[:, None], ids[None, :], w_own)


def attend_back_kernel(
    lines, heads, low_ref, outf_ref, lse_ref, cos_ref, sin_ref, idc_ref, idr_ref,
    weights, normed, mixed, d_attn, w_grad, w_grad_two, other, base,
    one_ref, qkv_grad, proj_grad, shift_ref, w_out, out_full,
    bias, dq, dk, dv, d_mixed, d_proj, wv, rows_in, mixed_in, base_in, other_in, out_low, tile_buf, w_sum,
    loads, ys, yr, ks, ts, *share_refs
):
    at = Place(lines)
    h = pl.program_id(0)
    slices = [(w_grad,) + piece for piece in columns_of(w_grad.shape[1])]
    slices = [(w_grad_two,) + piece for piece in columns_of(w_grad.shape[1])[KEPT:]] + slices
    share = Share(at, slices, w_sum, *share_refs)
    length, width = rows_in.shape
    local = length // 2

    def load_rows(source):
        return [
            pltpu.make_async_copy(source.at[i], rows_in.at[pl.ds(i * local, local)], loads.at[i])
            for i in range(2)
        ]

    mixed_copy = pltpu.make_async_copy(mixed, mixed_in, loads.at[2])
    weight_copy = pltpu.make_async_copy(weights, wv, loads.at[3])
    base_copy = pltpu.make_async_copy(base, base_in, loads.at[4])
    chunk = local // 4
    chunks = [pl.ds(q * chunk, chunk) for q in range(4)]
    other_copies = [
        remote(other.at[r], other_in.at[r], ys.at[0, q], yr.at[0, q], at.peer) for q, r in enumerate(chunks)
    ]
    out_copies = [
        remote(out_low.at[r], out_full.at[at.y, r], ys.at[1, q], yr.at[1, q], at.peer)
        for q, r in enumerate(chunks)
    ]
    out_keeps = [
        pltpu.make_async_copy(out_low.at[r], out_full.at[at.y, r], ks.at[q]) for q, r in enumerate(chunks)
    ]

    @pl.when(h == 0)
    def _():
        for copy in load_rows(d_attn) + [mixed_copy, weight_copy, base_copy]:
            copy.start()
        at.greet()
        share.flow.start()
        for copy in other_copies:
            copy.start()
        for copy in load_rows(d_attn) + [mixed_copy, weight_copy]:
            copy.wait()
        d_mixed[...] = dg(wv[3], rows_in[...], ((0,), (1,)), BF16)

        def body(i, carry):
            cols = pl.ds(pl.multiple_of(i * TILE, TILE), TILE)
            proj_grad[cols] = dg(rows_in[:, cols], mixed_in[...], ((0,), (1,)), BF16)
            return carry

        lax.fori_loop(0, width // TILE, body, 0)
        for copy in load_rows(normed):
            copy.start()

    fill_bias(bias, idc_ref, idr_ref)
    cosine, sine = cos_ref[...], sin_ref[...]
    mine = pl.ds(pl.multiple_of(h * HDIM, HDIM), HDIM)
    query, key = low_ref[0], low_ref[1]
    grad = d_mixed[mine]
    grad_f = grad.astype(F32)
    delta = jnp.sum(grad_f * outf_ref[...], axis=0, keepdims=True)
    nat = lambda t: t.astype(F32).T.astype(BF16)
    query_nat, key_nat, value_nat, grad_nat = nat(query), nat(key), nat(low_ref[2]), nat(grad)
    lse = lse_ref[0]
    factor = SCALE * LOG2E
    for start in range(0, length, QB):
        cols = slice(start, start + QB)
        logits = dg(key_nat, query[:, cols], ((1,), (0,)))
        probs = jnp.exp2(logits * factor + bias[:, cols] - lse[:, cols])
        d_probs = dg(value_nat, grad[:, cols], ((1,), (0,)))
        d_logits = (probs * (d_probs - delta[:, cols])).astype(BF16)
        part_v = dg(probs.astype(BF16), grad_nat[cols], ((1,), (0,)))
        part_k = dg(d_logits, query_nat[cols], ((1,), (0,)))
        dq[:, cols] = dg(key, d_logits, ((1,), (0,)))
        if start == 0:
            dv[...] = part_v
            dk[...] = part_k
        else:
            dv[...] += part_v
            dk[...] += part_k
    d_proj[0, mine] = rope_rows_back(dq[...] * SCALE, cosine, sine).astype(BF16)
    d_proj[1, mine] = rope_rows_back(dk[...].T * SCALE, cosine, sine).astype(BF16)
    d_proj[2, mine] = dv[...].T.astype(BF16)

    def out_rows(q):
        r = chunks[q]
        if q == 0:
            base_copy.wait()
        other_copies[q].wait()
        out_low[r] = (base_in[r] + other_in[r].astype(F32)).astype(BF16)
        out_copies[q].start()
        out_keeps[q].start()

    for q, step in enumerate((0, 1, 3, 5)):
        at_step(step, functools.partial(out_rows, q))

    ticks = share.flow.ticks()
    early = min(len(ticks), heads // 2 + 1)
    for i in range(early):
        at_step(max(0, 2 * i - 1), ticks[i])
    ticks = ticks[early:]

    @pl.when(h == heads - 1)
    def _():
        for copy in load_rows(normed):
            copy.wait()
        one_rows = jnp.ones((8, length), BF16)

        def one_body(i, carry):
            r = pl.ds(pl.multiple_of(i * TILE, TILE), TILE)
            total = dg(d_proj[0, :, r], wv[0], ((0,), (1,)))
            for j in range(1, 3):
                total += dg(d_proj[j, :, r], wv[j], ((0,), (1,)))
            one_ref[r] = total.astype(BF16)
            return carry

        lax.fori_loop(0, length // TILE, one_body, 0)
        for tick in ticks[:1]:
            tick()
        count = width // TILE

        def copy_out(i):
            where = pl.ds(pl.multiple_of(lax.rem(i, count) * TILE, TILE), TILE)
            slot = lax.rem(i, 2)
            return pltpu.make_async_copy(tile_buf.at[slot], qkv_grad.at[i // count, where], ts.at[slot])

        def grad_body(i, carry):
            cols = pl.ds(pl.multiple_of(lax.rem(i, count) * TILE, TILE), TILE)

            @pl.when(i >= 2)
            def _():
                copy_out(i - 2).wait()

            tile_buf[lax.rem(i, 2)] = dg(rows_in[:, cols], d_proj[i // count], ((0,), (1,)), BF16)
            copy_out(i).start()
            return carry

        lax.fori_loop(0, 3 * count, grad_body, 0)
        for i in range(max(0, 3 * count - 2), 3 * count):
            copy_out(i).wait()
        for j in range(3):
            shift_ref[j] = dg(one_rows, d_proj[j], ((1,), (1,)))
        for tick in ticks[1:]:
            tick()
        share.drain()
        w_out[...] = w_sum[...]
        for q, r in enumerate(chunks):
            out_copies[q].wait_send()
            there = out_full.at[1 - at.y, r]
            remote(there, there, ys.at[1, q], yr.at[1, q], at.peer).wait_recv()
            out_keeps[q].wait()


def attend_back(lines, low, outf, lse, cosine, sine, ids, *arrays):
    weights, w_grad = arrays[0], arrays[4]
    _, inner, length = low.shape
    width = weights.shape[1]
    local = length // 2
    heads = inner // HDIM
    half = HDIM // 2
    w_rows, quarter = w_grad.shape
    rows = w_rows // (2 * lines)
    pieces = columns_of(quarter)[KEPT:] + columns_of(quarter)
    columns = sum(count for _, count in pieces)
    head = lambda h: (0, h, 0)
    whole = lambda h: (0, 0)
    cube = lambda h: (0, 0, 0)
    anywhere = pl.BlockSpec(memory_space=pl.ANY)
    dma = pltpu.SemaphoreType.DMA
    shape = jax.ShapeDtypeStruct
    return pl.pallas_call(
        functools.partial(attend_back_kernel, lines, heads),
        grid=(heads,),
        in_specs=[
            pl.BlockSpec((3, HDIM, length), head),
            pl.BlockSpec((HDIM, length), lambda h: (h, 0)),
            pl.BlockSpec((1, 1, length), lambda h: (h, 0, 0)),
            pl.BlockSpec((half, length), whole),
            pl.BlockSpec((half, length), whole),
            pl.BlockSpec((length, 1), whole),
            pl.BlockSpec((1, length), whole),
        ]
        + [anywhere] * 8,
        out_specs=[
            pl.BlockSpec((length, width), whole),
            anywhere,
            pl.BlockSpec((width, inner), whole),
            pl.BlockSpec((3, 8, inner), cube),
            pl.BlockSpec((2, rows, columns), cube),
            anywhere,
        ],
        out_shape=[
            shape((length, width), BF16),
            shape((3, width, inner), BF16),
            shape((width, inner), BF16),
            shape((3, 8, inner), F32),
            shape((2, rows, columns), F32),
            shape((2, local, width), BF16),
        ],
        scratch_shapes=[
            pltpu.VMEM((length, length), F32),
            pltpu.VMEM((HDIM, length), F32),
            pltpu.VMEM((length, HDIM), F32),
            pltpu.VMEM((length, HDIM), F32),
            pltpu.VMEM((inner, length), BF16),
            pltpu.VMEM((3, inner, length), BF16),
            pltpu.VMEM(weights.shape, BF16),
            pltpu.VMEM((length, width), BF16),
            pltpu.VMEM((inner, length), BF16),
            pltpu.VMEM((local, width), F32),
            pltpu.VMEM((local, width), BF16),
            pltpu.VMEM((local, width), BF16),
            pltpu.VMEM((2, TILE, inner), BF16),
            pltpu.VMEM((2, rows, columns), F32),
            dma((5,)), dma((2, 4)), dma((2, 4)), dma((4,)), dma((2,)),
        ]
        + share_scratch(lines, rows, pieces),
        compiler_params=pltpu.CompilerParams(
            collective_id=4, has_side_effects=True, vmem_limit_bytes=63 << 20
        ),
        cost_estimate=pl.CostEstimate(
            flops=10 * inner * length * length + 20 * inner * length * width,
            transcendentals=heads * length * length,
            bytes_accessed=18 * inner * length,
        ),
        name="attend_back",
    )(low, outf, lse, cosine, sine, ids[:, None], ids[None, :], *arrays)


def rope_tables(patch_row, patch_col):
    quarter = HDIM // 4
    frequency = ROPE_BASE ** (-2.0 * jnp.arange(quarter, dtype=F32) / (HDIM // 2))
    angles = jnp.concatenate(
        [
            frequency[:, None] * patch_row.astype(F32)[None, :],
            frequency[:, None] * patch_col.astype(F32)[None, :],
        ],
        axis=0,
    )
    return jnp.cos(angles), jnp.sin(angles)


MESH = pl.DeviceIdType.MESH


def remote(src, dst, send_sem, recv_sem, device):
    return pltpu.make_async_remote_copy(
        src_ref=src,
        dst_ref=dst,
        send_sem=send_sem,
        recv_sem=recv_sem,
        device_id=device,
        device_id_type=MESH,
    )


class Place:
    def __init__(self, lines):
        self.lines = lines
        self.s = lax.axis_index("shard")
        self.c = lax.axis_index("ctx")
        self.y = lax.axis_index("tp")
        self.line = self.s // 2
        self.side = lax.rem(self.s, 2)
        self.sib = (self.s, 1 - self.c, self.y)
        self.peer = (self.s, self.c, 1 - self.y)
        self.beside = (self.line * 2 + 1 - self.side, self.c, self.y)

    def ahead(self, k):
        return (lax.rem(self.line + k, self.lines) * 2 + self.side, self.c, self.y)

    def source(self, k):
        return lax.rem(self.line + self.lines - k, self.lines) * 2

    def greet(self):
        barrier = pltpu.get_barrier_semaphore()
        others = [self.sib, self.peer, self.beside] + [self.ahead(k) for k in range(1, self.lines)]
        for other in others:
            pl.semaphore_signal(barrier, inc=1, device_id=other, device_id_type=MESH)
        pl.semaphore_wait(barrier, len(others))


def norm_rows(values):
    center = values - jnp.mean(values, -1, keepdims=True)
    spread = jnp.mean(center * center, -1, keepdims=True)
    return center * lax.rsqrt(spread + NORM_EPS)


def collect_kernel(
    lines, pieces, block, tok, gain, shift, dy, qb,
    out, normed, dy_sib, qb_out,
    norm_buf, own_sem, zs, zr, xs, xr, ys, yr, ms, mr,
):
    at = Place(lines)
    diag = at.c == at.y

    def part(p, s):
        j, first, count, _ = pieces[p]
        rows = block.shape[1]
        return out.at[j, pl.ds(pl.multiple_of(s * rows, rows), rows), pl.ds(first, count)]

    def own(p):
        j, first, count, _ = pieces[p]
        return block.at[j, :, pl.ds(first, count)]

    def z_copy(p, k, src):
        return remote(src, part(p, at.s), zs.at[p, k], zr.at[p, k], at.ahead(k))

    def x_copy(p, k, src):
        return remote(src, part(p, at.source(k) + at.side), xs.at[p, k], xr.at[p, k], at.beside)

    def y_copy(p, i, src, s):
        return remote(src, part(p, s), ys.at[p, i], yr.at[p, i], at.peer)

    def near(k):
        return at.source(k) + at.side

    def far(k):
        return at.source(k) + 1 - at.side

    def z_wait(p, k):
        z_copy(p, k, part(p, near(k))).wait_recv()

    def x_wait(p, k):
        x_copy(p, k, part(p, far(k))).wait_recv()

    def y_wait(p, i, s):
        y_copy(p, i, part(p, s), s).wait_recv()

    late = [p for p in range(len(pieces)) if pieces[p][3]]
    early = [p for p in range(len(pieces)) if not pieces[p][3]]
    order = late + early
    at.greet()

    own_rows = pl.ds(pl.multiple_of(at.s * block.shape[1], block.shape[1]), block.shape[1])
    own_copy = pltpu.make_async_copy(block, out.at[:, own_rows], own_sem.at[0])
    bias_copy = pltpu.make_async_copy(qb, qb_out, own_sem.at[1])

    @pl.when(diag)
    def _():
        own_copy.start()
        bias_copy.start()
        remote(qb, qb_out, ms.at[0], mr.at[0], at.peer).start()
        for p in early:
            y_copy(p, 0, own(p), at.s).start()
        for p in order[:LEAD]:
            for k in range(1, lines):
                z_copy(p, k, own(p)).start()
        for p in order:
            x_copy(p, 0, own(p)).start()
            if p in late:
                y_copy(p, 0, own(p), at.s).start()

    dy_copy = remote(dy, dy_sib, ms.at[1], mr.at[1], at.sib)
    dy_copy.start()
    norm_buf[...] = (norm_rows(tok[...].astype(F32)) * gain[...] + shift[...]).astype(BF16)
    norm_copy = remote(norm_buf, normed.at[at.c], ms.at[2], mr.at[2], at.sib)
    norm_copy.start()
    norm_keep = pltpu.make_async_copy(norm_buf, normed.at[at.c], own_sem.at[2])
    norm_keep.start()

    @pl.when(diag)
    def _():
        for step in range(len(order) + 1):
            if step < len(order):
                p = order[step]
                if step + LEAD < len(order):
                    for k in range(1, lines):
                        z_copy(order[step + LEAD], k, own(order[step + LEAD])).start()
                for k in range(1, lines):
                    z_wait(p, k)
                    x_copy(p, k, part(p, near(k))).start()
                    if p in late:
                        y_copy(p, k, part(p, near(k)), near(k)).start()
            if step > 0:
                p = order[step - 1]
                for k in range(lines):
                    x_wait(p, k)
                    if p in late:
                        y_copy(p, lines + k, part(p, far(k)), far(k)).start()
        own_copy.wait()
        bias_copy.wait()
        remote(qb, qb_out, ms.at[0], mr.at[0], at.peer).wait_send()
        for p in order:
            for k in range(1, lines):
                z_copy(p, k, own(p)).wait_send()
            for k in range(lines):
                x_copy(p, k, part(p, near(k))).wait_send()
            y_copy(p, 0, own(p), at.s).wait_send()
            if p in late:
                for k in range(1, lines):
                    y_copy(p, k, part(p, near(k)), near(k)).wait_send()
                for k in range(lines):
                    y_copy(p, lines + k, part(p, far(k)), far(k)).wait_send()

    @pl.when(jnp.logical_not(diag))
    def _():
        for p in early:
            y_wait(p, 0, at.s)
            for k in range(1, lines):
                z_copy(p, k, part(p, at.s)).start()
            x_copy(p, 0, part(p, at.s)).start()
        for step in range(len(early) + 1):
            if step < len(early):
                p = early[step]
                for k in range(1, lines):
                    z_wait(p, k)
                    x_copy(p, k, part(p, near(k))).start()
            if step > 0:
                for k in range(lines):
                    x_wait(early[step - 1], k)
        for p in early:
            for k in range(1, lines):
                z_copy(p, k, part(p, at.s)).wait_send()
            for k in range(lines):
                x_copy(p, k, part(p, near(k))).wait_send()
        remote(qb, qb_out, ms.at[0], mr.at[0], at.peer).wait_recv()
        for p in late:
            for k in range(lines):
                y_wait(p, k, near(k))
                y_wait(p, lines + k, far(k))

    dy_copy.wait()
    norm_copy.wait_send()
    remote(norm_buf, normed.at[1 - at.c], ms.at[2], mr.at[2], at.sib).wait_recv()
    norm_keep.wait()


def collect(lines, block, tok, gain, shift, dy, qb):
    groups, rows, inner = block.shape
    local, width = tok.shape
    cut = (inner * 3 // 5) // 128 * 128
    pieces = [(j, f, n, i < 5) for i, (j, f, n) in enumerate((j, f, n) for j in range(4) for f, n in ((0, cut), (cut, inner - cut)))]
    n = len(pieces)
    anywhere = pl.BlockSpec(memory_space=pl.ANY)
    vmem = pl.BlockSpec(memory_space=pltpu.VMEM)
    dma = pltpu.SemaphoreType.DMA
    return pl.pallas_call(
        functools.partial(collect_kernel, lines, pieces),
        in_specs=[anywhere, vmem, vmem, vmem, anywhere, anywhere],
        out_specs=[anywhere] * 4,
        out_shape=[
            jax.ShapeDtypeStruct((groups, 2 * lines * rows, inner), BF16),
            jax.ShapeDtypeStruct((2, local, width), BF16),
            jax.ShapeDtypeStruct(dy.shape, BF16),
            jax.ShapeDtypeStruct(qb.shape, F32),
        ],
        scratch_shapes=[
            pltpu.VMEM((local, width), BF16),
            dma((3,)),
            dma((n, lines)),
            dma((n, lines)),
            dma((n, lines)),
            dma((n, lines)),
            dma((n, 2 * lines)),
            dma((n, 2 * lines)),
            dma((3,)),
            dma((3,)),
        ],
        compiler_params=pltpu.CompilerParams(
            collective_id=0, has_side_effects=True, vmem_limit_bytes=63 << 20
        ),
        name="collect",
    )(block, tok, gain[None], shift[None], dy, qb)


class Gather:
    def __init__(self, at, own, full, pieces, own_sem, zs, zr, xs, xr):
        self.at, self.own, self.full, self.pieces = at, own, full, pieces
        self.own_sem, self.zs, self.zr, self.xs, self.xr = own_sem, zs, zr, xs, xr
        self.rows = own.shape[0]

    def part(self, p, s):
        start, count = self.pieces[p]
        return self.full.at[pl.ds(pl.multiple_of(s * self.rows, self.rows), self.rows), pl.ds(start, count)]

    def z_copy(self, p, k):
        start, count = self.pieces[p]
        src = self.own.at[:, pl.ds(start, count)]
        return remote(src, self.part(p, self.at.s), self.zs.at[p, k], self.zr.at[p, k], self.at.ahead(k))

    def x_copy(self, p, k):
        start, count = self.pieces[p]
        there = self.part(p, self.at.source(k) + self.at.side)
        src = self.own.at[:, pl.ds(start, count)] if k == 0 else there
        return remote(src, there, self.xs.at[p, k], self.xr.at[p, k], self.at.beside)

    def z_wait(self, p, k):
        there = self.part(p, self.at.source(k) + self.at.side)
        remote(there, there, self.zs.at[p, k], self.zr.at[p, k], self.at.ahead(k)).wait_recv()

    def x_wait(self, p, k):
        there = self.part(p, self.at.source(k) + 1 - self.at.side)
        remote(there, there, self.xs.at[p, k], self.xr.at[p, k], self.at.beside).wait_recv()

    def keep(self):
        there = self.full.at[pl.ds(pl.multiple_of(self.at.s * self.rows, self.rows), self.rows)]
        return pltpu.make_async_copy(self.own, there, self.own_sem)

    def begin(self, p):
        if p < len(self.pieces):
            for k in range(1, self.at.lines):
                self.z_copy(p, k).start()

    def start(self):
        self.keep().start()
        for p in range(AHEAD):
            self.begin(p)
        for p in range(len(self.pieces)):
            self.x_copy(p, 0).start()

    def tick(self, p):
        self.begin(p + AHEAD)
        for k in range(1, self.at.lines):
            self.z_wait(p, k)
            self.x_copy(p, k).start()

    def finish(self):
        for p in range(len(self.pieces)):
            for k in range(self.at.lines):
                self.x_wait(p, k)
        self.keep().wait()

    def drain(self):
        for p in range(len(self.pieces)):
            for k in range(self.at.lines):
                self.x_copy(p, k).wait_send()
                if k > 0:
                    self.z_copy(p, k).wait_send()


class Scatter:
    def __init__(self, at, block, mine, xbuf, zin, xs, xr, zs, zr, load=None):
        self.at, self.block, self.mine, self.xbuf, self.zin = at, block, mine, xbuf, zin
        self.xs, self.xr, self.zs, self.zr, self.load = xs, xr, zs, zr, load

    def x_copy(self, row):
        src = self.block(row, 1 - self.at.side)
        return remote(src, self.xbuf.at[row], self.xs.at[row], self.xr.at[row], self.at.beside)

    def load_copy(self, row):
        return pltpu.make_async_copy(self.block(row, self.at.side), self.mine.at[row], self.load.at[row])

    def z_copy(self, k):
        row = lax.rem(self.at.line + k, self.at.lines)
        return remote(self.mine.at[row], self.zin.at[k], self.zs.at[k], self.zr.at[k], self.at.ahead(k))

    def start(self):
        for row in range(self.at.lines):
            self.x_copy(row).start()
            if self.load is not None:
                self.load_copy(row).start()

    def middle(self):
        for row in range(self.at.lines):
            self.x_copy(row).wait_recv()
            if self.load is not None:
                self.load_copy(row).wait()
                here = self.mine[row]
            else:
                here = self.block(row, self.at.side)[...]
            self.mine[row] = (here.astype(F32) + self.xbuf[row].astype(F32)).astype(BF16)
        for k in range(1, self.at.lines):
            self.z_copy(k).start()

    def finish(self):
        total = self.mine[self.at.line].astype(F32)
        for k in range(1, self.at.lines):
            self.z_copy(k).wait_recv()
            total += self.zin[k].astype(F32)
        return total

    def drain(self):
        for row in range(self.at.lines):
            self.x_copy(row).wait_send()
        for k in range(1, self.at.lines):
            self.z_copy(k).wait_send()


class Flow:
    def __init__(self, units, begin, done, lag=1):
        self.units, self.begin, self.done, self.lag = units, begin, done, lag

    def start(self):
        for i in range(min(AHEAD, len(self.units))):
            self.begin(i)

    def tick(self, i):
        count = len(self.units)
        if i < count:
            self.units[i].middle()
            if i + AHEAD < count:
                self.begin(i + AHEAD)
        if 0 <= i - self.lag < count:
            self.done(i - self.lag, self.units[i - self.lag].finish())

    def ticks(self):
        return [functools.partial(self.tick, i) for i in range(len(self.units) + self.lag)]


class Share:
    def __init__(self, at, slices, out, mine, xbuf, zin, xs, xr, zs, zr, load, cs, cr):
        rows = out.shape[1]
        self.at, self.out, self.cs, self.cr = at, out, cs, cr
        self.places, units, total = [], [], 0
        for i, (grad, start, count) in enumerate(slices):

            def block(line, side, grad=grad, start=start, count=count):
                first = pl.multiple_of((2 * line + side) * rows, rows)
                return grad.at[pl.ds(first, rows), pl.ds(start, count)]

            cut = lambda ref: ref.at[:, :, pl.ds(total, count)]
            units.append(
                Scatter(
                    at, block, cut(mine), cut(xbuf), cut(zin), xs.at[i], xr.at[i], zs.at[i], zr.at[i], load.at[i]
                )
            )
            self.places.append((total, count))
            total += count
        self.flow = Flow(units, lambda i: units[i].start(), self.done, lag=2)

    def share(self, i, core):
        start, count = self.places[i]
        here = self.out.at[core, :, pl.ds(start, count)]
        return remote(here, here, self.cs.at[i], self.cr.at[i], self.at.sib)

    def done(self, i, total):
        start, count = self.places[i]
        self.out[self.at.c, :, start : start + count] = total
        self.share(i, self.at.c).start()

    def drain(self):
        for i, unit in enumerate(self.flow.units):
            unit.drain()
            self.share(i, self.at.c).wait_send()
            self.share(i, 1 - self.at.c).wait_recv()


def columns_of(quarter):
    return [(start, 256) for start in range(0, quarter, 256)]


def share_scratch(lines, rows, pieces):
    n = len(pieces)
    dma = pltpu.SemaphoreType.DMA
    slab = pltpu.VMEM((lines, rows, sum(count for _, count in pieces)), BF16)
    return [slab] * 3 + [dma((n, lines))] * 5 + [dma((n,))] * 2


def gather_scratch(lines, quarter):
    n = len(columns_of(quarter))
    dma = pltpu.SemaphoreType.DMA
    return [dma] + [dma((n, lines))] * 4


def settle_kernel(
    lines, pieces, qkv, proj, d_one, d_hid, tok, gain, vec,
    attn_out, grad_full, vec_out,
    grad_own, here, mine, ax, ai, ay, al, one_in, vown, vbuf, vin,
    hs, axs, axr, azs, azr, ays, ayr, cs, cr, vs, vr, os, orr, ms, mr, ks,
):
    at = Place(lines)
    diag = at.c == at.y
    first = [p for p in range(len(pieces)) if pieces[p][3]]
    last = [p for p in range(len(pieces)) if not pieces[p][3]]

    def cut(ref, p):
        _, start, count, _ = pieces[p]
        return ref.at[..., pl.ds(start, count)]

    def source(p):
        j = pieces[p][0]
        return cut(proj if j == 3 else qkv.at[j], p)

    def local_part(p):
        return cut(here.at[pieces[p][0]], p)

    class Direct(Scatter):
        def __init__(self, p):
            j = pieces[p][0]
            super().__init__(
                at, lambda line, side: local_part(p).at[line, side],
                cut(mine.at[j], p), cut(ax.at[j], p), cut(ai.at[j], p),
                axs.at[p], axr.at[p], azs.at[p], azr.at[p],
            )
            self.p = p

        def x_copy(self, row):
            src = source(self.p).at[row, 1 - at.side]
            return remote(src, self.xbuf.at[row], self.xs.at[row], self.xr.at[row], at.beside)

    def summed(p):
        j = pieces[p][0]
        return Scatter(
            at, lambda line, side: cut(ay.at[j, line, side], p),
            cut(mine.at[j], p), cut(ax.at[j], p), cut(ai.at[j], p),
            axs.at[p], axr.at[p], azs.at[p], azr.at[p],
        )

    def pair_copy(p, half):
        side = (1 - at.side, at.side)[half]
        there = cut(ay.at[pieces[p][0], :, side], p)
        return remote(source(p).at[:, side], there, ays.at[p, half], ayr.at[p, half], at.peer)

    def last_copy(p):
        j = pieces[p][0]
        return remote(cut(al.at[j, 0], p), cut(al.at[j, 1], p), ays.at[p, 0], ayr.at[p, 0], at.peer)

    def attn_share(p):
        there = cut(attn_out.at[pieces[p][0]], p)
        return remote(there, there, cs.at[p], cr.at[p], at.sib)

    order = last + first
    diag_units = [Direct(p) for p in last] + [summed(p) for p in first]
    off_units = [Direct(p) for p in last]

    def diag_begin(i):
        p = order[i]
        if p in first:
            j, start, count, _ = pieces[p]
            for half in range(2):
                pair_copy(p, half).wait_recv()
            for row in range(lines):
                for side in range(2):
                    both = local_part(p)[row, side].astype(F32) + cut(ay.at[j, row, side], p)[...].astype(F32)
                    ay[j, row, side, :, start : start + count] = both.astype(BF16)
        diag_units[i].start()

    def diag_done(i, total):
        p = order[i]
        j, start, count, _ = pieces[p]
        attn_out[j, :, start : start + count] = total
        if p in first:
            attn_share(p).start()

    def off_done(i, total):
        j, start, count, _ = pieces[last[i]]
        al[j, 0, :, start : start + count] = total.astype(BF16)
        last_copy(last[i]).start()

    diag_flow = Flow(diag_units, diag_begin, diag_done)
    off_flow = Flow(off_units, lambda i: off_units[i].start(), off_done)

    def ticks(begin, end):
        @pl.when(diag)
        def _():
            for i in range(begin, end):
                diag_flow.tick(i)

        @pl.when(jnp.logical_not(diag))
        def _():
            for i in range(begin, end):
                off_flow.tick(i)

    loads = [
        pltpu.make_async_copy(qkv, here.at[pl.ds(0, 3)], hs.at[0]),
        pltpu.make_async_copy(proj, here.at[3], hs.at[1]),
    ]
    for load in loads:
        load.start()
    at.greet()
    one_copy = remote(d_one.at[1 - at.c], one_in, os, orr, at.sib)
    one_copy.start()

    @pl.when(diag)
    def _():
        for i in range(min(AHEAD, len(last))):
            diag_units[i].start()

    @pl.when(jnp.logical_not(diag))
    def _():
        for p in first:
            for half in range(2):
                pair_copy(p, half).start()
        off_flow.start()

    one_copy.wait_recv()
    local = tok.shape[0]
    tile = TILE // 2
    grad_copies, grad_keeps = [], []
    sums = [jnp.zeros((1, tok.shape[1]), F32) for _ in range(2)]
    for q in range(local // tile):
        r = pl.ds(q * tile, tile)
        value = tok[r].astype(F32)
        center = value - jnp.mean(value, -1, keepdims=True)
        inverse = lax.rsqrt(jnp.mean(center * center, -1, keepdims=True) + NORM_EPS)
        normal = center * inverse
        grad = d_one[at.c, r].astype(F32) + one_in[r].astype(F32)
        grad_own[r] = (d_hid[r] + norm_back(grad, normal, inverse, gain[...])).astype(BF16)
        copy = remote(grad_own.at[r], grad_full.at[at.y, r], ms.at[q], mr.at[q], at.peer)
        keep = pltpu.make_async_copy(grad_own.at[r], grad_full.at[at.y, r], ks.at[q])
        keep.start()
        grad_keeps.append(keep)
        grad_copies.append(copy)
        for i, t in enumerate((grad * normal, grad)):
            sums[i] += jnp.sum(t, axis=0, keepdims=True)
    vown[...] = vec[...]
    for i in range(2):
        vown[i : i + 1] = sums[i]

    def small_copy(stage, device):
        src = vown if stage == 0 else vbuf.at[stage - 1]
        return remote(src, vin.at[stage], vs.at[stage], vr.at[stage], device)

    steps = [at.sib, at.peer, at.beside]

    def small_start(stage):
        small_copy(stage, steps[stage]).start()

    def small_add(stage):
        small_copy(stage, steps[stage]).wait_recv()
        before = vown[...] if stage == 0 else vbuf[stage - 1]
        vbuf[stage] = before + vin[stage]

    def line_copy(k):
        return remote(vbuf.at[2], vin.at[3 + at.line], vs.at[2 + k], vr.at[2 + k], at.ahead(k))

    def line_wait(k):
        there = vin.at[3 + at.source(k) // 2]
        remote(vbuf.at[2], there, vs.at[2 + k], vr.at[2 + k], at.ahead(k)).wait_recv()

    small_start(0)
    for load in loads:
        load.wait()
    total_ticks = len(order) + 1
    small_add(0)
    small_start(1)
    for i in range(total_ticks):
        ticks(i, i + 1)
        if i >= 1 and grad_copies[i - 1 : i]:
            grad_copies[i - 1].start()
        if i == total_ticks // 2:
            small_add(1)
            small_start(2)
        if i == total_ticks - 2:
            small_add(2)
            for k in range(1, lines):
                line_copy(k).start()
            vin[3 + at.line] = vbuf[2]

    @pl.when(diag)
    def _():
        for p in last:
            j, start, count, _ = pieces[p]
            last_copy(p).wait_recv()
            attn_out[j, :, start : start + count] += cut(al.at[j, 1], p)[...].astype(F32)
            attn_share(p).start()

    for k in range(1, lines):
        line_wait(k)
    total = vin[3]
    for row in range(1, lines):
        total = total + vin[3 + row]
    vec_out[...] = total

    @pl.when(diag)
    def _():
        for unit in diag_units:
            unit.drain()
        for p in order:
            attn_share(p).wait_send()

    @pl.when(jnp.logical_not(diag))
    def _():
        for unit in off_units:
            unit.drain()
        for p in last:
            last_copy(p).wait_send()
        for p in first:
            for half in range(2):
                pair_copy(p, half).wait_send()
        for p in order:
            attn_share(p).wait_recv()

    for stage in range(3):
        small_copy(stage, steps[stage]).wait_send()
    for k in range(1, lines):
        line_copy(k).wait_send()
    one_copy.wait_send()
    for q, copy in enumerate(grad_copies):
        copy.wait_send()
        there = grad_full.at[1 - at.y, pl.ds(q * tile, tile)]
        remote(there, there, ms.at[q], mr.at[q], at.peer).wait_recv()
        grad_keeps[q].wait()


def settle(lines, qkv, proj, d_one, d_hid, tok, gain, vec):
    _, _, _, rows, inner = qkv.shape
    local, width = tok.shape
    pieces = settle_pieces(inner)
    n = len(pieces)
    tiles = local // TILE * 2
    anywhere = pl.BlockSpec(memory_space=pl.ANY)
    vmem = pl.BlockSpec(memory_space=pltpu.VMEM)
    dma = pltpu.SemaphoreType.DMA
    stage = (4, lines, rows, inner)
    return pl.pallas_call(
        functools.partial(settle_kernel, lines, pieces),
        in_specs=[anywhere] * 2 + [vmem] * 5,
        out_specs=[vmem, anywhere, vmem],
        out_shape=[
            jax.ShapeDtypeStruct((4, rows, inner), F32),
            jax.ShapeDtypeStruct((2, local, width), BF16),
            jax.ShapeDtypeStruct(vec.shape, F32),
        ],
        scratch_shapes=[
            pltpu.VMEM((local, width), BF16),
            pltpu.VMEM((4, lines, 2, rows, inner), BF16),
            pltpu.VMEM(stage, BF16),
            pltpu.VMEM(stage, BF16),
            pltpu.VMEM(stage, BF16),
            pltpu.VMEM((4, lines, 2, rows, inner), BF16),
            pltpu.VMEM((4, 2, rows, inner), BF16),
            pltpu.VMEM((local, width), BF16),
            pltpu.VMEM(vec.shape, F32),
            pltpu.VMEM((3,) + vec.shape, F32),
            pltpu.VMEM((3 + lines,) + vec.shape, F32),
            dma((2,)),
            dma((n, lines)), dma((n, lines)), dma((n, lines)), dma((n, lines)), dma((n, 2)), dma((n, 2)),
            dma((n,)), dma((n,)), dma((2 + lines,)), dma((2 + lines,)),
            dma, dma, dma((tiles,)), dma((tiles,)), dma((tiles,)),
        ],
        compiler_params=pltpu.CompilerParams(
            collective_id=1, has_side_effects=True, vmem_limit_bytes=63 << 20
        ),
        name="settle",
    )(qkv, proj, d_one, d_hid, tok, gain[None], vec)


def settle_pieces(inner):
    cuts = [(f, min(SLICE, inner - f)) for f in range(0, inner, SLICE)]
    every = [(j, f, n) for j in (3, 0, 1, 2) for f, n in cuts]
    return [(j, f, n, i >= len(every) - FIRST) for i, (j, f, n) in enumerate(every)]


def feed_kernel(
    lines, part, tok, params, w1_in, w2_own, dy_in, dy_sib,
    d_attn, d_hid, base, mlp_other, g1, g2, g2_out, vec,
    w1, w2, two, dy, act, dpre, hid, sbuf, rbuf, mbuf, ybuf, yin, acc, grad_tile, wide_tile,
    loads, ps, pr, ns, nr, ss, sr, ts, tr, ys, yr, os, dos, dor, gs, outs, keeps,
    own_sem, zs, zr, xs, xr, *share_refs,
):
    at = Place(lines)
    proj_bias, gain, shift, b1, b2 = [params.at[pl.ds(i, 1)] for i in range(5)]
    c, y = at.c, at.y
    local = hid.shape[0]
    tiles = local // TILE
    pieces = columns_of(w1.shape[1])
    gather = Gather(at, w2_own, w2, pieces, own_sem, zs, zr, xs, xr)
    share = Share(at, [(g2,) + piece for piece in pieces[:KEPT]], g2_out, *share_refs)
    gather_ticks = [functools.partial(gather.tick, i) for i in range(len(pieces))]
    share_ticks = share.flow.ticks()

    def advance(ticks, count=1):
        for _ in range(count):
            if ticks:
                ticks.pop(0)()

    def rows(g, q):
        return pl.ds((g * tiles + q) * TILE, TILE)

    def group(g):
        return pl.ds(g * local, local)

    def near_rows(q):
        return pl.ds(q * TILE, TILE)

    copies = [
        pltpu.make_async_copy(tok, ybuf, loads.at[0]),
        pltpu.make_async_copy(part.at[c], yin, loads.at[1]),
        pltpu.make_async_copy(w1_in, w1, loads.at[2]),
        pltpu.make_async_copy(dy_in.at[y], dy.at[group(0)], loads.at[3]),
        pltpu.make_async_copy(dy_sib.at[y], dy.at[group(1)], loads.at[4]),
        pltpu.make_async_copy(dy_in.at[1 - y], dy.at[group(2)], loads.at[5]),
        pltpu.make_async_copy(dy_sib.at[1 - y], dy.at[group(3)], loads.at[6]),
    ]
    for copy in copies:
        copy.start()
    at.greet()
    part_copy = remote(part.at[1 - c], rbuf.at[0], ps, pr, at.sib)
    part_copy.start()
    gather.start()

    def two_sib(q):
        return remote(two.at[rows(0, q)], two.at[rows(1, q)], ns.at[0, q], nr.at[0, q], at.sib)

    def two_peer(q):
        return remote(two.at[rows(0, q)], two.at[rows(2, q)], ns.at[1, q], nr.at[1, q], at.peer)

    def two_pass(q):
        return remote(two.at[rows(2, q)], two.at[rows(3, q)], ns.at[2, q], nr.at[2, q], at.sib)

    copies[0].wait()
    copies[1].wait()
    part_copy.wait_recv()
    for q in range(tiles):
        r = near_rows(q)
        value = ybuf[r].astype(F32) + yin[r].astype(F32) + rbuf[0, r].astype(F32) + proj_bias[...]
        hid[r] = value
        two[rows(0, q)] = (norm_rows(value) * gain[...] + shift[...]).astype(BF16)
        two_peer(q).start()
        two_sib(q).start()

    def first_layer(start, count):
        def body(i, carry):
            r = pl.ds(pl.multiple_of((start + i) * TILE, TILE), TILE)
            pre = dg(two[r], w1[...], ((1,), (0,))) + b1[...]
            sig = jax.nn.sigmoid(GELU * pre)
            act[r] = (pre * sig).astype(BF16)
            dpre[r] = (sig + GELU * pre * sig * (1.0 - sig)).astype(BF16)
            return carry

        lax.fori_loop(0, count, body, 0)

    copies[2].wait()
    first_layer(0, tiles)
    advance(gather_ticks)
    for q in range(tiles):
        two_sib(q).wait_recv()
    first_layer(tiles, tiles)
    advance(gather_ticks)
    for q in range(tiles):
        two_peer(q).wait_recv()
        two_pass(q).start()
        first_layer(2 * tiles + q, 1)
        advance(gather_ticks)
    for q in range(tiles):
        two_pass(q).wait_recv()
    first_layer(3 * tiles, tiles)
    for copy in copies[3:]:
        copy.wait()

    def weight_grad(left, right, out):
        count = out.shape[0] // TILE

        def copy(i):
            slot = lax.rem(i, 2)
            where = pl.ds(pl.multiple_of(i * TILE, TILE), TILE)
            return pltpu.make_async_copy(grad_tile.at[slot], out.at[where], gs.at[slot])

        def body(i, carry):
            cols = pl.ds(pl.multiple_of(i * TILE, TILE), TILE)

            @pl.when(i >= 2)
            def _():
                copy(i - 2).wait()

            grad_tile[lax.rem(i, 2)] = dg(left[:, cols], right[...], ((0,), (0,))).astype(BF16)
            copy(i).start()
            return carry

        lax.fori_loop(0, count, body, 0)
        for i in range(max(0, count - 2), count):
            copy(i).wait()

    advance(gather_ticks, len(gather_ticks))
    weight_grad(dy, act, g2)
    gather.finish()
    share.flow.start()

    shift_sum = jnp.zeros((1, b1.shape[1]), F32)

    def to_norm(g, q):
        r = rows(g, q)
        low = (dg(dy[r], w2[...], ((1,), (0,))) * dpre[r].astype(F32)).astype(BF16)
        dpre[r] = low
        return dg(low, w1[...], ((1,), (1,))), jnp.sum(low.astype(F32), axis=0, keepdims=True)

    def swap(kind, q):
        r = near_rows(q)
        return remote(sbuf.at[kind, r], rbuf.at[kind, r], ss.at[kind, q], sr.at[kind, q], at.sib)

    def y_copy(q):
        r = near_rows(q)
        return remote(ybuf.at[r], yin.at[r], ys.at[q], yr.at[q], at.peer)

    for kind in range(2):
        for q in range(tiles):
            r = near_rows(q)
            value, total = to_norm(3 - 2 * kind, q)
            sbuf[kind, r] = value.astype(BF16)
            shift_sum += total
            swap(kind, q).start()
            value, total = to_norm(2 - 2 * kind, q)
            shift_sum += total
            swap(kind, q).wait_recv()
            value += rbuf[kind, r].astype(F32)
            if kind == 0:
                ybuf[r] = value.astype(BF16)
                y_copy(q).start()
            else:
                acc[r] = value
                advance(share_ticks)

    weight_grad(two, dpre, g1)
    advance(share_ticks)

    def swap_out(kind, q):
        r = near_rows(q)
        return remote(sbuf.at[kind, r], mbuf.at[kind, r], ts.at[kind, q], tr.at[kind, q], at.sib)

    def other_out(q):
        r = near_rows(q)
        return pltpu.make_async_copy(mbuf.at[0, r], mlp_other.at[r], outs.at[q])

    def base_out(q):
        return pltpu.make_async_copy(wide_tile.at[q % 2], base.at[near_rows(q)], keeps.at[q])

    for kind in range(2):
        for q in range(tiles):
            r = near_rows(q)
            swap(kind, q).wait_send()
            sbuf[kind, r] = dg(act[rows(3 - 2 * kind, q)], w2[...], ((1,), (1,)), BF16)
            swap_out(kind, q).start()
            value = dg(act[rows(2 - 2 * kind, q)], w2[...], ((1,), (1,)))
            swap_out(kind, q).wait_recv()
            value += mbuf[kind, r].astype(F32)
            if kind == 0:
                mbuf[0, r] = value.astype(BF16)
                other_out(q).start()
            else:
                if q >= 2:
                    base_out(q - 2).wait()
                wide_tile[q % 2] = hid[r] + value + b2[...]
                base_out(q).start()
        advance(share_ticks)

    def attn_copy(q):
        r = near_rows(q)
        return remote(ybuf.at[r], d_attn.at[c, r], dos.at[q], dor.at[q], at.sib)

    def attn_keep(q):
        r = near_rows(q)
        return pltpu.make_async_copy(ybuf.at[r], d_attn.at[c, r], os.at[q])

    def hid_keep(q):
        r = near_rows(q)
        return pltpu.make_async_copy(acc.at[r], d_hid.at[r], os.at[tiles + q])

    sums = [jnp.zeros((1, hid.shape[1]), F32) for _ in range(4)]
    for q in range(tiles):
        r = near_rows(q)
        y_copy(q).wait()
        grad = acc[r] + yin[r].astype(F32)
        value = hid[r]
        center = value - jnp.mean(value, -1, keepdims=True)
        inverse = lax.rsqrt(jnp.mean(center * center, -1, keepdims=True) + NORM_EPS)
        normal = center * inverse
        out_grad = dy[rows(0, q)].astype(F32)
        total = out_grad + norm_back(grad, normal, inverse, gain[...])
        low = total.astype(BF16)
        ybuf[r] = low
        attn_copy(q).start()
        attn_keep(q).start()
        acc[r] = total
        hid_keep(q).start()
        for i, t in enumerate((low.astype(F32), grad * normal, grad, out_grad)):
            sums[i] += jnp.sum(t, axis=0, keepdims=True)
    for i in range(4):
        vec[i : i + 1] = sums[i]
    vec[4:5] = shift_sum
    vec[5:8] = jnp.zeros((3, hid.shape[1]), F32)

    advance(share_ticks, len(share_ticks))
    share.drain()
    gather.drain()
    part_copy.wait_send()
    for q in range(tiles):
        two_sib(q).wait_send()
        two_peer(q).wait_send()
        two_pass(q).wait_send()
        other_out(q).wait()
        if q >= tiles - 2:
            base_out(q).wait()
        for kind in range(2):
            swap_out(kind, q).wait_send()
        attn_copy(q).wait_send()
        attn_keep(q).wait()
        hid_keep(q).wait()
        there = d_attn.at[1 - c, near_rows(q)]
        remote(there, there, dos.at[q], dor.at[q], at.sib).wait_recv()


def feed(lines, part, tok, params, w1, w2_own, dy, dy_sib):
    local, width = tok.shape
    rows, quarter = w2_own.shape
    kept = columns_of(quarter)[:KEPT]
    tiles = local // TILE
    anywhere = pl.BlockSpec(memory_space=pl.ANY)
    vmem = pl.BlockSpec(memory_space=pltpu.VMEM)
    dma = pltpu.SemaphoreType.DMA
    slots = pltpu.VMEM((local, width), BF16)
    shape = jax.ShapeDtypeStruct
    return pl.pallas_call(
        functools.partial(feed_kernel, lines),
        in_specs=[anywhere] * 2 + [vmem] + [anywhere] * 4,
        out_specs=[anywhere] * 6 + [vmem] * 2,
        out_shape=[
            shape((2, local, width), BF16),
            shape((local, width), F32),
            shape((local, width), F32),
            shape((local, width), BF16),
            shape((width, quarter), BF16),
            shape((width, quarter), BF16),
            shape((2, rows, sum(n for _, n in kept)), F32),
            shape((8, width), F32),
        ],
        scratch_shapes=[
            pltpu.VMEM((width, quarter), BF16),
            pltpu.VMEM((width, quarter), BF16),
            pltpu.VMEM((4 * local, width), BF16),
            pltpu.VMEM((4 * local, width), BF16),
            pltpu.VMEM((4 * local, quarter), BF16),
            pltpu.VMEM((4 * local, quarter), BF16),
            pltpu.VMEM((local, width), F32),
            pltpu.VMEM((2, local, width), BF16),
            pltpu.VMEM((2, local, width), BF16),
            pltpu.VMEM((2, local, width), BF16),
            slots,
            slots,
            pltpu.VMEM((local, width), F32),
            pltpu.VMEM((2, TILE, quarter), BF16),
            pltpu.VMEM((2, TILE, width), F32),
            dma((7,)), dma, dma,
            dma((3, tiles)), dma((3, tiles)),
            dma((2, tiles)), dma((2, tiles)), dma((2, tiles)), dma((2, tiles)),
            dma((tiles,)), dma((tiles,)), dma((2 * tiles,)), dma((tiles,)), dma((tiles,)), dma((2,)),
            dma((tiles,)), dma((tiles,)),
        ]
        + gather_scratch(lines, quarter)
        + share_scratch(lines, rows, kept),
        compiler_params=pltpu.CompilerParams(
            collective_id=2, has_side_effects=True, vmem_limit_bytes=63 << 20
        ),
        name="feed",
    )(part, tok, params, w1, w2_own, dy, dy_sib)


def norm_back(grad_out, normal, inverse, gain):
    scaled = grad_out * gain
    return inverse * (
        scaled
        - jnp.mean(scaled, -1, keepdims=True)
        - normal * jnp.mean(scaled * normal, -1, keepdims=True)
    )


class Links:
    def __init__(self, shards):
        self.shards = shards
        self.lines = shards // 2
        self.s = lax.axis_index("shard")
        self.c = lax.axis_index("ctx")
        self.y = lax.axis_index("tp")
        self.line = self.s // 2
        self.side = self.s % 2
        self.diag = self.c == self.y

    def send(self, value, target, where=lambda c, y: True):
        flat = lambda s, c, y: (s * 2 + c) * 2 + y
        pairs = []
        for s in range(self.shards):
            for c in range(2):
                for y in range(2):
                    if where(c, y):
                        pairs.append((flat(s, c, y), flat(*target(s, c, y))))
        return lax.ppermute(value, AXES, pairs)

    def across(self, value, where=lambda c, y: True):
        return self.send(value, lambda s, c, y: (s, c, 1 - y), where)


def per_device(
    tokens,
    patch_meta,
    attn_norm_gain,
    attn_norm_bias,
    qkv_weight,
    qkv_bias,
    proj_weight,
    proj_bias,
    mlp_norm_gain,
    mlp_norm_bias,
    fc1_weight,
    fc1_bias,
    fc2_weight,
    fc2_bias,
    cotangent,
    *,
    shards,
):
    net = Links(shards)
    c, y = net.c, net.y
    local = tokens.shape[2]
    width = tokens.shape[3]
    full = patch_meta.shape[3]
    inner = qkv_weight.shape[2]
    rows = width // shards
    quarter = fc1_weight.shape[1] // 2
    pick = lambda t, i, d=0: lax.dynamic_index_in_dim(t, i, d, False)
    mine_or = lambda own, other: jnp.where(net.diag, own, other)

    def both(own, other, index):
        return jnp.where(index == 0, jnp.stack([own, other]), jnp.stack([other, own]))

    attn_block = jnp.concatenate([qkv_weight, proj_weight.T[None]], axis=0)
    grad_out = cotangent.reshape(2, local, width)
    tok = pick(tokens, y).reshape(local, width)
    attn_full, normed, grad_out_sib, bias_qkv = collect(
        net.lines, attn_block, tok, attn_norm_gain, attn_norm_bias, grad_out, qkv_bias
    )
    fc1_block = lax.dynamic_slice_in_dim(fc1_weight, c * quarter, quarter, 1)
    fc2_block = lax.dynamic_slice_in_dim(fc2_weight, c * quarter, quarter, 0).T
    bias_fc1 = lax.dynamic_slice_in_dim(fc1_bias, c * quarter, quarter, 0)

    meta = pick(patch_meta, y, 1).reshape(3, full)
    ids = meta[0]
    cosine, sine = rope_tables(meta[1], meta[2])
    shift = jnp.pad(bias_qkv, ((0, 5), (0, 0)))
    low, mixed, mixed_f, lse, attn_part, fc1_full = attend(
        net.lines, attn_full, normed, shift, cosine, sine, ids, fc1_block
    )
    attn_part = attn_part.reshape(2, local, width)
    params = jnp.stack([proj_bias, mlp_norm_gain, mlp_norm_bias, bias_fc1, fc2_bias])
    d_attn, d_hidden, base, mlp_other, grad_fc1_part, grad_fc2_part, fc2_sum, sums_two = feed(
        net.lines, attn_part, tok, params, fc1_full, fc2_block, grad_out, grad_out_sib,
    )
    d_one_part, grad_qkv_part, grad_proj_part, qkv_shift, fc1_sum, block_output = attend_back(
        net.lines, low, mixed_f, lse, cosine, sine, ids, attn_full, normed, mixed, d_attn,
        grad_fc1_part, grad_fc2_part, mlp_other, base,
    )
    late = fc1_sum.shape[2] - quarter
    fc2_sum = jnp.concatenate([fc2_sum, fc1_sum[:, :, :late]], axis=2)
    fc1_sum = fc1_sum[:, :, late:]
    d_one_part = d_one_part.reshape(2, local, width)
    qkv_shift = qkv_shift[:, 0]

    fc1_shift = sums_two[4]
    zero_qkv, zero_fc1 = jnp.zeros_like(qkv_shift), jnp.zeros_like(fc1_shift)
    small = jnp.concatenate(
        [
            jnp.zeros((2 * width,), F32),
            sums_two[0],
            sums_two[1],
            sums_two[2],
            sums_two[3],
            jnp.where(c == 0, qkv_shift, zero_qkv).reshape(-1),
            jnp.where(c == 1, qkv_shift, zero_qkv).reshape(-1),
        ]
        + [jnp.where((y == i) & (c == j), fc1_shift, zero_fc1) for i in range(2) for j in range(2)]
    )
    blocks = (net.lines, 2, rows, inner)
    attn_sum, input_grad, small = settle(
        net.lines, grad_qkv_part.reshape((3,) + blocks), grad_proj_part.reshape(blocks), d_one_part,
        d_hidden, tok, attn_norm_gain, small.reshape(-1, width),
    )
    small = small.reshape(-1)
    input_grad = input_grad.astype(F32)
    grad_qkv, grad_proj = attn_sum[:3], attn_sum[3].T
    grad_fc1 = jnp.moveaxis(fc1_sum, 0, 1).reshape(rows, 2 * quarter)
    grad_fc2 = jnp.moveaxis(fc2_sum, 1, 2).reshape(2 * quarter, rows)

    vec = lambda i: small[i * width : (i + 1) * width]
    at = 6 * width
    qkv_shifts = small[at : at + 6 * inner].reshape(2, 3, inner)
    fc1_shifts = small[at + 6 * inner :].reshape(2, 2 * quarter)
    out_shape = tokens.shape
    return (
        block_output.reshape(out_shape),
        input_grad.reshape(out_shape),
        vec(0),
        vec(1),
        grad_qkv,
        pick(qkv_shifts, y),
        grad_proj,
        vec(2),
        vec(3),
        vec(4),
        grad_fc1,
        pick(fc1_shifts, y),
        grad_fc2,
        vec(5),
    )


def solution(mesh):
    slots = P(None, "shard", "ctx", None)
    placed = (
        slots,
        P(None, None, "shard", None),
        P(),
        P(),
        P(None, "shard", "tp"),
        P(None, "tp"),
        P("tp", "shard"),
        P(),
        P(),
        P(),
        P("shard", "tp"),
        P("tp"),
        P("tp", "shard"),
        P(),
        slots,
    )
    return jax.shard_map(
        functools.partial(per_device, shards=mesh.shape["shard"]),
        mesh=mesh,
        in_specs=placed,
        out_specs=(
            slots,
            slots,
            P(),
            P(),
            P(None, "shard", "tp"),
            P(None, "tp"),
            P("tp", "shard"),
            P(),
            P(),
            P(),
            P("shard", "tp"),
            P("tp"),
            P("tp", "shard"),
            P(),
        ),
        check_vma=False,
    )
```
